256 devices in a mesh: group: 4 (over y), dev: 64 (over z, x, core).
Axes of the slice: x: 4, y: 4, z: 8, core: 2. Of those that a mesh axis runs over, the one named last changes fastest.
Arguments:
- q_compressed: bfloat16 [256, 1536], P('group'), may hold values from -6 to 6
- w_q_nope: bfloat16 [1536, 16384], P(None, 'dev'), may hold values from -0.15625 to 0.15625
- w_q_rope: bfloat16 [1536, 8192], P(None, 'dev'), may hold values from -0.15625 to 0.15625
- w_uk: bfloat16 [128, 128, 512], P('dev'), may hold values from -0.5 to 0.5
- w_uv: bfloat16 [128, 512, 128], P('dev'), may hold values from -0.25 to 0.25
- w_o: bfloat16 [16384, 7168], P('dev'), may hold values from -0.046875 to 0.046875
- kv_cache: bfloat16 [4, 64, 2, 2048, 576], P('group', 'dev'), may hold values from -320 to 320
- draft_kv: bfloat16 [256, 576], P('group'), may hold values from -18 to 18
- context_length: int32 [64], replicated, may hold values from 6145 to 24576
- slot_sequence: int32 [4, 64, 2], replicated, may hold values from -1 to 63, as said below
- slot_slab: int32 [4, 64, 2], replicated, may hold values from -1 to 11
Outputs:
- attn_output: float32 [256, 7168], P(('group', 'dev'))
The draws below stay inside these ranges and needn't reach their ends.
Inputs may be any that keep to these rules, and one draw needn't show every extreme that they name: For each sequence s, slabs 0 to ceil(context_length[s] / 2048) - 1 each stand in exactly one slot of the pool, slot_sequence naming s and slot_slab the slab's number; all other slots hold -1 in both tables. The sequences' slab counts are, in some order, 4 + floor(i * 8 / 63) for i from 0 to 63. A group's slots take the slabs of its own sequences first; slabs beyond a group's 64 * 2 slots stand in free slots of other groups.
All inputs are finite; a program needn't handle non-finite values.
Results may differ from the reference program's by a relative error of at most 0.02.
The reference program's roundings to bfloat16 on the way (of `q_nope`, `queries`, `attended` and `head_values`) count: a program that leaves them out, or rounds other values in their place, can miss the bound.
Values may be sent and summed in bfloat16 or wider, within the bound.
No kernel may reach another device: no remote copies, remote signals or barrier semaphores. Data moves between devices by JAX's collectives and lax.ppermute only.
A program may use at most 64 MiB of HBM per device.

```python
import jax
import jax.numpy as jnp
from jax import lax

D = 7168
HEADS = 128
QRANK = 1536
NOPE = 128
ROPE = 64
LATENT = 512
VDIM = 128
DRAFT = 4
SLOTS = 2
MIN_SLABS = 4
MAX_SLABS = 12
SLAB = 2048
GROUPS = 4
HOLDERS = 64
SEQ_GRP = 16
SEQS = 64
TOKENS = 256
KV = 576


def placement(key):
    base_key = jax.random.fold_in(key, 5)
    key_heavy, key_order, key_tail, key_spread = jax.random.split(base_key, 4)
    seq_count = SEQ_GRP * GROUPS
    capacity = HOLDERS * SLOTS
    heavy = jax.random.randint(key_heavy, (), 0, GROUPS)
    home_group = jnp.arange(seq_count, dtype=jnp.int32) // SEQ_GRP
    score = jnp.where(home_group == heavy, seq_count, 0) + jax.random.permutation(key_order, seq_count).astype(jnp.int32)
    ranking = jnp.argsort(jnp.argsort(score, stable=True), stable=True).astype(jnp.int32)
    slab_count = MIN_SLABS + ranking * (MAX_SLABS - MIN_SLABS) // (seq_count - 1)
    tail_tokens = jax.random.randint(key_tail, (seq_count,), 1, SLAB + 1)
    tail_tokens = jnp.where(ranking == 0, 1, jnp.where(ranking == seq_count - 1, SLAB, tail_tokens))
    lengths = ((slab_count - 1) * SLAB + tail_tokens).astype(jnp.int32)
    per_group = slab_count.reshape(GROUPS, SEQ_GRP)
    starts = jnp.cumsum(per_group, axis=1) - per_group
    load = jnp.sum(per_group, axis=1)
    kept = jnp.minimum(load, capacity)
    spill = load - kept
    free_slots = capacity - kept
    spill_start = jnp.cumsum(spill) - spill
    free_start = jnp.cumsum(free_slots) - free_slots
    position = jnp.arange(capacity, dtype=jnp.int32)
    at_home = position[None, :] < kept[:, None]
    free_rank = free_start[:, None] + position[None, :] - kept[:, None]
    used_spill = jnp.logical_not(at_home) & (free_rank < jnp.sum(spill))
    inside = (spill_start[None, None, :] <= free_rank[:, :, None]) & (free_rank[:, :, None] < (spill_start + spill)[None, None, :])
    source = jnp.sum(inside.astype(jnp.int32) * jnp.arange(GROUPS, dtype=jnp.int32)[None, None, :], axis=2)
    owner_group = jnp.where(at_home, jnp.arange(GROUPS, dtype=jnp.int32)[:, None], source)
    group_rank = jnp.where(at_home, position[None, :], capacity + free_rank - spill_start[source])
    owner_starts = starts[owner_group]
    member = jnp.sum((owner_starts <= group_rank[:, :, None]).astype(jnp.int32), axis=2) - 1
    member = jnp.clip(member, 0, SEQ_GRP - 1)
    sequence = owner_group * SEQ_GRP + member
    slab_number = group_rank - jnp.take_along_axis(owner_starts, member[..., None], axis=2)[..., 0]
    live = at_home | used_spill
    sequence = jnp.where(live, sequence, -1)
    slab_number = jnp.where(live, slab_number, -1)
    perms = jnp.stack([jax.random.permutation(jax.random.fold_in(key_spread, group_id), HOLDERS) for group_id in range(GROUPS)])
    inverse = jnp.argsort(perms, axis=1).astype(jnp.int32)
    spot = jnp.arange(SLOTS, dtype=jnp.int32)[None, None, :] * HOLDERS + inverse[:, :, None]
    spot = spot.reshape(GROUPS, -1)
    table_sequence = jnp.take_along_axis(sequence, spot, axis=1).reshape(GROUPS, HOLDERS, SLOTS)
    table_slab = jnp.take_along_axis(slab_number, spot, axis=1).reshape(GROUPS, HOLDERS, SLOTS)
    return (lengths, table_sequence.astype(jnp.int32), table_slab.astype(jnp.int32))


def draw_context_length(key, part):
    return placement(key)[0]


def draw_slot_sequence(key, part):
    return placement(key)[1]


def draw_slot_slab(key, part):
    return placement(key)[2]


def draw_kv_cache(key, part):
    shape = (GROUPS, HOLDERS, SLOTS, SLAB, LATENT + ROPE)
    key_base = jax.random.fold_in(jax.random.fold_in(key, 11), 0)
    drawn = jnp.clip(1.5 * jax.random.normal(key_base, shape, jnp.float32), -9.0, 9.0)
    return drawn.astype(jnp.bfloat16)


def block_levels(key, shape, shards, smallest, largest):
    gain, own = 1.0, jax.random.fold_in(key, 6)
    for axis_at, blocks in shards:
        heights = jnp.exp(jax.random.uniform(jax.random.fold_in(own, axis_at), (blocks,), jnp.float32, smallest / len(shards), largest / len(shards)))
        gain = gain * jnp.repeat(heights, shape[axis_at] // blocks).reshape([-1 if axis == axis_at else 1 for axis in range(len(shape))])
    return gain


def noise(rng, extent, spread, limit, cuts=(), held_as=jnp.bfloat16):
    result = jax.random.normal(rng, extent, jnp.float32) * spread
    if len(cuts) > 0:
        result = block_levels(rng, extent, cuts, -0.22, 0.18) * result
    return jnp.clip(result, min=-limit, max=limit).astype(held_as)


def setup_inputs(seed: int = 0) -> dict:
    keys = jax.random.split(jax.random.key(seed), 12)
    return {
        "q_compressed": noise(keys[0], (TOKENS, QRANK), 1.0, 6.0, ((0, 4),)),
        "w_q_nope": noise(keys[1], (QRANK, HEADS * NOPE), QRANK ** -0.5, 0.15625, ((1, 64),)),
        "w_q_rope": noise(keys[2], (QRANK, HEADS * ROPE), QRANK ** -0.5, 0.15625, ((1, 64),)),
        "w_uk": noise(keys[3], (HEADS, NOPE, LATENT), NOPE ** -0.5, 0.5, ((0, 64),)),
        "w_uv": noise(keys[4], (HEADS, LATENT, VDIM), LATENT ** -0.5, 0.25, ((0, 64),)),
        "w_o": noise(keys[5], (HEADS * VDIM, D), (HEADS * VDIM) ** -0.5, 0.046875, ((0, 64),)),
        "kv_cache": draw_kv_cache(jax.random.fold_in(keys[11], 71), 0),
        "draft_kv": noise(keys[7], (TOKENS, KV), 3.0, 18.0, ((0, 4),)),
        "context_length": draw_context_length(jax.random.fold_in(keys[11], 71), 0),
        "slot_sequence": draw_slot_sequence(jax.random.fold_in(keys[11], 71), 0),
        "slot_slab": draw_slot_slab(jax.random.fold_in(keys[11], 71), 0),
    }


EMPTY = -1e30


def slot_partial(row_block, slab_keys, valid_count):
    scores = lax.dot_general(row_block, slab_keys, (((1,), (1,)), ((), ())), preferred_element_type=jnp.float32)
    is_valid = jnp.arange(slab_keys.shape[0], dtype=jnp.int32) < valid_count
    masked = jnp.where(is_valid[None, :], scores, EMPTY)
    row_peak = jnp.max(masked, axis=1)
    weights = jnp.where(is_valid[None, :], jnp.exp(masked - row_peak[:, None]), 0.0)
    row_total = jnp.maximum(jnp.sum(weights, axis=1), 1.0)
    mixture = jnp.dot(weights.astype(jnp.bfloat16), slab_keys[:, :LATENT], preferred_element_type=jnp.float32)
    return row_peak + jnp.log(row_total), mixture / row_total[:, None]


def merge_blocks(block_log, block_out, block_owner, own_log, own_out):
    owners_count = own_log.shape[0]
    matches = block_owner[None, :] == jnp.arange(owners_count, dtype=jnp.int32)[:, None]
    picked = jnp.where(matches[:, :, None, None], block_log[None], EMPTY)
    top_log = jnp.maximum(jnp.max(picked, axis=1), own_log)
    weights = jnp.where(matches[:, :, None, None], jnp.exp(picked - top_log[:, None]), 0.0)
    own_weight = jnp.exp(own_log - top_log)
    weight_sum = jnp.sum(weights, axis=1) + own_weight
    summed = jnp.einsum('sbtx,btxl->stxl', weights, block_out, precision=lax.Precision.HIGHEST)
    summed = summed + own_weight[..., None] * own_out
    return top_log + jnp.log(weight_sum), summed / weight_sum[..., None]


def reference(q_compressed, w_q_nope, w_q_rope, w_uk, w_uv, w_o, kv_cache, draft_kv, context_length, slot_sequence, slot_slab):
    token_count = q_compressed.shape[0]
    key_width = LATENT + ROPE
    q_nope = jnp.dot(q_compressed, w_q_nope, preferred_element_type=jnp.float32).astype(jnp.bfloat16)
    q_nope = q_nope.reshape(token_count, HEADS, NOPE)
    q_rope = jnp.dot(q_compressed, w_q_rope, preferred_element_type=jnp.float32).reshape(token_count, HEADS, ROPE)
    absorbed = jnp.einsum('thn,hnl->thl', q_nope.astype(jnp.float32), w_uk.astype(jnp.float32), precision=lax.Precision.HIGHEST)
    queries = (jnp.concatenate([absorbed, q_rope], axis=2) * (NOPE + ROPE) ** -0.5).astype(jnp.bfloat16)
    by_sequence = queries.reshape(SEQS, DRAFT * HEADS, key_width)
    pool_owner = slot_sequence.reshape(-1).astype(jnp.int32)
    pool_number = slot_slab.reshape(-1).astype(jnp.int32)
    slabs_flat = kv_cache.reshape(-1, SLAB, key_width)

    def one_slot(slot_number):
        slot_owner = pool_owner[slot_number]
        chosen = jnp.maximum(slot_owner, 0)
        row_block = lax.dynamic_index_in_dim(by_sequence, chosen, 0, keepdims=False)
        valid_count = jnp.where(slot_owner >= 0, context_length[chosen] - pool_number[slot_number] * SLAB, 0)
        slab_keys = lax.dynamic_index_in_dim(slabs_flat, slot_number, 0, keepdims=False)
        return slot_partial(row_block, slab_keys, valid_count)

    slot_log, slot_out = lax.map(one_slot, jnp.arange(pool_owner.shape[0], dtype=jnp.int32))
    slot_log = slot_log.reshape(-1, DRAFT, HEADS)
    slot_out = slot_out.reshape(-1, DRAFT, HEADS, LATENT)

    draft_rows = queries.reshape(SEQS, DRAFT, HEADS, key_width).astype(jnp.float32)
    draft_keys = draft_kv.reshape(SEQS, DRAFT, key_width).astype(jnp.float32)
    scores = jnp.einsum('sthk,suk->sthu', draft_rows, draft_keys, precision=lax.Precision.HIGHEST)
    causal = jnp.arange(DRAFT)[None, :] <= jnp.arange(DRAFT)[:, None]
    masked = jnp.where(causal[None, :, None, :], scores, EMPTY)
    draft_peak = jnp.max(masked, axis=3)
    weights = jnp.where(causal[None, :, None, :], jnp.exp(masked - draft_peak[..., None]), 0.0)
    draft_total = jnp.sum(weights, axis=3)
    rounded = lax.optimization_barrier(weights.astype(jnp.bfloat16)).astype(jnp.float32)
    mixture = jnp.einsum('sthu,sul->sthl', rounded, draft_keys[..., :LATENT], precision=lax.Precision.HIGHEST)
    draft_log = draft_peak + jnp.log(draft_total)
    draft_out = mixture / draft_total[..., None]

    final_log, final_out = merge_blocks(slot_log, slot_out, pool_owner, draft_log, draft_out)
    attended = final_out.astype(jnp.bfloat16).reshape(token_count, HEADS, LATENT)
    head_values = jnp.einsum('thl,hlv->thv', attended.astype(jnp.float32), w_uv.astype(jnp.float32), precision=lax.Precision.HIGHEST)
    head_values = head_values.astype(jnp.bfloat16).reshape(token_count, HEADS * VDIM)
    return jnp.dot(head_values, w_o, preferred_element_type=jnp.float32)
```

```python
import jax
import jax.numpy as jnp
from jax import lax
from jax.experimental import pallas as pl
from jax.experimental.pallas import tpu as pltpu
from jax.sharding import Mesh
from jax.sharding import PartitionSpec as P

NOPE = 128
ROPE = 64
LATENT = 512
VDIM = 128
DRAFT = 4
SEQ_GRP = 16
TOK_GRP = SEQ_GRP * DRAFT
SLOTS = 2
KEY = LATENT + ROPE
WIDE = 2 * LATENT + 2 * ROPE
PART = SLOTS * 2 * LATENT + 128
NARROW = 2 * NOPE + 2 * ROPE
EMPTY = -1e30
SCALE = (NOPE + ROPE) ** -0.5
F32 = jnp.float32
BF16 = jnp.bfloat16
CONTRACT_LAST = (((1,), (1,)), ((), ()))

VMEM = pl.BlockSpec(memory_space=pltpu.VMEM)
SMEM = pl.BlockSpec(memory_space=pltpu.SMEM)


def dot(a, b):
    return jnp.dot(a, b, preferred_element_type=F32)


def dot_t(a, b):
    return lax.dot_general(a, b, CONTRACT_LAST, preferred_element_type=F32)


def call(kernel, outs, args, specs, scratch=(), vmem=32):
    return pl.pallas_call(
        kernel,
        out_shape=outs,
        in_specs=specs,
        out_specs=jax.tree.map(lambda _: VMEM, outs),
        scratch_shapes=list(scratch),
        compiler_params=pltpu.CompilerParams(vmem_limit_bytes=vmem << 20),
    )(*args)


def three_terms(value):
    high = value.astype(BF16).astype(F32)
    middle = (value - high).astype(BF16).astype(F32)
    return high, middle, (value - high - middle).astype(BF16).astype(F32)


def put_terms(tile, value, first):
    lane = lax.broadcasted_iota(jnp.int32, tile.shape, 1)
    for i, term in enumerate(three_terms(value)):
        tile = jnp.where(lane == first + i, term, tile)
    return tile


def project_kernel(q_ref, wn_ref, wr_ref, out_ref):
    out_ref[:, : 2 * NOPE] = dot(q_ref[...], wn_ref[...]).astype(BF16)
    out_ref[:, 2 * NOPE :] = (dot(q_ref[...], wr_ref[...]) * SCALE).astype(BF16)


def spread_kernel(core_ref, q_ref, code_ref, own_ref, mate_ref, out_ref, rows):
    core = core_ref[0]
    rows[...] = jnp.zeros_like(rows)
    for block in range(q_ref.shape[0] // TOK_GRP):
        at = pl.ds(block * TOK_GRP, TOK_GRP)
        side = pl.multiple_of(jnp.where(core == block % 2, 0, NOPE), NOPE)
        for par in range(2):
            rows[at, pl.ds(par * 2 * NOPE + side, NOPE)] = q_ref[at, par * NOPE : (par + 1) * NOPE]
        rows[at, 4 * NOPE :] = q_ref[at, 2 * NOPE :]
    count = code_ref.shape[0] // SLOTS
    for slot in range(SLOTS):
        code = code_ref[slot * count : (slot + 1) * count, :]
        column = lax.broadcasted_iota(jnp.int32, (count, rows.shape[0]), 1)
        picked = dot(jnp.where(column == code, 1.0, 0.0).astype(BF16), rows[...]).astype(BF16)
        for par in range(2):
            weight = jnp.concatenate([own_ref[par], mate_ref[par]], axis=0)
            absorbed = dot(picked[:, par * 2 * NOPE : (par + 1) * 2 * NOPE], weight) * SCALE
            first = slot * WIDE + par * LATENT
            out_ref[:, first : first + LATENT] = absorbed.astype(BF16)
        out_ref[:, slot * WIDE + 2 * LATENT : (slot + 1) * WIDE] = picked[:, 4 * NOPE :]


def draft_kernel(q_ref, uk_ref, uv_ref, kv_ref, hv_ref, log_ref):
    row = lax.broadcasted_iota(jnp.int32, (TOK_GRP, TOK_GRP), 0)
    col = lax.broadcasted_iota(jnp.int32, (TOK_GRP, TOK_GRP), 1)
    seen = (row // DRAFT == col // DRAFT) & (col <= row)
    lane = lax.broadcasted_iota(jnp.int32, log_ref.shape, 1)
    logs = jnp.zeros(log_ref.shape, F32)
    for par in range(2):
        absorbed = (dot(q_ref[:, par * NOPE : (par + 1) * NOPE], uk_ref[par]) * SCALE).astype(BF16)
        first = 2 * NOPE + par * ROPE
        scores = dot_t(absorbed, kv_ref[:, :LATENT])
        scores += dot_t(q_ref[:, first : first + ROPE], kv_ref[:, LATENT:])
        scores = jnp.where(seen, scores, EMPTY)
        peak = jnp.max(scores, axis=1, keepdims=True)
        weights = jnp.where(seen, jnp.exp(scores - peak), 0.0)
        total = jnp.sum(weights, axis=1, keepdims=True)
        mixture = dot(weights.astype(BF16), kv_ref[:, :LATENT]) / total
        hv_ref[:, par * VDIM : (par + 1) * VDIM] = dot(mixture.astype(BF16), uv_ref[par])
        logs = jnp.where(lane == par, peak + jnp.log(total), logs)
    log_ref[...] = logs


def attend_kernel(count_ref, x_ref, kv_ref, out_ref, queries, scores):
    slot = pl.program_id(0)
    count = count_ref[slot]
    half = x_ref.shape[0]
    for par in range(2):
        at = slice(par * half, (par + 1) * half)
        queries[at, :LATENT] = x_ref[:, par * LATENT : (par + 1) * LATENT]
        first = 2 * LATENT + par * ROPE
        queries[at, LATENT:] = x_ref[:, first : first + ROPE]
    slab = kv_ref.shape[0]
    chunk = 512
    peak = jnp.full((2 * half, 1), EMPTY, F32)
    for first in range(0, slab, chunk):
        score = dot_t(queries[...], kv_ref[first : first + chunk, :])
        position = lax.broadcasted_iota(jnp.int32, score.shape, 1) + first
        score = jnp.where(position < count, score, EMPTY)
        scores[:, first : first + chunk] = score
        peak = jnp.maximum(peak, jnp.max(score, axis=1, keepdims=True))
    reference = jnp.maximum(peak, EMPTY / 10)
    total = jnp.zeros((2 * half, 1), F32)
    mixture = jnp.zeros((2 * half, LATENT), F32)
    for first in range(0, slab, chunk):
        weights = jnp.exp(scores[:, first : first + chunk] - reference)
        total += jnp.sum(weights, axis=1, keepdims=True)
        mixture += dot(weights.astype(BF16), kv_ref[first : first + chunk, :LATENT])
    total = jnp.maximum(total, 1.0)
    mixture = (mixture / total).astype(BF16)
    log = peak + jnp.log(total)
    start = slot * 2 * LATENT
    lane = lax.broadcasted_iota(jnp.int32, (half, 128), 1)
    tile = jnp.where(slot == 0, jnp.zeros((half, 128), F32), out_ref[:, SLOTS * 2 * LATENT :].astype(F32))
    for par in range(2):
        at = slice(par * half, (par + 1) * half)
        out_ref[:, pl.ds(pl.multiple_of(start + par * LATENT, LATENT), LATENT)] = mixture[at]
        for i, term in enumerate(three_terms(log[at])):
            tile = jnp.where(lane == slot * 6 + par * 3 + i, term, tile)
    out_ref[:, SLOTS * 2 * LATENT :] = tile.astype(BF16)


def attend(count, x, kv):
    rows = x.shape[0]
    slab = kv.shape[1]
    return pl.pallas_call(
        attend_kernel,
        out_shape=jax.ShapeDtypeStruct((rows, PART), BF16),
        grid_spec=pltpu.PrefetchScalarGridSpec(
            num_scalar_prefetch=1,
            grid=(SLOTS,),
            in_specs=[
                pl.BlockSpec((rows, WIDE), lambda k, _: (0, k)),
                pl.BlockSpec((None, slab, KEY), lambda k, _: (k, 0, 0)),
            ],
            out_specs=pl.BlockSpec((rows, PART), lambda k, _: (0, 0)),
            scratch_shapes=[
                pltpu.VMEM((2 * rows, KEY), BF16),
                pltpu.VMEM((2 * rows, slab), F32),
            ],
        ),
        compiler_params=pltpu.CompilerParams(
            dimension_semantics=("arbitrary",), vmem_limit_bytes=48 << 20
        ),
    )(count, x, kv)


def merge_kernel(core_ref, y_ref, code_ref, own_ref, mate_ref, out_ref):
    core = core_ref[0]
    rows, cols = out_ref.shape[0], y_ref.shape[0]
    base = SLOTS * 2 * LATENT
    logs = jnp.transpose(y_ref[:, base:].astype(F32))
    row = lax.broadcasted_iota(jnp.int32, (rows, cols), 0)
    match = [row == code_ref[slot : slot + 1, :] for slot in range(SLOTS)]
    is_own = (lax.broadcasted_iota(jnp.int32, (rows, VDIM), 0) // TOK_GRP) % 2 == core
    tile = jnp.zeros((rows, 128), F32)
    for par in range(2):
        held = []
        for slot in range(SLOTS):
            at = slot * 6 + par * 3
            log = logs[at : at + 1, :] + logs[at + 1 : at + 2, :] + logs[at + 2 : at + 3, :]
            held.append(jnp.where(match[slot], log, EMPTY))
        peak = jnp.max(jnp.maximum(held[0], held[1]), axis=1, keepdims=True)
        total = jnp.zeros((rows, 1), F32)
        mixture = jnp.zeros((rows, LATENT), F32)
        for slot in range(SLOTS):
            weights = jnp.where(match[slot], jnp.exp(held[slot] - peak), 0.0)
            total += jnp.sum(weights, axis=1, keepdims=True)
            first = slot * 2 * LATENT + par * LATENT
            mixture += dot(weights.astype(BF16), y_ref[:, first : first + LATENT])
        total = jnp.maximum(total, 1.0)
        mixture = (mixture / total).astype(BF16)
        values = jnp.where(is_own, dot(mixture, own_ref[par]), dot(mixture, mate_ref[par]))
        out_ref[:, par * VDIM : (par + 1) * VDIM] = values.astype(BF16)
        tile = put_terms(tile, peak + jnp.log(total), par * 3)
    out_ref[:, 2 * VDIM :] = tile.astype(BF16)


def finish_kernel(z_ref, hv_ref, log_ref, order_ref, out_ref):
    blocks = z_ref.shape[0] // TOK_GRP
    values = []
    for par in range(2):
        logs = [log_ref[:, par : par + 1]]
        parts = [hv_ref[:, par * VDIM : (par + 1) * VDIM]]
        for block in range(blocks):
            at = slice(block * TOK_GRP, (block + 1) * TOK_GRP)
            terms = z_ref[at, 2 * VDIM :].astype(F32)
            first = par * 3
            logs.append(
                terms[:, first : first + 1]
                + terms[:, first + 1 : first + 2]
                + terms[:, first + 2 : first + 3]
            )
            parts.append(z_ref[at, par * VDIM : (par + 1) * VDIM].astype(F32))
        peak = logs[0]
        for log in logs[1:]:
            peak = jnp.maximum(peak, log)
        total = jnp.zeros_like(peak)
        summed = jnp.zeros_like(parts[0])
        for log, part in zip(logs, parts):
            weight = jnp.exp(log - peak)
            total += weight
            summed += weight * part
        values.append((summed / total).astype(BF16))
    out_ref[...] = dot(order_ref[...], jnp.concatenate(values, axis=1)).astype(BF16)


def exchange(array, axes, peers):
    blocks = array.reshape(peers, array.shape[0] // peers, *array.shape[1:])
    return lax.all_to_all(blocks, axes, 0, 0, tiled=True).reshape(array.shape)


def shards(
    q_compressed,
    w_q_nope,
    w_q_rope,
    w_uk,
    w_uv,
    w_o,
    kv_cache,
    draft_kv,
    context_length,
    slot_sequence,
    slot_slab,
):
    groups, zs, xs, cores = (lax.axis_size(a) for a in ("group", "z", "x", "core"))
    group, z, x, core = (lax.axis_index(a) for a in ("group", "z", "x", "core"))
    chips = zs * xs
    core_id = core.astype(jnp.int32).reshape(1)
    swap = [(i, 1 - i) for i in range(cores)]
    mate_uk = lax.ppermute(w_uk, "core", swap)
    mate_uv = lax.ppermute(w_uv, "core", swap)

    table = lax.dynamic_index_in_dim(slot_sequence, group, 0, keepdims=False)
    table = table.reshape(chips, cores, SLOTS)
    held = lax.dynamic_index_in_dim(table, core, 1, keepdims=False)
    code = (held >> 4) * (2 * TOK_GRP) + (held & 15) * DRAFT
    inner = jnp.arange(2, dtype=jnp.int32)[:, None] * TOK_GRP + jnp.arange(DRAFT, dtype=jnp.int32)
    code = code.T[:, :, None] + inner.reshape(-1)
    code = jnp.where((held >= 0).T[:, :, None], code, -1)
    code_row = code.reshape(SLOTS, -1)
    code_col = code.reshape(-1, 1)

    chip = z * xs + x
    mine = lax.dynamic_index_in_dim(held, chip, 0, keepdims=False)
    slabs = lax.dynamic_index_in_dim(slot_slab, group, 0, keepdims=False).reshape(chips, cores, SLOTS)
    slabs = lax.dynamic_index_in_dim(slabs, chip, 0, keepdims=False)
    slabs = lax.dynamic_index_in_dim(slabs, core, 0, keepdims=False)
    is_mine = mine[:, None] == jnp.arange(context_length.shape[0], dtype=jnp.int32)
    length = jnp.sum(jnp.where(is_mine, context_length, 0), axis=1)
    count = jnp.where(mine >= 0, length - slabs * kv_cache.shape[3], 0).astype(jnp.int32)

    narrow = call(
        project_kernel,
        jax.ShapeDtypeStruct((TOK_GRP, NARROW), BF16),
        (q_compressed, w_q_nope, w_q_rope),
        [VMEM] * 3,
    )
    copies = groups * cores
    spread = jnp.broadcast_to(narrow, (copies, *narrow.shape))
    every = lax.all_to_all(spread, ("group", "core"), 0, 0, tiled=True).reshape(-1, NARROW)
    draft_hv, draft_log = call(
        draft_kernel,
        (
            jax.ShapeDtypeStruct((TOK_GRP, 2 * VDIM), F32),
            jax.ShapeDtypeStruct((TOK_GRP, 128), F32),
        ),
        (narrow, w_uk, w_uv, draft_kv),
        [VMEM] * 4,
    )
    rows = chips * cores * DRAFT
    wide = call(
        spread_kernel,
        jax.ShapeDtypeStruct((rows, SLOTS * WIDE), BF16),
        (core_id, every, code_col, w_uk, mate_uk),
        [SMEM] + [VMEM] * 4,
        [pltpu.VMEM((copies * TOK_GRP, 5 * NOPE), BF16)],
    )
    arrived = exchange(wide, ("z", "x"), chips)
    partials = attend(count, arrived, kv_cache.reshape(kv_cache.shape[2:]))
    back = exchange(partials, ("z", "x"), chips)
    merged = call(
        merge_kernel,
        jax.ShapeDtypeStruct((copies * TOK_GRP, NARROW), BF16),
        (core_id, back, code_row, w_uv, mate_uv),
        [SMEM] + [VMEM] * 4,
    )
    home = exchange(merged, ("group", "core"), copies)
    token = jnp.arange(TOK_GRP, dtype=jnp.int32).reshape(zs, xs, cores)
    token = token.transpose(2, 1, 0).reshape(-1, 1)
    order = (token == jnp.arange(TOK_GRP, dtype=jnp.int32)).astype(BF16)
    head_values = call(
        finish_kernel,
        jax.ShapeDtypeStruct((TOK_GRP, 2 * VDIM), BF16),
        (home, draft_hv, draft_log, order),
        [VMEM] * 4,
    )
    sums = jnp.dot(head_values, w_o, preferred_element_type=F32)
    for axis, peers in (("core", cores), ("x", xs), ("z", zs)):
        sums = sums.astype(BF16).reshape(peers, -1, w_o.shape[1])
        tiles = lax.all_to_all(sums, axis, 0, 0, tiled=True)
        sums = jnp.sum(tiles.astype(F32), axis=0)
    return sums


def solution(mesh):
    fine = Mesh(mesh.devices.reshape(4, 8, 4, 2), ("group", "z", "x", "core"))
    dev = ("z", "x", "core")
    placed = (
        P("group", None),
        P(None, dev),
        P(None, dev),
        P(dev, None, None),
        P(dev, None, None),
        P(dev, None),
        P("group", dev, None, None, None),
        P("group", None),
        P(),
        P(),
        P(),
    )
    return jax.shard_map(
        shards, mesh=fine, in_specs=placed, out_specs=P(("group", *dev), None), check_vma=False
    )
```

```python
import jax
import jax.numpy as jnp
from jax import lax
from jax.experimental import pallas as pl
from jax.experimental.pallas import tpu as pltpu
from jax.sharding import Mesh
from jax.sharding import PartitionSpec as P

NOPE = 128
ROPE = 64
LATENT = 512
VDIM = 128
DRAFT = 4
SEQ_GRP = 16
TOK_GRP = SEQ_GRP * DRAFT
SLOTS = 2
KEY = LATENT + ROPE
WIDE = 2 * LATENT + 2 * ROPE
PART = SLOTS * 2 * LATENT + 128
NARROW = 2 * NOPE + 2 * ROPE
EMPTY = -1e30
SCALE = (NOPE + ROPE) ** -0.5
F32 = jnp.float32
BF16 = jnp.bfloat16
CONTRACT_LAST = (((1,), (1,)), ((), ()))

VMEM = pl.BlockSpec(memory_space=pltpu.VMEM)
SMEM = pl.BlockSpec(memory_space=pltpu.SMEM)


def dot(a, b):
    return jnp.dot(a, b, preferred_element_type=F32)


def dot_t(a, b):
    return lax.dot_general(a, b, CONTRACT_LAST, preferred_element_type=F32)


def call(kernel, outs, args, specs, scratch=(), vmem=32):
    return pl.pallas_call(
        kernel,
        out_shape=outs,
        in_specs=specs,
        out_specs=jax.tree.map(lambda _: VMEM, outs),
        scratch_shapes=list(scratch),
        compiler_params=pltpu.CompilerParams(vmem_limit_bytes=vmem << 20),
    )(*args)


def three_terms(value):
    high = value.astype(BF16).astype(F32)
    middle = (value - high).astype(BF16).astype(F32)
    return high, middle, (value - high - middle).astype(BF16).astype(F32)


def put_terms(tile, value, first):
    lane = lax.broadcasted_iota(jnp.int32, tile.shape, 1)
    for i, term in enumerate(three_terms(value)):
        tile = jnp.where(lane == first + i, term, tile)
    return tile


def project_kernel(q_ref, wn_ref, wr_ref, out_ref):
    narrow = dot(q_ref[...], wn_ref[...]).astype(BF16)
    ropes = (dot(q_ref[...], wr_ref[...]) * SCALE).astype(BF16)
    for copy in range(out_ref.shape[0]):
        out_ref[copy, :, : 2 * NOPE] = narrow
        out_ref[copy, :, 2 * NOPE :] = ropes


def spread_kernel(core_ref, q_ref, code_ref, own_ref, mate_ref, out_ref, rows):
    core = core_ref[0]
    rows[...] = jnp.zeros_like(rows)
    for block in range(q_ref.shape[0] // TOK_GRP):
        at = pl.ds(block * TOK_GRP, TOK_GRP)
        side = pl.multiple_of(jnp.where(core == block % 2, 0, NOPE), NOPE)
        for par in range(2):
            rows[at, pl.ds(par * 2 * NOPE + side, NOPE)] = q_ref[at, par * NOPE : (par + 1) * NOPE]
        rows[at, 4 * NOPE :] = q_ref[at, 2 * NOPE :]
    count = code_ref.shape[0] // SLOTS
    for slot in range(SLOTS):
        code = code_ref[slot * count : (slot + 1) * count, :]
        column = lax.broadcasted_iota(jnp.int32, (count, rows.shape[0]), 1)
        picked = dot(jnp.where(column == code, 1.0, 0.0).astype(BF16), rows[...]).astype(BF16)
        for par in range(2):
            weight = jnp.concatenate([own_ref[par], mate_ref[par]], axis=0)
            absorbed = dot(picked[:, par * 2 * NOPE : (par + 1) * 2 * NOPE], weight) * SCALE
            first = slot * WIDE + par * LATENT
            out_ref[:, first : first + LATENT] = absorbed.astype(BF16)
        out_ref[:, slot * WIDE + 2 * LATENT : (slot + 1) * WIDE] = picked[:, 4 * NOPE :]


def draft_kernel(place_ref, q_ref, own_uk, mate_uk, own_uv, mate_uv, kv_ref, hv_ref, log_ref):
    group, core = place_ref[0], place_ref[1]
    half = hv_ref.shape[0]
    row = 2 * lax.broadcasted_iota(jnp.int32, (half, TOK_GRP), 0) + core
    col = lax.broadcasted_iota(jnp.int32, (half, TOK_GRP), 1)
    seen = (row // DRAFT == col // DRAFT) & (col <= row)
    pick = jnp.where(row == col, 1.0, 0.0).astype(BF16)
    lane = lax.broadcasted_iota(jnp.int32, log_ref.shape, 1)
    logs = jnp.zeros(log_ref.shape, F32)
    for hp in range(2):
        at = pl.multiple_of((group * 2 + hp) * TOK_GRP, TOK_GRP)
        rows = dot(pick, q_ref[pl.ds(at, TOK_GRP), :]).astype(BF16)
        for par in range(2):
            uk = jnp.where(core == hp, own_uk[par], mate_uk[par])
            uv = jnp.where(core == hp, own_uv[par], mate_uv[par])
            absorbed = (dot(rows[:, par * NOPE : (par + 1) * NOPE], uk) * SCALE).astype(BF16)
            first = 2 * NOPE + par * ROPE
            scores = dot_t(absorbed, kv_ref[:, :LATENT])
            scores += dot_t(rows[:, first : first + ROPE], kv_ref[:, LATENT:])
            scores = jnp.where(seen, scores, EMPTY)
            peak = jnp.max(scores, axis=1, keepdims=True)
            weights = jnp.where(seen, jnp.exp(scores - peak), 0.0)
            total = jnp.sum(weights, axis=1, keepdims=True)
            mixture = dot(weights.astype(BF16), kv_ref[:, :LATENT]) / total
            head = hp * 2 + par
            hv_ref[:, head * VDIM : (head + 1) * VDIM] = dot(mixture.astype(BF16), uv)
            logs = jnp.where(lane == head, peak + jnp.log(total), logs)
    log_ref[...] = logs


def attend_kernel(count_ref, x_ref, kv_ref, out_ref, queries, scores):
    slot = pl.program_id(0)
    count = count_ref[slot]
    half = x_ref.shape[0]
    for par in range(2):
        at = slice(par * half, (par + 1) * half)
        queries[at, :LATENT] = x_ref[:, par * LATENT : (par + 1) * LATENT]
        first = 2 * LATENT + par * ROPE
        queries[at, LATENT:] = x_ref[:, first : first + ROPE]
    slab = kv_ref.shape[1]
    chunk = 512
    peak = jnp.full((2 * half, 1), EMPTY, F32)
    for first in range(0, slab, chunk):
        score = dot(queries[...], kv_ref[:, first : first + chunk])
        position = lax.broadcasted_iota(jnp.int32, score.shape, 1) + first
        score = jnp.where(position < count, score, EMPTY)
        scores[:, first : first + chunk] = score
        peak = jnp.maximum(peak, jnp.max(score, axis=1, keepdims=True))
    reference = jnp.maximum(peak, EMPTY / 10)
    total = jnp.zeros((2 * half, 1), F32)
    mixture = jnp.zeros((2 * half, LATENT), F32)
    for first in range(0, slab, chunk):
        weights = jnp.exp(scores[:, first : first + chunk] - reference)
        total += jnp.sum(weights, axis=1, keepdims=True)
        mixture += dot_t(weights.astype(BF16), kv_ref[:LATENT, first : first + chunk])
    total = jnp.maximum(total, 1.0)
    mixture = (mixture / total).astype(BF16)
    log = peak + jnp.log(total)
    start = slot * 2 * LATENT
    lane = lax.broadcasted_iota(jnp.int32, (half, 128), 1)
    tile = jnp.where(slot == 0, jnp.zeros((half, 128), F32), out_ref[:, SLOTS * 2 * LATENT :].astype(F32))
    for par in range(2):
        at = slice(par * half, (par + 1) * half)
        out_ref[:, pl.ds(pl.multiple_of(start + par * LATENT, LATENT), LATENT)] = mixture[at]
        for i, term in enumerate(three_terms(log[at])):
            tile = jnp.where(lane == slot * 6 + par * 3 + i, term, tile)
    out_ref[:, SLOTS * 2 * LATENT :] = tile.astype(BF16)


def attend(count, x, kv):
    rows = x.shape[0]
    slab = kv.shape[2]
    return pl.pallas_call(
        attend_kernel,
        out_shape=jax.ShapeDtypeStruct((rows, PART), BF16),
        grid_spec=pltpu.PrefetchScalarGridSpec(
            num_scalar_prefetch=1,
            grid=(SLOTS,),
            in_specs=[
                pl.BlockSpec((rows, WIDE), lambda k, _: (0, k)),
                pl.BlockSpec((None, KEY, slab), lambda k, _: (k, 0, 0)),
            ],
            out_specs=pl.BlockSpec((rows, PART), lambda k, _: (0, 0)),
            scratch_shapes=[
                pltpu.VMEM((2 * rows, KEY), BF16),
                pltpu.VMEM((2 * rows, slab), F32),
            ],
        ),
        compiler_params=pltpu.CompilerParams(
            dimension_semantics=("arbitrary",), vmem_limit_bytes=48 << 20
        ),
    )(count, x, kv)


def merge_kernel(core_ref, y_ref, code_ref, own_ref, mate_ref, out_ref):
    core = core_ref[0]
    rows, cols = out_ref.shape[0], y_ref.shape[0]
    base = SLOTS * 2 * LATENT
    logs = jnp.transpose(y_ref[:, base:].astype(F32))
    row = lax.broadcasted_iota(jnp.int32, (rows, cols), 0)
    tile = jnp.zeros((rows, 128), F32)
    for hp in range(2):
        match = [row == code_ref[hp * 2 + slot : hp * 2 + slot + 1, :] for slot in range(SLOTS)]
        for par in range(2):
            held = []
            for slot in range(SLOTS):
                at = slot * 6 + par * 3
                log = logs[at : at + 1, :] + logs[at + 1 : at + 2, :] + logs[at + 2 : at + 3, :]
                held.append(jnp.where(match[slot], log, EMPTY))
            peak = jnp.max(jnp.maximum(held[0], held[1]), axis=1, keepdims=True)
            total = jnp.zeros((rows, 1), F32)
            mixture = jnp.zeros((rows, LATENT), F32)
            for slot in range(SLOTS):
                weights = jnp.where(match[slot], jnp.exp(held[slot] - peak), 0.0)
                total += jnp.sum(weights, axis=1, keepdims=True)
                first = slot * 2 * LATENT + par * LATENT
                mixture += dot(weights.astype(BF16), y_ref[:, first : first + LATENT])
            total = jnp.maximum(total, 1.0)
            mixture = (mixture / total).astype(BF16)
            head = hp * 2 + par
            values = dot(mixture, jnp.where(core == hp, own_ref[par], mate_ref[par]))
            out_ref[:, head * VDIM : (head + 1) * VDIM] = values.astype(BF16)
            tile = put_terms(tile, peak + jnp.log(total), head * 3)
    out_ref[:, 4 * VDIM :] = tile.astype(BF16)


def finish_kernel(core_ref, z_ref, hv_ref, log_ref, own_ref, mate_ref, out_ref):
    half = hv_ref.shape[0]
    values = []
    for head in range(4):
        logs = [log_ref[:, head : head + 1]]
        parts = [hv_ref[:, head * VDIM : (head + 1) * VDIM]]
        for block in range(z_ref.shape[0] // half):
            at = slice(block * half, (block + 1) * half)
            terms = z_ref[at, 4 * VDIM :].astype(F32)
            first = head * 3
            logs.append(
                terms[:, first : first + 1]
                + terms[:, first + 1 : first + 2]
                + terms[:, first + 2 : first + 3]
            )
            parts.append(z_ref[at, head * VDIM : (head + 1) * VDIM].astype(F32))
        peak = logs[0]
        for log in logs[1:]:
            peak = jnp.maximum(peak, log)
        total = jnp.zeros_like(peak)
        summed = jnp.zeros_like(parts[0])
        for log, part in zip(logs, parts):
            weight = jnp.exp(log - peak)
            total += weight
            summed += weight * part
        values.append(summed / total)
    pairs = [jnp.concatenate(values[hp * 2 : hp * 2 + 2], axis=1) for hp in range(2)]
    own = jnp.where(core_ref[0] == 0, pairs[0], pairs[1]).astype(BF16)
    mate = jnp.where(core_ref[0] == 0, pairs[1], pairs[0]).astype(BF16)
    out_ref[...] = (dot(own, own_ref[...]) + dot(mate, mate_ref[...])).astype(BF16)


def exchange(array, axes, peers):
    blocks = array.reshape(peers, array.shape[0] // peers, *array.shape[1:])
    return lax.all_to_all(blocks, axes, 0, 0, tiled=True).reshape(array.shape)


def shards(
    q_compressed,
    w_q_nope,
    w_q_rope,
    w_uk,
    w_uv,
    w_o,
    kv_cache,
    draft_kv,
    context_length,
    slot_sequence,
    slot_slab,
):
    groups, zs, xs, cores = (lax.axis_size(a) for a in ("group", "z", "x", "core"))
    group, z, x, core = (lax.axis_index(a) for a in ("group", "z", "x", "core"))
    chips = zs * xs
    core_id = core.astype(jnp.int32).reshape(1)
    swap = [(i, 1 - i) for i in range(cores)]
    mate_uk = lax.ppermute(w_uk, "core", swap)

    table = lax.dynamic_index_in_dim(slot_sequence, group, 0, keepdims=False)
    table = table.reshape(chips, cores, SLOTS)
    held = lax.dynamic_index_in_dim(table, core, 1, keepdims=False)
    hp = jnp.arange(2, dtype=jnp.int32)[:, None]
    draft = jnp.arange(DRAFT, dtype=jnp.int32)
    filled = (held >= 0).T[:, :, None]
    code = ((held >> 4) * (2 * TOK_GRP) + (held & 15) * DRAFT).T[:, :, None]
    code = jnp.where(filled, code + (hp * TOK_GRP + draft).reshape(-1), -1).reshape(-1, 1)
    row = ((held >> 4) * TOK_GRP + (held & 15) * 2).T[:, :, None, None]
    row = row + (draft & 1) * (TOK_GRP // 2) + (draft >> 1)
    row = jnp.where(filled[..., None], row, -1)
    row = jnp.where(hp == hp.reshape(2, 1, 1, 1, 1), row, -1).reshape(2 * SLOTS, -1)

    chip = z * xs + x
    mine = lax.dynamic_index_in_dim(held, chip, 0, keepdims=False)
    slabs = lax.dynamic_index_in_dim(slot_slab, group, 0, keepdims=False).reshape(chips, cores, SLOTS)
    slabs = lax.dynamic_index_in_dim(slabs, chip, 0, keepdims=False)
    slabs = lax.dynamic_index_in_dim(slabs, core, 0, keepdims=False)
    is_mine = mine[:, None] == jnp.arange(context_length.shape[0], dtype=jnp.int32)
    length = jnp.sum(jnp.where(is_mine, context_length, 0), axis=1)
    count = jnp.where(mine >= 0, length - slabs * kv_cache.shape[3], 0).astype(jnp.int32)

    copies = groups * cores
    narrow = pl.pallas_call(
        project_kernel,
        out_shape=jax.ShapeDtypeStruct((copies, TOK_GRP, NARROW), BF16),
        compiler_params=pltpu.CompilerParams(vmem_limit_bytes=32 << 20),
    )(q_compressed, w_q_nope, w_q_rope)
    every = lax.all_to_all(narrow, ("group", "core"), 0, 0, tiled=True).reshape(-1, NARROW)
    rows = chips * cores * DRAFT
    wide = call(
        spread_kernel,
        jax.ShapeDtypeStruct((rows, SLOTS * WIDE), BF16),
        (core_id, every, code, w_uk, mate_uk),
        [SMEM] + [VMEM] * 4,
        [pltpu.VMEM((copies * TOK_GRP, 5 * NOPE), BF16)],
    )
    late_o, late_uv, wide = lax.optimization_barrier((w_o, w_uv, wide))
    mate_uv = lax.ppermute(late_uv, "core", swap)
    mate_o = lax.ppermute(late_o, "core", swap)
    arrived = exchange(wide, ("z", "x"), chips)
    place = jnp.stack([group, core]).astype(jnp.int32)
    draft_hv, draft_log = call(
        draft_kernel,
        (
            jax.ShapeDtypeStruct((TOK_GRP // 2, 4 * VDIM), F32),
            jax.ShapeDtypeStruct((TOK_GRP // 2, 128), F32),
        ),
        (place, every, w_uk, mate_uk, w_uv, mate_uv, draft_kv),
        [SMEM] + [VMEM] * 6,
    )
    partials = attend(count, arrived, jnp.swapaxes(kv_cache.reshape(kv_cache.shape[2:]), 1, 2))
    back = exchange(partials, ("z", "x"), chips)
    merged = call(
        merge_kernel,
        jax.ShapeDtypeStruct((groups * TOK_GRP, 4 * VDIM + 128), BF16),
        (core_id, back, row, w_uv, mate_uv),
        [SMEM] + [VMEM] * 4,
    )
    home = exchange(merged, ("group", "core"), copies)
    sums = call(
        finish_kernel,
        jax.ShapeDtypeStruct((chips, w_o.shape[1]), BF16),
        (core_id, home, draft_hv, draft_log, w_o, mate_o),
        [SMEM] + [VMEM] * 5,
    )
    tiles = lax.all_to_all(sums.reshape(chips, 8, -1), ("z", "x"), 0, 0, tiled=True)
    return jnp.sum(tiles.astype(F32), axis=0).reshape(1, -1)


def solution(mesh):
    fine = Mesh(mesh.devices.reshape(4, 8, 4, 2), ("group", "z", "x", "core"))
    dev = ("z", "x", "core")
    placed = (
        P("group", None),
        P(None, dev),
        P(None, dev),
        P(dev, None, None),
        P(dev, None, None),
        P(dev, None),
        P("group", dev, None, None, None),
        P("group", None),
        P(),
        P(),
        P(),
    )
    return jax.shard_map(
        shards, mesh=fine, in_specs=placed, out_specs=P(("group", *dev), None), check_vma=False
    )
```

```python
import jax
import jax.numpy as jnp
from jax import lax
from jax.experimental import pallas as pl
from jax.experimental.pallas import tpu as pltpu
from jax.sharding import Mesh
from jax.sharding import PartitionSpec as P

NOPE = 128
ROPE = 64
LATENT = 512
VDIM = 128
DRAFT = 4
SEQ_GRP = 16
TOK_GRP = SEQ_GRP * DRAFT
SLOTS = 2
KEY = LATENT + ROPE
WIDE = 2 * LATENT + 2 * ROPE
PART = SLOTS * 2 * LATENT + 128
NARROW = 2 * NOPE + 2 * ROPE
PIECES = 4
EMPTY = -1e30
SCALE = (NOPE + ROPE) ** -0.5
F32 = jnp.float32
BF16 = jnp.bfloat16
CONTRACT_LAST = (((1,), (1,)), ((), ()))

VMEM = pl.BlockSpec(memory_space=pltpu.VMEM)
SMEM = pl.BlockSpec(memory_space=pltpu.SMEM)
HBM = pl.BlockSpec(memory_space=pltpu.HBM)


def in_hbm(array):
    return pltpu.with_memory_space_constraint(array, pltpu.HBM)


def dot(a, b):
    return jnp.dot(a, b, preferred_element_type=F32)


def dot_t(a, b):
    return lax.dot_general(a, b, CONTRACT_LAST, preferred_element_type=F32)


def call(kernel, outs, args, specs, scratch=(), vmem=32):
    return pl.pallas_call(
        kernel,
        out_shape=outs,
        in_specs=specs,
        out_specs=jax.tree.map(lambda _: VMEM, outs),
        scratch_shapes=list(scratch),
        compiler_params=pltpu.CompilerParams(vmem_limit_bytes=vmem << 20),
    )(*args)


def three_terms(value):
    high = value.astype(BF16).astype(F32)
    middle = (value - high).astype(BF16).astype(F32)
    return high, middle, (value - high - middle).astype(BF16).astype(F32)


def put_terms(tile, value, first):
    lane = lax.broadcasted_iota(jnp.int32, tile.shape, 1)
    for i, term in enumerate(three_terms(value)):
        tile = jnp.where(lane == first + i, term, tile)
    return tile


def project_kernel(q_hbm, wn_hbm, wr_hbm, out_ref, q_ref, wn_ref, wr_ref, sems):
    copies = []
    depth = wn_ref.shape[0] // 2
    for i, (source, target) in enumerate(((q_hbm, q_ref), (wr_hbm, wr_ref))):
        copies.append(pltpu.make_async_copy(source, target, sems.at[i]))
    for i in range(2):
        at = pl.ds(i * depth, depth)
        copies.append(pltpu.make_async_copy(wn_hbm.at[at], wn_ref.at[at], sems.at[2 + i]))
    for copy in copies:
        copy.start()
    copies[0].wait()
    copies[1].wait()
    ropes = (dot(q_ref[...], wr_ref[...]) * SCALE).astype(BF16)
    copies[2].wait()
    copies[3].wait()
    narrow = dot(q_ref[...], wn_ref[...]).astype(BF16)
    for copy in range(out_ref.shape[0]):
        out_ref[copy, :, : 2 * NOPE] = narrow
        out_ref[copy, :, 2 * NOPE :] = ropes


def spread_kernel(core_ref, q_ref, code_ref, own_ref, mate_ref, out_ref, rows):
    core = core_ref[0]

    @pl.when(pl.program_id(0) == 0)
    def _():
        rows[...] = jnp.zeros_like(rows)
        for block in range(q_ref.shape[0] // TOK_GRP):
            at = pl.ds(block * TOK_GRP, TOK_GRP)
            side = pl.multiple_of(jnp.where(core == block % 2, 0, NOPE), NOPE)
            for par in range(2):
                part = q_ref[at, par * NOPE : (par + 1) * NOPE]
                rows[at, pl.ds(par * 2 * NOPE + side, NOPE)] = part
            rows[at, 4 * NOPE :] = q_ref[at, 2 * NOPE :]

    column = lax.broadcasted_iota(jnp.int32, (code_ref.shape[0], rows.shape[0]), 1)
    pick = jnp.where(column == code_ref[...], 1.0, 0.0).astype(BF16)
    picked = dot(pick, rows[...]).astype(BF16)
    for par in range(2):
        weight = jnp.concatenate([own_ref[par], mate_ref[par]], axis=0)
        absorbed = dot(picked[:, par * 2 * NOPE : (par + 1) * 2 * NOPE], weight) * SCALE
        out_ref[:, par * LATENT : (par + 1) * LATENT] = absorbed.astype(BF16)
    out_ref[:, 2 * LATENT :] = picked[:, 4 * NOPE :]


def draft_kernel(place_ref, q_ref, own_uk, mate_uk, own_uv, mate_uv, kv_ref, hv_ref, log_ref):
    group, core = place_ref[0], place_ref[1]
    half = hv_ref.shape[0]
    row = 2 * lax.broadcasted_iota(jnp.int32, (half, TOK_GRP), 0) + core
    col = lax.broadcasted_iota(jnp.int32, (half, TOK_GRP), 1)
    seen = (row // DRAFT == col // DRAFT) & (col <= row)
    pick = jnp.where(row == col, 1.0, 0.0).astype(BF16)
    lane = lax.broadcasted_iota(jnp.int32, log_ref.shape, 1)
    logs = jnp.zeros(log_ref.shape, F32)
    for hp in range(2):
        at = pl.multiple_of((group * 2 + hp) * TOK_GRP, TOK_GRP)
        rows = dot(pick, q_ref[pl.ds(at, TOK_GRP), :]).astype(BF16)
        for par in range(2):
            uk = jnp.where(core == hp, own_uk[par], mate_uk[par])
            uv = jnp.where(core == hp, own_uv[par], mate_uv[par])
            absorbed = (dot(rows[:, par * NOPE : (par + 1) * NOPE], uk) * SCALE).astype(BF16)
            first = 2 * NOPE + par * ROPE
            scores = dot_t(absorbed, kv_ref[:, :LATENT])
            scores += dot_t(rows[:, first : first + ROPE], kv_ref[:, LATENT:])
            scores = jnp.where(seen, scores, EMPTY)
            peak = jnp.max(scores, axis=1, keepdims=True)
            weights = jnp.where(seen, jnp.exp(scores - peak), 0.0)
            total = jnp.sum(weights, axis=1, keepdims=True)
            mixture = dot(weights.astype(BF16), kv_ref[:, :LATENT]) / total
            head = hp * 2 + par
            hv_ref[:, head * VDIM : (head + 1) * VDIM] = dot(mixture.astype(BF16), uv)
            logs = jnp.where(lane == head, peak + jnp.log(total), logs)
    log_ref[...] = logs


def attend_kernel(count_ref, x_ref, kv_hbm, out_hbm, queries, scores, out_ref, kv_ref, sems, in_sems):
    half = x_ref.shape[0]
    slab = kv_ref.shape[2]
    chunk = 256
    piece = slab // PIECES
    arriving = []
    for i in range(SLOTS * PIECES):
        at = (i // PIECES, slice(None), pl.ds(i % PIECES * piece, piece))
        arriving.append(pltpu.make_async_copy(kv_hbm.at[at], kv_ref.at[at], in_sems.at[i]))
        arriving[-1].start()
    base = SLOTS * 2 * LATENT
    lane = lax.broadcasted_iota(jnp.int32, (half, 128), 1)
    tile = jnp.zeros((half, 128), F32)
    copies = []
    for slot in range(SLOTS):
        count = count_ref[slot]
        for par in range(2):
            at = slice(par * half, (par + 1) * half)
            first = slot * WIDE + par * LATENT
            queries[at, :LATENT] = x_ref[:, first : first + LATENT]
            first = slot * WIDE + 2 * LATENT + par * ROPE
            queries[at, LATENT:] = x_ref[:, first : first + ROPE]
        peak = jnp.full((2 * half, 1), EMPTY, F32)
        for first in range(0, slab, chunk):
            if first % piece == 0:
                arriving[slot * PIECES + first // piece].wait()
            score = dot(queries[...], kv_ref[slot, :, first : first + chunk])
            position = lax.broadcasted_iota(jnp.int32, score.shape, 1) + first
            score = jnp.where(position < count, score, EMPTY)
            scores[:, first : first + chunk] = score
            peak = jnp.maximum(peak, jnp.max(score, axis=1, keepdims=True))
        reference = jnp.maximum(peak, EMPTY / 10)
        total = jnp.zeros((2 * half, 1), F32)
        mixture = jnp.zeros((2 * half, LATENT), F32)
        for first in range(0, slab, chunk):
            weights = jnp.exp(scores[:, first : first + chunk] - reference)
            total += jnp.sum(weights, axis=1, keepdims=True)
            mixture += dot_t(weights.astype(BF16), kv_ref[slot, :LATENT, first : first + chunk])
        total = jnp.maximum(total, 1.0)
        mixture = (mixture * (1.0 / total)).astype(BF16)
        log = peak + jnp.log(total)
        start = slot * 2 * LATENT
        for par in range(2):
            at = slice(par * half, (par + 1) * half)
            out_ref[:, start + par * LATENT : start + (par + 1) * LATENT] = mixture[at]
            for i, term in enumerate(three_terms(log[at])):
                tile = jnp.where(lane == slot * 6 + par * 3 + i, term, tile)
        end = start + 2 * LATENT
        if slot == SLOTS - 1:
            out_ref[:, base:] = tile.astype(BF16)
            end = PART
        at = pl.ds(start, end - start)
        copies.append(pltpu.make_async_copy(out_ref.at[:, at], out_hbm.at[:, at], sems.at[slot]))
        copies[-1].start()
    for copy in copies:
        copy.wait()


def attend(count, x, kv):
    rows = x.shape[0]
    return pl.pallas_call(
        attend_kernel,
        out_shape=jax.ShapeDtypeStruct((rows, PART), BF16),
        in_specs=[SMEM, VMEM, HBM],
        out_specs=HBM,
        scratch_shapes=[
            pltpu.VMEM((2 * rows, KEY), BF16),
            pltpu.VMEM((2 * rows, kv.shape[2]), F32),
            pltpu.VMEM((rows, PART), BF16),
            pltpu.VMEM(kv.shape, BF16),
            pltpu.SemaphoreType.DMA((SLOTS,)),
            pltpu.SemaphoreType.DMA((SLOTS * PIECES,)),
        ],
        compiler_params=pltpu.CompilerParams(vmem_limit_bytes=32 << 20),
    )(count, x, in_hbm(kv))


def merge_kernel(core_ref, y_ref, code_ref, own_ref, mate_ref, out_ref):
    core = core_ref[0]
    rows, cols = out_ref.shape[0], y_ref.shape[0]
    base = SLOTS * 2 * LATENT
    logs = jnp.transpose(y_ref[:, base:].astype(F32))
    row = lax.broadcasted_iota(jnp.int32, (rows, cols), 0)
    tile = jnp.zeros((rows, 128), F32)
    for hp in range(2):
        match = [row == code_ref[hp * 2 + slot : hp * 2 + slot + 1, :] for slot in range(SLOTS)]
        for par in range(2):
            held = []
            for slot in range(SLOTS):
                at = slot * 6 + par * 3
                log = logs[at : at + 1, :] + logs[at + 1 : at + 2, :] + logs[at + 2 : at + 3, :]
                held.append(jnp.where(match[slot], log, EMPTY))
            peak = jnp.max(jnp.maximum(held[0], held[1]), axis=1, keepdims=True)
            total = jnp.zeros((rows, 1), F32)
            mixture = jnp.zeros((rows, LATENT), F32)
            for slot in range(SLOTS):
                weights = jnp.where(match[slot], jnp.exp(held[slot] - peak), 0.0)
                total += jnp.sum(weights, axis=1, keepdims=True)
                first = slot * 2 * LATENT + par * LATENT
                mixture += dot(weights.astype(BF16), y_ref[:, first : first + LATENT])
            total = jnp.maximum(total, 1.0)
            mixture = (mixture / total).astype(BF16)
            head = hp * 2 + par
            values = dot(mixture, jnp.where(core == hp, own_ref[par], mate_ref[par]))
            out_ref[:, head * VDIM : (head + 1) * VDIM] = values.astype(BF16)
            tile = put_terms(tile, peak + jnp.log(total), head * 3)
    out_ref[:, 4 * VDIM :] = tile.astype(BF16)


def finish_kernel(core_ref, z_ref, hv_ref, log_ref, own_hbm, mate_hbm, out_ref, o_ref, sems):
    half = hv_ref.shape[0]
    piece = out_ref.shape[1] // PIECES
    arriving = []
    for i in range(PIECES):
        at = (slice(None), pl.ds(i * piece, piece))
        for side, source in enumerate((own_hbm, mate_hbm)):
            target = o_ref.at[side].at[at]
            arriving.append(pltpu.make_async_copy(source.at[at], target, sems.at[2 * i + side]))
            arriving[-1].start()
    values = []
    for head in range(4):
        logs = [log_ref[:, head : head + 1]]
        parts = [hv_ref[:, head * VDIM : (head + 1) * VDIM]]
        for block in range(z_ref.shape[0] // half):
            at = slice(block * half, (block + 1) * half)
            terms = z_ref[at, 4 * VDIM :].astype(F32)
            first = head * 3
            logs.append(
                terms[:, first : first + 1]
                + terms[:, first + 1 : first + 2]
                + terms[:, first + 2 : first + 3]
            )
            parts.append(z_ref[at, head * VDIM : (head + 1) * VDIM].astype(F32))
        peak = logs[0]
        for log in logs[1:]:
            peak = jnp.maximum(peak, log)
        total = jnp.zeros_like(peak)
        summed = jnp.zeros_like(parts[0])
        for log, part in zip(logs, parts):
            weight = jnp.exp(log - peak)
            total += weight
            summed += weight * part
        values.append(summed / total)
    pairs = [jnp.concatenate(values[hp * 2 : hp * 2 + 2], axis=1) for hp in range(2)]
    own = jnp.where(core_ref[0] == 0, pairs[0], pairs[1]).astype(BF16)
    mate = jnp.where(core_ref[0] == 0, pairs[1], pairs[0]).astype(BF16)
    for i in range(PIECES):
        arriving[2 * i].wait()
        arriving[2 * i + 1].wait()
        at = slice(i * piece, (i + 1) * piece)
        out_ref[:, at] = (dot(own, o_ref[0, :, at]) + dot(mate, o_ref[1, :, at])).astype(BF16)


def total_kernel(tiles_ref, out_ref):
    total = jnp.sum(tiles_ref[...].astype(F32), axis=0)
    width = total.shape[1]
    for i in range(total.shape[0]):
        out_ref[:, i * width : (i + 1) * width] = total[i : i + 1]


def exchange(array, axes, peers):
    blocks = array.reshape(peers, array.shape[0] // peers, *array.shape[1:])
    return lax.all_to_all(blocks, axes, 0, 0, tiled=True).reshape(array.shape)


def shards(
    q_compressed,
    w_q_nope,
    w_q_rope,
    w_uk,
    w_uv,
    w_o,
    kv_cache,
    draft_kv,
    context_length,
    slot_sequence,
    slot_slab,
):
    groups, zs, xs, cores = (lax.axis_size(a) for a in ("group", "z", "x", "core"))
    group, z, x, core = (lax.axis_index(a) for a in ("group", "z", "x", "core"))
    chips = zs * xs
    core_id = core.astype(jnp.int32).reshape(1)
    swap = [(i, 1 - i) for i in range(cores)]
    mate_uk = lax.ppermute(w_uk, "core", swap)

    table = lax.dynamic_index_in_dim(slot_sequence, group, 0, keepdims=False)
    table = table.reshape(chips, cores, SLOTS)
    held = lax.dynamic_index_in_dim(table, core, 1, keepdims=False)
    hp = jnp.arange(2, dtype=jnp.int32)[:, None]
    draft = jnp.arange(DRAFT, dtype=jnp.int32)
    filled = (held >= 0).T[:, :, None]
    code = ((held >> 4) * (2 * TOK_GRP) + (held & 15) * DRAFT).T[:, :, None]
    code = jnp.where(filled, code + (hp * TOK_GRP + draft).reshape(-1), -1).reshape(-1, 1)
    row = ((held >> 4) * TOK_GRP + (held & 15) * 2).T[:, :, None, None]
    row = row + (draft & 1) * (TOK_GRP // 2) + (draft >> 1)
    row = jnp.where(filled[..., None], row, -1)
    row = jnp.where(hp == hp.reshape(2, 1, 1, 1, 1), row, -1).reshape(2 * SLOTS, -1)

    chip = z * xs + x
    mine = lax.dynamic_index_in_dim(held, chip, 0, keepdims=False)
    slabs = lax.dynamic_index_in_dim(slot_slab, group, 0, keepdims=False).reshape(chips, cores, SLOTS)
    slabs = lax.dynamic_index_in_dim(slabs, chip, 0, keepdims=False)
    slabs = lax.dynamic_index_in_dim(slabs, core, 0, keepdims=False)
    is_mine = mine[:, None] == jnp.arange(context_length.shape[0], dtype=jnp.int32)
    length = jnp.sum(jnp.where(is_mine, context_length, 0), axis=1)
    count = jnp.where(mine >= 0, length - slabs * kv_cache.shape[3], 0).astype(jnp.int32)

    copies = groups * cores
    narrow = pl.pallas_call(
        project_kernel,
        out_shape=jax.ShapeDtypeStruct((copies, TOK_GRP, NARROW), BF16),
        in_specs=[HBM] * 3,
        out_specs=VMEM,
        scratch_shapes=[
            *(pltpu.VMEM(a.shape, BF16) for a in (q_compressed, w_q_nope, w_q_rope)),
            pltpu.SemaphoreType.DMA((4,)),
        ],
        compiler_params=pltpu.CompilerParams(vmem_limit_bytes=16 << 20),
    )(*(in_hbm(a) for a in (q_compressed, w_q_nope, w_q_rope)))
    every = lax.all_to_all(narrow, ("group", "core"), 0, 0, tiled=True).reshape(-1, NARROW)
    rows = chips * cores * DRAFT
    wide = pl.pallas_call(
        spread_kernel,
        out_shape=jax.ShapeDtypeStruct((rows, SLOTS * WIDE), BF16),
        grid=(SLOTS,),
        in_specs=[SMEM, VMEM, pl.BlockSpec((rows, 1), lambda k: (k, 0)), VMEM, VMEM],
        out_specs=pl.BlockSpec((rows, WIDE), lambda k: (0, k)),
        scratch_shapes=[pltpu.VMEM((copies * TOK_GRP, 5 * NOPE), BF16)],
        compiler_params=pltpu.CompilerParams(
            dimension_semantics=("arbitrary",), vmem_limit_bytes=16 << 20
        ),
    )(core_id, every, code, w_uk, mate_uk)
    slabs_kv = jnp.swapaxes(kv_cache.reshape(kv_cache.shape[2:]), 1, 2)
    late_o, late_uv, wide = lax.optimization_barrier((w_o, w_uv, wide))
    mate_uv = lax.ppermute(late_uv, "core", swap)
    mate_o = lax.ppermute(late_o, "core", swap)
    arrived = exchange(wide, ("z", "x"), chips)
    place = jnp.stack([group, core]).astype(jnp.int32)
    draft_hv, draft_log = call(
        draft_kernel,
        (
            jax.ShapeDtypeStruct((TOK_GRP // 2, 4 * VDIM), F32),
            jax.ShapeDtypeStruct((TOK_GRP // 2, 128), F32),
        ),
        (place, every, w_uk, mate_uk, w_uv, mate_uv, draft_kv),
        [SMEM] + [VMEM] * 6,
    )
    partials = attend(count, arrived, slabs_kv)
    back = exchange(partials, ("z", "x"), chips)
    merged = call(
        merge_kernel,
        jax.ShapeDtypeStruct((groups * TOK_GRP, 4 * VDIM + 128), BF16),
        (core_id, back, row, w_uv, mate_uv),
        [SMEM] + [VMEM] * 4,
    )
    home = exchange(merged, ("group", "core"), copies)
    sums = call(
        finish_kernel,
        jax.ShapeDtypeStruct((chips, w_o.shape[1]), BF16),
        (core_id, home, draft_hv, draft_log, in_hbm(w_o), in_hbm(mate_o)),
        [SMEM, VMEM, VMEM, VMEM, HBM, HBM],
        [pltpu.VMEM((2, *w_o.shape), BF16), pltpu.SemaphoreType.DMA((2 * PIECES,))],
    )
    tiles = lax.all_to_all(sums.reshape(chips, 8, -1), ("z", "x"), 0, 0, tiled=True)
    return call(
        total_kernel, jax.ShapeDtypeStruct((1, w_o.shape[1]), F32), (tiles,), [VMEM]
    )


def solution(mesh):
    fine = Mesh(mesh.devices.reshape(4, 8, 4, 2), ("group", "z", "x", "core"))
    dev = ("z", "x", "core")
    placed = (
        P("group", None),
        P(None, dev),
        P(None, dev),
        P(dev, None, None),
        P(dev, None, None),
        P(dev, None),
        P("group", dev, None, None, None),
        P("group", None),
        P(),
        P(),
        P(),
    )
    return jax.shard_map(
        shards, mesh=fine, in_specs=placed, out_specs=P(("group", *dev), None), check_vma=False
    )
```

```python
import jax
import jax.numpy as jnp
from jax import lax
from jax.experimental import pallas as pl
from jax.experimental.pallas import tpu as pltpu
from jax.sharding import Mesh
from jax.sharding import PartitionSpec as P

NOPE = 128
ROPE = 64
LATENT = 512
VDIM = 128
DRAFT = 4
SEQ_GRP = 16
TOK_GRP = SEQ_GRP * DRAFT
SLOTS = 2
KEY = LATENT + ROPE
WIDE = 2 * LATENT + 2 * ROPE
PART = SLOTS * 2 * LATENT + 128
NARROW = 2 * NOPE + 2 * ROPE
PIECES = 4
EMPTY = -1e30
SCALE = (NOPE + ROPE) ** -0.5
F32 = jnp.float32
BF16 = jnp.bfloat16
CONTRACT_LAST = (((1,), (1,)), ((), ()))

VMEM = pl.BlockSpec(memory_space=pltpu.VMEM)
SMEM = pl.BlockSpec(memory_space=pltpu.SMEM)
HBM = pl.BlockSpec(memory_space=pltpu.HBM)


def in_hbm(array):
    return pltpu.with_memory_space_constraint(array, pltpu.HBM)


def dot(a, b):
    return jnp.dot(a, b, preferred_element_type=F32)


def dot_t(a, b):
    return lax.dot_general(a, b, CONTRACT_LAST, preferred_element_type=F32)


def call(kernel, outs, args, specs, scratch=(), vmem=32):
    return pl.pallas_call(
        kernel,
        out_shape=outs,
        in_specs=specs,
        out_specs=jax.tree.map(lambda _: VMEM, outs),
        scratch_shapes=list(scratch),
        compiler_params=pltpu.CompilerParams(vmem_limit_bytes=vmem << 20),
    )(*args)


def three_terms(value):
    high = value.astype(BF16).astype(F32)
    middle = (value - high).astype(BF16).astype(F32)
    return high, middle, (value - high - middle).astype(BF16).astype(F32)


def put_terms(tile, value, first):
    lane = lax.broadcasted_iota(jnp.int32, tile.shape, 1)
    for i, term in enumerate(three_terms(value)):
        tile = jnp.where(lane == first + i, term, tile)
    return tile


def project_kernel(q_hbm, wn_hbm, wr_hbm, out_ref, q_ref, wn_ref, wr_ref, sems):
    copies = []
    depth = wn_ref.shape[0] // 2
    for i, (source, target) in enumerate(((q_hbm, q_ref), (wr_hbm, wr_ref))):
        copies.append(pltpu.make_async_copy(source, target, sems.at[i]))
    for i in range(2):
        at = pl.ds(i * depth, depth)
        copies.append(pltpu.make_async_copy(wn_hbm.at[at], wn_ref.at[at], sems.at[2 + i]))
    for copy in copies:
        copy.start()
    copies[0].wait()
    copies[1].wait()
    out_ref[:, 2 * NOPE :] = (dot(q_ref[...], wr_ref[...]) * SCALE).astype(BF16)
    copies[2].wait()
    copies[3].wait()
    out_ref[:, : 2 * NOPE] = dot(q_ref[...], wn_ref[...]).astype(BF16)


def spread_kernel(own_q, mate_q, code_ref, own_ref, mate_ref, out_ref, rows):
    @pl.when(pl.program_id(0) == 0)
    def _():
        rows[...] = jnp.zeros_like(rows)
        count = own_q.shape[0]
        for rel, q_ref in enumerate((own_q, mate_q)):
            at = slice(rel * count, (rel + 1) * count)
            for par in range(2):
                first = par * 2 * NOPE + rel * NOPE
                rows[at, first : first + NOPE] = q_ref[:, par * NOPE : (par + 1) * NOPE]
            rows[at, 4 * NOPE :] = q_ref[:, 2 * NOPE :]

    column = lax.broadcasted_iota(jnp.int32, (code_ref.shape[0], rows.shape[0]), 1)
    pick = jnp.where(column == code_ref[...], 1.0, 0.0).astype(BF16)
    picked = dot(pick, rows[...]).astype(BF16)
    for par in range(2):
        weight = jnp.concatenate([own_ref[par], mate_ref[par]], axis=0)
        absorbed = dot(picked[:, par * 2 * NOPE : (par + 1) * 2 * NOPE], weight) * SCALE
        out_ref[:, par * LATENT : (par + 1) * LATENT] = absorbed.astype(BF16)
    out_ref[:, 2 * LATENT :] = picked[:, 4 * NOPE :]


def draft_kernel(
    core_ref, own_q, mate_q, own_uk, mate_uk, own_uv, mate_uv, kv_ref, hv_ref, log_ref
):
    core = core_ref[0]
    half = hv_ref.shape[0]
    row = 2 * lax.broadcasted_iota(jnp.int32, (half, TOK_GRP), 0) + core
    col = lax.broadcasted_iota(jnp.int32, (half, TOK_GRP), 1)
    seen = (row // DRAFT == col // DRAFT) & (col <= row)
    pick = jnp.where(row == col, 1.0, 0.0).astype(BF16)
    lane = lax.broadcasted_iota(jnp.int32, log_ref.shape, 1)
    logs = jnp.zeros(log_ref.shape, F32)
    sides = ((core, own_q, own_uk, own_uv), (1 - core, mate_q, mate_uk, mate_uv))
    for hp, q_ref, uk_ref, uv_ref in sides:
        rows = dot(pick, q_ref[:TOK_GRP, :]).astype(BF16)
        for par in range(2):
            narrow = rows[:, par * NOPE : (par + 1) * NOPE]
            absorbed = (dot(narrow, uk_ref[par]) * SCALE).astype(BF16)
            first = 2 * NOPE + par * ROPE
            scores = dot_t(absorbed, kv_ref[:, :LATENT])
            scores += dot_t(rows[:, first : first + ROPE], kv_ref[:, LATENT:])
            scores = jnp.where(seen, scores, EMPTY)
            peak = jnp.max(scores, axis=1, keepdims=True)
            weights = jnp.where(seen, jnp.exp(scores - peak), 0.0)
            total = jnp.sum(weights, axis=1, keepdims=True)
            mixture = dot(weights.astype(BF16), kv_ref[:, :LATENT]) / total
            head = hp * 2 + par
            at = pl.ds(pl.multiple_of(head * VDIM, VDIM), VDIM)
            hv_ref[:, at] = dot(mixture.astype(BF16), uv_ref[par])
            logs = jnp.where(lane == head, peak + jnp.log(total), logs)
    log_ref[...] = logs


def attend_kernel(
    count_ref, x_ref, kv_hbm, out_hbm, queries, scores, weights, out_ref, kv_ref, sems, in_sems
):
    half = x_ref.shape[0]
    slab = kv_ref.shape[2]
    chunk = 256
    arriving = []
    for slot in range(SLOTS):
        arriving.append(pltpu.make_async_copy(kv_hbm.at[slot], kv_ref.at[slot], in_sems.at[slot]))
        arriving[-1].start()
    base = SLOTS * 2 * LATENT
    lane = lax.broadcasted_iota(jnp.int32, (half, 128), 1)
    tile = jnp.zeros((half, 128), F32)
    copies = []
    for slot in range(SLOTS):
        count = count_ref[slot]
        for par in range(2):
            at = slice(par * half, (par + 1) * half)
            first = slot * WIDE + par * LATENT
            queries[at, :LATENT] = x_ref[:, first : first + LATENT]
            first = slot * WIDE + 2 * LATENT + par * ROPE
            queries[at, LATENT:] = x_ref[:, first : first + ROPE]
        peak = jnp.full((2 * half, 1), EMPTY, F32)
        arriving[slot].wait()
        for first in range(0, slab, chunk):
            score = dot(queries[...], kv_ref[slot, :, first : first + chunk])
            position = lax.broadcasted_iota(jnp.int32, score.shape, 1) + first
            score = jnp.where(position < count, score, EMPTY)
            scores[:, first : first + chunk] = score
            peak = jnp.maximum(peak, jnp.max(score, axis=1, keepdims=True))
        reference = jnp.maximum(peak, EMPTY / 10)
        total = jnp.zeros((2 * half, 1), F32)
        for first in range(0, slab, chunk):
            weight = jnp.exp(scores[:, first : first + chunk] - reference)
            total += jnp.sum(weight, axis=1, keepdims=True)
            weights[:, first : first + chunk] = weight.astype(BF16)
        total = jnp.maximum(total, 1.0)
        mixture = dot_t(weights[...], kv_ref[slot, :LATENT, :])
        mixture = (mixture * (1.0 / total)).astype(BF16)
        log = peak + jnp.log(total)
        start = slot * 2 * LATENT
        for par in range(2):
            at = slice(par * half, (par + 1) * half)
            out_ref[:, start + par * LATENT : start + (par + 1) * LATENT] = mixture[at]
            for i, term in enumerate(three_terms(log[at])):
                tile = jnp.where(lane == slot * 6 + par * 3 + i, term, tile)
        end = start + 2 * LATENT
        if slot == SLOTS - 1:
            out_ref[:, base:] = tile.astype(BF16)
            end = PART
        at = pl.ds(start, end - start)
        copies.append(pltpu.make_async_copy(out_ref.at[:, at], out_hbm.at[:, at], sems.at[slot]))
        copies[-1].start()
    for copy in copies:
        copy.wait()


def attend(count, x, kv):
    rows = x.shape[0]
    return pl.pallas_call(
        attend_kernel,
        out_shape=jax.ShapeDtypeStruct((rows, PART), BF16),
        in_specs=[SMEM, VMEM, HBM],
        out_specs=HBM,
        scratch_shapes=[
            pltpu.VMEM((2 * rows, KEY), BF16),
            pltpu.VMEM((2 * rows, kv.shape[2]), F32),
            pltpu.VMEM((2 * rows, kv.shape[2]), BF16),
            pltpu.VMEM((rows, PART), BF16),
            pltpu.VMEM(kv.shape, BF16),
            pltpu.SemaphoreType.DMA((SLOTS,)),
            pltpu.SemaphoreType.DMA((SLOTS,)),
        ],
        compiler_params=pltpu.CompilerParams(vmem_limit_bytes=32 << 20),
    )(count, x, in_hbm(kv))


def merge_kernel(core_ref, y_ref, code_ref, own_ref, mate_ref, out_ref):
    core = core_ref[0]
    rows, cols = out_ref.shape[0], y_ref.shape[0]
    base = SLOTS * 2 * LATENT
    logs = jnp.transpose(y_ref[:, base:].astype(F32))
    row = lax.broadcasted_iota(jnp.int32, (rows, cols), 0)
    tile = jnp.zeros((rows, 128), F32)
    for hp in range(2):
        match = [row == code_ref[hp * 2 + slot : hp * 2 + slot + 1, :] for slot in range(SLOTS)]
        for par in range(2):
            held = []
            for slot in range(SLOTS):
                at = slot * 6 + par * 3
                log = logs[at : at + 1, :] + logs[at + 1 : at + 2, :] + logs[at + 2 : at + 3, :]
                held.append(jnp.where(match[slot], log, EMPTY))
            peak = jnp.max(jnp.maximum(held[0], held[1]), axis=1, keepdims=True)
            total = jnp.zeros((rows, 1), F32)
            mixture = jnp.zeros((rows, LATENT), F32)
            for slot in range(SLOTS):
                weights = jnp.where(match[slot], jnp.exp(held[slot] - peak), 0.0)
                total += jnp.sum(weights, axis=1, keepdims=True)
                first = slot * 2 * LATENT + par * LATENT
                mixture += dot(weights.astype(BF16), y_ref[:, first : first + LATENT])
            total = jnp.maximum(total, 1.0)
            mixture = (mixture / total).astype(BF16)
            head = hp * 2 + par
            values = dot(mixture, jnp.where(core == hp, own_ref[par], mate_ref[par]))
            out_ref[:, head * VDIM : (head + 1) * VDIM] = values.astype(BF16)
            tile = put_terms(tile, peak + jnp.log(total), head * 3)
    out_ref[:, 4 * VDIM :] = tile.astype(BF16)


def finish_kernel(core_ref, z_ref, hv_ref, log_ref, own_hbm, mate_hbm, out_ref, o_ref, sems):
    half = hv_ref.shape[0]
    piece = out_ref.shape[1] // PIECES
    arriving = []
    for i in range(PIECES):
        at = (slice(None), pl.ds(i * piece, piece))
        for side, source in enumerate((own_hbm, mate_hbm)):
            target = o_ref.at[side].at[at]
            arriving.append(pltpu.make_async_copy(source.at[at], target, sems.at[2 * i + side]))
            arriving[-1].start()
    values = []
    for head in range(4):
        logs = [log_ref[:, head : head + 1]]
        parts = [hv_ref[:, head * VDIM : (head + 1) * VDIM]]
        for block in range(z_ref.shape[0] // half):
            at = slice(block * half, (block + 1) * half)
            terms = z_ref[at, 4 * VDIM :].astype(F32)
            first = head * 3
            logs.append(
                terms[:, first : first + 1]
                + terms[:, first + 1 : first + 2]
                + terms[:, first + 2 : first + 3]
            )
            parts.append(z_ref[at, head * VDIM : (head + 1) * VDIM].astype(F32))
        peak = logs[0]
        for log in logs[1:]:
            peak = jnp.maximum(peak, log)
        total = jnp.zeros_like(peak)
        summed = jnp.zeros_like(parts[0])
        for log, part in zip(logs, parts):
            weight = jnp.exp(log - peak)
            total += weight
            summed += weight * part
        values.append(summed / total)
    pairs = [jnp.concatenate(values[hp * 2 : hp * 2 + 2], axis=1) for hp in range(2)]
    own = jnp.where(core_ref[0] == 0, pairs[0], pairs[1]).astype(BF16)
    mate = jnp.where(core_ref[0] == 0, pairs[1], pairs[0]).astype(BF16)
    for i in range(PIECES):
        arriving[2 * i].wait()
        arriving[2 * i + 1].wait()
        at = slice(i * piece, (i + 1) * piece)
        out_ref[:, at] = (dot(own, o_ref[0, :, at]) + dot(mate, o_ref[1, :, at])).astype(BF16)


def total_kernel(tiles_ref, out_ref):
    total = jnp.sum(tiles_ref[...].astype(F32), axis=0)
    width = total.shape[1]
    for i in range(total.shape[0]):
        out_ref[:, i * width : (i + 1) * width] = total[i : i + 1]


def exchange(array, axes, peers):
    blocks = array.reshape(peers, array.shape[0] // peers, *array.shape[1:])
    return lax.all_to_all(blocks, axes, 0, 0, tiled=True).reshape(array.shape)


def shards(
    q_compressed,
    w_q_nope,
    w_q_rope,
    w_uk,
    w_uv,
    w_o,
    kv_cache,
    draft_kv,
    context_length,
    slot_sequence,
    slot_slab,
):
    groups, zs, xs, cores = (lax.axis_size(a) for a in ("group", "z", "x", "core"))
    group, z, x, core = (lax.axis_index(a) for a in ("group", "z", "x", "core"))
    chips = zs * xs
    core_id = core.astype(jnp.int32).reshape(1)
    swap = [(i, 1 - i) for i in range(cores)]

    table = lax.dynamic_index_in_dim(slot_sequence, group, 0, keepdims=False)
    table = table.reshape(chips, cores, SLOTS)
    held = lax.dynamic_index_in_dim(table, core, 1, keepdims=False)
    hp = jnp.arange(2, dtype=jnp.int32)[:, None]
    draft = jnp.arange(DRAFT, dtype=jnp.int32)
    filled = (held >= 0).T[:, :, None]
    shift = (group - (held >> 4)) & (groups - 1)
    code = (shift * TOK_GRP + (held & 15) * DRAFT).T[:, :, None]
    code = code + ((hp != core) * (groups * TOK_GRP) + draft).reshape(-1)
    code = jnp.where(filled, code, -1).reshape(-1, 1)
    row = ((held >> 4) * TOK_GRP + (held & 15) * 2).T[:, :, None, None]
    row = row + (draft & 1) * (TOK_GRP // 2) + (draft >> 1)
    row = jnp.where(filled[..., None], row, -1)
    row = jnp.where(hp == hp.reshape(2, 1, 1, 1, 1), row, -1).reshape(2 * SLOTS, -1)

    chip = z * xs + x
    mine = lax.dynamic_index_in_dim(held, chip, 0, keepdims=False)
    slabs = lax.dynamic_index_in_dim(slot_slab, group, 0, keepdims=False).reshape(chips, cores, SLOTS)
    slabs = lax.dynamic_index_in_dim(slabs, chip, 0, keepdims=False)
    slabs = lax.dynamic_index_in_dim(slabs, core, 0, keepdims=False)
    is_mine = mine[:, None] == jnp.arange(context_length.shape[0], dtype=jnp.int32)
    length = jnp.sum(jnp.where(is_mine, context_length, 0), axis=1)
    count = jnp.where(mine >= 0, length - slabs * kv_cache.shape[3], 0).astype(jnp.int32)

    copies = groups * cores
    narrow = pl.pallas_call(
        project_kernel,
        out_shape=jax.ShapeDtypeStruct((TOK_GRP, NARROW), BF16),
        in_specs=[HBM] * 3,
        out_specs=VMEM,
        scratch_shapes=[
            *(pltpu.VMEM(a.shape, BF16) for a in (q_compressed, w_q_nope, w_q_rope)),
            pltpu.SemaphoreType.DMA((4,)),
        ],
        compiler_params=pltpu.CompilerParams(vmem_limit_bytes=16 << 20),
    )(*(in_hbm(a) for a in (q_compressed, w_q_nope, w_q_rope)))
    late_uk, narrow = lax.optimization_barrier((w_uk, narrow))
    own_q = [narrow]
    for k in range(1, groups):
        own_q.append(lax.ppermute(narrow, "group", [(i, (i + k) % groups) for i in range(groups)]))
    own_q = jnp.concatenate(own_q, axis=0)
    mate_q = lax.ppermute(own_q, "core", swap)
    mate_uk = lax.ppermute(late_uk, "core", swap)
    rows = chips * cores * DRAFT
    wide = pl.pallas_call(
        spread_kernel,
        out_shape=jax.ShapeDtypeStruct((rows, SLOTS * WIDE), BF16),
        grid=(SLOTS,),
        in_specs=[VMEM, VMEM, pl.BlockSpec((rows, 1), lambda k: (k, 0)), VMEM, VMEM],
        out_specs=pl.BlockSpec((rows, WIDE), lambda k: (0, k)),
        scratch_shapes=[pltpu.VMEM((copies * TOK_GRP, 5 * NOPE), BF16)],
        compiler_params=pltpu.CompilerParams(
            dimension_semantics=("arbitrary",), vmem_limit_bytes=16 << 20
        ),
    )(own_q, mate_q, code, w_uk, mate_uk)
    slabs_kv = jnp.swapaxes(kv_cache.reshape(kv_cache.shape[2:]), 1, 2)
    late_o, late_uv, wide = lax.optimization_barrier((w_o, w_uv, wide))
    mate_uv = lax.ppermute(late_uv, "core", swap)
    mate_o = lax.ppermute(late_o, "core", swap)
    arrived = exchange(wide, ("z", "x"), chips)
    draft_hv, draft_log = call(
        draft_kernel,
        (
            jax.ShapeDtypeStruct((TOK_GRP // 2, 4 * VDIM), F32),
            jax.ShapeDtypeStruct((TOK_GRP // 2, 128), F32),
        ),
        (core_id, own_q, mate_q, w_uk, mate_uk, w_uv, mate_uv, draft_kv),
        [SMEM] + [VMEM] * 7,
    )
    partials = attend(count, arrived, slabs_kv)
    back = exchange(partials, ("z", "x"), chips)
    merged = call(
        merge_kernel,
        jax.ShapeDtypeStruct((groups * TOK_GRP, 4 * VDIM + 128), BF16),
        (core_id, back, row, w_uv, mate_uv),
        [SMEM] + [VMEM] * 4,
    )
    home = exchange(merged, ("group", "core"), copies)
    sums = call(
        finish_kernel,
        jax.ShapeDtypeStruct((chips, w_o.shape[1]), BF16),
        (core_id, home, draft_hv, draft_log, in_hbm(w_o), in_hbm(mate_o)),
        [SMEM, VMEM, VMEM, VMEM, HBM, HBM],
        [pltpu.VMEM((2, *w_o.shape), BF16), pltpu.SemaphoreType.DMA((2 * PIECES,))],
    )
    tiles = lax.all_to_all(sums.reshape(chips, 8, -1), ("z", "x"), 0, 0, tiled=True)
    return call(
        total_kernel, jax.ShapeDtypeStruct((1, w_o.shape[1]), F32), (tiles,), [VMEM]
    )


def solution(mesh):
    fine = Mesh(mesh.devices.reshape(4, 8, 4, 2), ("group", "z", "x", "core"))
    dev = ("z", "x", "core")
    placed = (
        P("group", None),
        P(None, dev),
        P(None, dev),
        P(dev, None, None),
        P(dev, None, None),
        P(dev, None),
        P("group", dev, None, None, None),
        P("group", None),
        P(),
        P(),
        P(),
    )
    return jax.shard_map(
        shards, mesh=fine, in_specs=placed, out_specs=P(("group", *dev), None), check_vma=False
    )
```

```python
import jax
import jax.numpy as jnp
from jax import lax
from jax.experimental import pallas as pl
from jax.experimental.pallas import tpu as pltpu
from jax.sharding import Mesh
from jax.sharding import PartitionSpec as P

NOPE = 128
ROPE = 64
LATENT = 512
VDIM = 128
DRAFT = 4
SEQ_GRP = 16
TOK_GRP = SEQ_GRP * DRAFT
SLOTS = 2
KEY = LATENT + ROPE
WIDE = 2 * LATENT + 2 * ROPE
PART = SLOTS * 2 * LATENT + 128
NARROW = 2 * NOPE + 2 * ROPE
EMPTY = -1e30
SCALE = (NOPE + ROPE) ** -0.5
F32 = jnp.float32
BF16 = jnp.bfloat16
CONTRACT_LAST = (((1,), (1,)), ((), ()))

VMEM = pl.BlockSpec(memory_space=pltpu.VMEM)
SMEM = pl.BlockSpec(memory_space=pltpu.SMEM)
HBM = pl.BlockSpec(memory_space=pltpu.HBM)


def in_hbm(array):
    return pltpu.with_memory_space_constraint(array, pltpu.HBM)


def dot(a, b):
    return jnp.dot(a, b, preferred_element_type=F32)


def dot_t(a, b):
    return lax.dot_general(a, b, CONTRACT_LAST, preferred_element_type=F32)


def call(kernel, outs, args, specs, scratch=(), vmem=32, cost=None):
    return pl.pallas_call(
        kernel,
        out_shape=outs,
        in_specs=specs,
        out_specs=jax.tree.map(lambda _: VMEM, outs),
        scratch_shapes=list(scratch),
        compiler_params=pltpu.CompilerParams(vmem_limit_bytes=vmem << 20),
        cost_estimate=cost,
    )(*args)


def three_terms(value):
    high = value.astype(BF16).astype(F32)
    middle = (value - high).astype(BF16).astype(F32)
    return high, middle, (value - high - middle).astype(BF16).astype(F32)


def put_terms(tile, value, first):
    lane = lax.broadcasted_iota(jnp.int32, tile.shape, 1)
    for i, term in enumerate(three_terms(value)):
        tile = jnp.where(lane == first + i, term, tile)
    return tile


def project_kernel(q_hbm, wn_hbm, wr_hbm, out_ref, q_ref, wn_ref, wr_ref, sems):
    copies = []
    depth = wn_ref.shape[0] // 2
    for i, (source, target) in enumerate(((q_hbm, q_ref), (wr_hbm, wr_ref))):
        copies.append(pltpu.make_async_copy(source, target, sems.at[i]))
    for i in range(2):
        at = pl.ds(i * depth, depth)
        copies.append(pltpu.make_async_copy(wn_hbm.at[at], wn_ref.at[at], sems.at[2 + i]))
    for copy in copies:
        copy.start()
    copies[0].wait()
    copies[1].wait()
    out_ref[:, 2 * NOPE :] = (dot(q_ref[...], wr_ref[...]) * SCALE).astype(BF16)
    copies[2].wait()
    copies[3].wait()
    out_ref[:, : 2 * NOPE] = dot(q_ref[...], wn_ref[...]).astype(BF16)


def spread_kernel(own_q, mate_q, code_ref, own_ref, mate_ref, out_ref, rows):
    @pl.when(pl.program_id(0) == 0)
    def _():
        rows[...] = jnp.zeros_like(rows)
        count = own_q.shape[0]
        for rel, q_ref in enumerate((own_q, mate_q)):
            at = slice(rel * count, (rel + 1) * count)
            for par in range(2):
                first = par * 2 * NOPE + rel * NOPE
                rows[at, first : first + NOPE] = q_ref[:, par * NOPE : (par + 1) * NOPE]
            rows[at, 4 * NOPE :] = q_ref[:, 2 * NOPE :]

    column = lax.broadcasted_iota(jnp.int32, (code_ref.shape[0], rows.shape[0]), 1)
    pick = jnp.where(column == code_ref[...], 1.0, 0.0).astype(BF16)
    picked = dot(pick, rows[...]).astype(BF16)
    for par in range(2):
        weight = jnp.concatenate([own_ref[par], mate_ref[par]], axis=0)
        absorbed = dot(picked[:, par * 2 * NOPE : (par + 1) * 2 * NOPE], weight) * SCALE
        out_ref[:, par * LATENT : (par + 1) * LATENT] = absorbed.astype(BF16)
    out_ref[:, 2 * LATENT :] = picked[:, 4 * NOPE :]


def draft_kernel(
    core_ref, own_q, mate_q, own_uk, mate_uk, own_uv, mate_uv, kv_ref, hv_ref, log_ref
):
    core = core_ref[0]
    half = hv_ref.shape[0]
    row = 2 * lax.broadcasted_iota(jnp.int32, (half, TOK_GRP), 0) + core
    col = lax.broadcasted_iota(jnp.int32, (half, TOK_GRP), 1)
    seen = (row // DRAFT == col // DRAFT) & (col <= row)
    pick = jnp.where(row == col, 1.0, 0.0).astype(BF16)
    lane = lax.broadcasted_iota(jnp.int32, log_ref.shape, 1)
    logs = jnp.zeros(log_ref.shape, F32)
    sides = ((core, own_q, own_uk, own_uv), (1 - core, mate_q, mate_uk, mate_uv))
    for hp, q_ref, uk_ref, uv_ref in sides:
        rows = dot(pick, q_ref[:TOK_GRP, :]).astype(BF16)
        for par in range(2):
            narrow = rows[:, par * NOPE : (par + 1) * NOPE]
            absorbed = (dot(narrow, uk_ref[par]) * SCALE).astype(BF16)
            first = 2 * NOPE + par * ROPE
            scores = dot_t(absorbed, kv_ref[:, :LATENT])
            scores += dot_t(rows[:, first : first + ROPE], kv_ref[:, LATENT:])
            scores = jnp.where(seen, scores, EMPTY)
            peak = jnp.max(scores, axis=1, keepdims=True)
            weights = jnp.where(seen, jnp.exp(scores - peak), 0.0)
            total = jnp.sum(weights, axis=1, keepdims=True)
            mixture = dot(weights.astype(BF16), kv_ref[:, :LATENT]) / total
            head = hp * 2 + par
            at = pl.ds(pl.multiple_of(head * VDIM, VDIM), VDIM)
            hv_ref[:, at] = dot(mixture.astype(BF16), uv_ref[par])
            logs = jnp.where(lane == head, peak + jnp.log(total), logs)
    log_ref[...] = logs


def attend_kernel(
    count_ref, x_ref, kv_ref, out_hbm, queries, scores, weights, out_ref, sems
):
    half = x_ref.shape[0]
    slab = kv_ref.shape[2]
    chunk = 256
    base = SLOTS * 2 * LATENT
    lane = lax.broadcasted_iota(jnp.int32, (half, 128), 1)
    tile = jnp.zeros((half, 128), F32)
    copies = []
    for slot in range(SLOTS):
        count = count_ref[slot]
        for par in range(2):
            at = slice(par * half, (par + 1) * half)
            first = slot * WIDE + par * LATENT
            queries[at, :LATENT] = x_ref[:, first : first + LATENT]
            first = slot * WIDE + 2 * LATENT + par * ROPE
            queries[at, LATENT:] = x_ref[:, first : first + ROPE]
        peak = jnp.full((2 * half, 1), EMPTY, F32)
        for first in range(0, slab, chunk):
            score = dot(queries[...], kv_ref[slot, :, first : first + chunk])
            position = lax.broadcasted_iota(jnp.int32, score.shape, 1) + first
            score = jnp.where(position < count, score, EMPTY)
            scores[:, first : first + chunk] = score
            peak = jnp.maximum(peak, jnp.max(score, axis=1, keepdims=True))
        reference = jnp.maximum(peak, EMPTY / 10)
        total = jnp.zeros((2 * half, 1), F32)
        for first in range(0, slab, chunk):
            weight = jnp.exp(scores[:, first : first + chunk] - reference)
            total += jnp.sum(weight, axis=1, keepdims=True)
            weights[:, first : first + chunk] = weight.astype(BF16)
        total = jnp.maximum(total, 1.0)
        mixture = dot_t(weights[...], kv_ref[slot, :LATENT, :])
        mixture = (mixture * (1.0 / total)).astype(BF16)
        log = peak + jnp.log(total)
        start = slot * 2 * LATENT
        for par in range(2):
            at = slice(par * half, (par + 1) * half)
            out_ref[:, start + par * LATENT : start + (par + 1) * LATENT] = mixture[at]
            for i, term in enumerate(three_terms(log[at])):
                tile = jnp.where(lane == slot * 6 + par * 3 + i, term, tile)
        end = start + 2 * LATENT
        if slot == SLOTS - 1:
            out_ref[:, base:] = tile.astype(BF16)
            end = PART
        at = pl.ds(start, end - start)
        copies.append(pltpu.make_async_copy(out_ref.at[:, at], out_hbm.at[:, at], sems.at[slot]))
        copies[-1].start()
    for copy in copies:
        copy.wait()


def attend(count, x, kv):
    rows = x.shape[0]
    return pl.pallas_call(
        attend_kernel,
        out_shape=jax.ShapeDtypeStruct((rows, PART), BF16),
        in_specs=[SMEM, VMEM, VMEM],
        out_specs=HBM,
        scratch_shapes=[
            pltpu.VMEM((2 * rows, KEY), BF16),
            pltpu.VMEM((2 * rows, kv.shape[2]), F32),
            pltpu.VMEM((2 * rows, kv.shape[2]), BF16),
            pltpu.VMEM((rows, PART), BF16),
            pltpu.SemaphoreType.DMA((SLOTS,)),
        ],
        compiler_params=pltpu.CompilerParams(vmem_limit_bytes=32 << 20),
    )(count, x, kv)


def merge_kernel(core_ref, y_ref, code_ref, own_ref, mate_ref, out_ref):
    core = core_ref[0]
    rows, cols = out_ref.shape[0], y_ref.shape[0]
    base = SLOTS * 2 * LATENT
    logs = jnp.transpose(y_ref[:, base:].astype(F32))
    row = lax.broadcasted_iota(jnp.int32, (rows, cols), 0)
    tile = jnp.zeros((rows, 128), F32)
    for hp in range(2):
        match = [row == code_ref[hp * 2 + slot : hp * 2 + slot + 1, :] for slot in range(SLOTS)]
        for par in range(2):
            held = []
            for slot in range(SLOTS):
                at = slot * 6 + par * 3
                log = logs[at : at + 1, :] + logs[at + 1 : at + 2, :] + logs[at + 2 : at + 3, :]
                held.append(jnp.where(match[slot], log, EMPTY))
            peak = jnp.max(jnp.maximum(held[0], held[1]), axis=1, keepdims=True)
            total = jnp.zeros((rows, 1), F32)
            mixture = jnp.zeros((rows, LATENT), F32)
            for slot in range(SLOTS):
                weights = jnp.where(match[slot], jnp.exp(held[slot] - peak), 0.0)
                total += jnp.sum(weights, axis=1, keepdims=True)
                first = slot * 2 * LATENT + par * LATENT
                mixture += dot(weights.astype(BF16), y_ref[:, first : first + LATENT])
            total = jnp.maximum(total, 1.0)
            mixture = (mixture / total).astype(BF16)
            head = hp * 2 + par
            values = dot(mixture, jnp.where(core == hp, own_ref[par], mate_ref[par]))
            out_ref[:, head * VDIM : (head + 1) * VDIM] = values.astype(BF16)
            tile = put_terms(tile, peak + jnp.log(total), head * 3)
    out_ref[:, 4 * VDIM :] = tile.astype(BF16)


def finish_kernel(core_ref, z_ref, hv_ref, log_ref, o_ref, out_ref):
    half = hv_ref.shape[0]
    values = []
    for head in range(4):
        logs = [log_ref[:, head : head + 1]]
        parts = [hv_ref[:, head * VDIM : (head + 1) * VDIM]]
        for block in range(z_ref.shape[0] // half):
            at = slice(block * half, (block + 1) * half)
            terms = z_ref[at, 4 * VDIM :].astype(F32)
            first = head * 3
            logs.append(
                terms[:, first : first + 1]
                + terms[:, first + 1 : first + 2]
                + terms[:, first + 2 : first + 3]
            )
            parts.append(z_ref[at, head * VDIM : (head + 1) * VDIM].astype(F32))
        peak = logs[0]
        for log in logs[1:]:
            peak = jnp.maximum(peak, log)
        total = jnp.zeros_like(peak)
        summed = jnp.zeros_like(parts[0])
        for log, part in zip(logs, parts):
            weight = jnp.exp(log - peak)
            total += weight
            summed += weight * part
        values.append(summed / total)
    pairs = [jnp.concatenate(values[hp * 2 : hp * 2 + 2], axis=1) for hp in range(2)]
    own = jnp.where(core_ref[0] == 0, pairs[0], pairs[1])
    mate = jnp.where(core_ref[0] == 0, pairs[1], pairs[0])
    head_values = jnp.concatenate([own, mate], axis=1).astype(BF16)
    out_ref[...] = dot(head_values, o_ref[...]).astype(BF16)


def total_kernel(tiles_ref, out_ref):
    total = jnp.sum(tiles_ref[...].astype(F32), axis=0)
    width = total.shape[1]
    for i in range(total.shape[0]):
        out_ref[:, i * width : (i + 1) * width] = total[i : i + 1]


def exchange(array, axes, peers):
    blocks = array.reshape(peers, array.shape[0] // peers, *array.shape[1:])
    return lax.all_to_all(blocks, axes, 0, 0, tiled=True).reshape(array.shape)


def shards(
    q_compressed,
    w_q_nope,
    w_q_rope,
    w_uk,
    w_uv,
    w_o,
    kv_cache,
    draft_kv,
    context_length,
    slot_sequence,
    slot_slab,
):
    groups, zs, xs, cores = (lax.axis_size(a) for a in ("group", "z", "x", "core"))
    group, z, x, core = (lax.axis_index(a) for a in ("group", "z", "x", "core"))
    chips = zs * xs
    core_id = core.astype(jnp.int32).reshape(1)
    swap = [(i, 1 - i) for i in range(cores)]

    table = lax.dynamic_index_in_dim(slot_sequence, group, 0, keepdims=False)
    table = table.reshape(chips, cores, SLOTS)
    held = lax.dynamic_index_in_dim(table, core, 1, keepdims=False)
    hp = jnp.arange(2, dtype=jnp.int32)[:, None]
    draft = jnp.arange(DRAFT, dtype=jnp.int32)
    filled = (held >= 0).T[:, :, None]
    shift = (group - (held >> 4)) & (groups - 1)
    code = (shift * TOK_GRP + (held & 15) * DRAFT).T[:, :, None]
    code = code + ((hp != core) * (groups * TOK_GRP) + draft).reshape(-1)
    code = jnp.where(filled, code, -1).reshape(-1, 1)
    row = ((held >> 4) * TOK_GRP + (held & 15) * 2).T[:, :, None, None]
    row = row + (draft & 1) * (TOK_GRP // 2) + (draft >> 1)
    row = jnp.where(filled[..., None], row, -1)
    row = jnp.where(hp == hp.reshape(2, 1, 1, 1, 1), row, -1).reshape(2 * SLOTS, -1)

    chip = z * xs + x
    mine = lax.dynamic_index_in_dim(held, chip, 0, keepdims=False)
    slabs = lax.dynamic_index_in_dim(slot_slab, group, 0, keepdims=False).reshape(chips, cores, SLOTS)
    slabs = lax.dynamic_index_in_dim(slabs, chip, 0, keepdims=False)
    slabs = lax.dynamic_index_in_dim(slabs, core, 0, keepdims=False)
    is_mine = mine[:, None] == jnp.arange(context_length.shape[0], dtype=jnp.int32)
    length = jnp.sum(jnp.where(is_mine, context_length, 0), axis=1)
    count = jnp.where(mine >= 0, length - slabs * kv_cache.shape[3], 0).astype(jnp.int32)

    copies = groups * cores
    narrow = pl.pallas_call(
        project_kernel,
        out_shape=jax.ShapeDtypeStruct((TOK_GRP, NARROW), BF16),
        in_specs=[HBM] * 3,
        out_specs=VMEM,
        scratch_shapes=[
            *(pltpu.VMEM(a.shape, BF16) for a in (q_compressed, w_q_nope, w_q_rope)),
            pltpu.SemaphoreType.DMA((4,)),
        ],
        compiler_params=pltpu.CompilerParams(vmem_limit_bytes=16 << 20),
    )(*(in_hbm(a) for a in (q_compressed, w_q_nope, w_q_rope)))
    late_uk, narrow = lax.optimization_barrier((w_uk, narrow))
    own_q = [narrow]
    for k in range(1, groups):
        own_q.append(lax.ppermute(narrow, "group", [(i, (i + k) % groups) for i in range(groups)]))
    own_q = jnp.concatenate(own_q, axis=0)
    mate_q = lax.ppermute(own_q, "core", swap)
    mate_uk = lax.ppermute(late_uk, "core", swap)
    rows = chips * cores * DRAFT
    wide = pl.pallas_call(
        spread_kernel,
        out_shape=jax.ShapeDtypeStruct((rows, SLOTS * WIDE), BF16),
        grid=(SLOTS,),
        in_specs=[VMEM, VMEM, pl.BlockSpec((rows, 1), lambda k: (k, 0)), VMEM, VMEM],
        out_specs=pl.BlockSpec((rows, WIDE), lambda k: (0, k)),
        scratch_shapes=[pltpu.VMEM((copies * TOK_GRP, 5 * NOPE), BF16)],
        compiler_params=pltpu.CompilerParams(
            dimension_semantics=("arbitrary",), vmem_limit_bytes=16 << 20
        ),
        cost_estimate=pl.CostEstimate(flops=30 << 30, transcendentals=0, bytes_accessed=80 << 20),
    )(own_q, mate_q, code, w_uk, mate_uk)
    slabs_kv = jnp.swapaxes(kv_cache.reshape(kv_cache.shape[2:]), 1, 2)
    late_uv, wide = lax.optimization_barrier((w_uv, wide))
    late_o, count = lax.optimization_barrier((w_o, count))
    mate_uv = lax.ppermute(late_uv, "core", swap)
    mate_o = lax.ppermute(late_o, "core", swap)
    arrived = exchange(wide, ("z", "x"), chips)
    draft_hv, draft_log = call(
        draft_kernel,
        (
            jax.ShapeDtypeStruct((TOK_GRP // 2, 4 * VDIM), F32),
            jax.ShapeDtypeStruct((TOK_GRP // 2, 128), F32),
        ),
        (core_id, own_q, mate_q, w_uk, mate_uk, w_uv, mate_uv, draft_kv),
        [SMEM] + [VMEM] * 7,
    )
    partials = attend(count, arrived, slabs_kv)
    back = exchange(partials, ("z", "x"), chips)
    both_o = jnp.concatenate([w_o, mate_o], axis=0)
    back, draft_hv, draft_log, both_o = lax.optimization_barrier((back, draft_hv, draft_log, both_o))
    merged = call(
        merge_kernel,
        jax.ShapeDtypeStruct((groups * TOK_GRP, 4 * VDIM + 128), BF16),
        (core_id, back, row, w_uv, mate_uv),
        [SMEM] + [VMEM] * 4,
        vmem=16,
        cost=pl.CostEstimate(flops=3 << 30, transcendentals=1 << 19, bytes_accessed=8 << 20),
    )
    home = exchange(merged, ("group", "core"), copies)
    sums = call(
        finish_kernel,
        jax.ShapeDtypeStruct((chips, w_o.shape[1]), BF16),
        (core_id, home, draft_hv, draft_log, both_o),
        [SMEM] + [VMEM] * 4,
    )
    tiles = lax.all_to_all(sums.reshape(chips, 8, -1), ("z", "x"), 0, 0, tiled=True)
    return call(
        total_kernel, jax.ShapeDtypeStruct((1, w_o.shape[1]), F32), (tiles,), [VMEM]
    )


def solution(mesh):
    fine = Mesh(mesh.devices.reshape(4, 8, 4, 2), ("group", "z", "x", "core"))
    dev = ("z", "x", "core")
    placed = (
        P("group", None),
        P(None, dev),
        P(None, dev),
        P(dev, None, None),
        P(dev, None, None),
        P(dev, None),
        P("group", dev, None, None, None),
        P("group", None),
        P(),
        P(),
        P(),
    )
    return jax.shard_map(
        shards, mesh=fine, in_specs=placed, out_specs=P(("group", *dev), None), check_vma=False
    )
```

```python
import jax
import jax.numpy as jnp
from jax import lax
from jax.experimental import pallas as pl
from jax.experimental.pallas import tpu as pltpu
from jax.sharding import Mesh
from jax.sharding import PartitionSpec as P

NOPE = 128
ROPE = 64
LATENT = 512
VDIM = 128
DRAFT = 4
SEQ_GRP = 16
TOK_GRP = SEQ_GRP * DRAFT
SLOTS = 2
KEY = LATENT + ROPE
WIDE = 2 * LATENT + 2 * ROPE
PART = SLOTS * 2 * LATENT + 128
NARROW = 2 * NOPE + 2 * ROPE
EMPTY = -1e30
SCALE = (NOPE + ROPE) ** -0.5
F32 = jnp.float32
BF16 = jnp.bfloat16
CONTRACT_LAST = (((1,), (1,)), ((), ()))

VMEM = pl.BlockSpec(memory_space=pltpu.VMEM)
SMEM = pl.BlockSpec(memory_space=pltpu.SMEM)
HBM = pl.BlockSpec(memory_space=pltpu.HBM)


def in_hbm(array):
    return pltpu.with_memory_space_constraint(array, pltpu.HBM)


def dot(a, b):
    return jnp.dot(a, b, preferred_element_type=F32)


def dot_t(a, b):
    return lax.dot_general(a, b, CONTRACT_LAST, preferred_element_type=F32)


def call(kernel, outs, args, specs, scratch=(), vmem=32, cost=None):
    return pl.pallas_call(
        kernel,
        out_shape=outs,
        in_specs=specs,
        out_specs=jax.tree.map(lambda _: VMEM, outs),
        scratch_shapes=list(scratch),
        compiler_params=pltpu.CompilerParams(vmem_limit_bytes=vmem << 20),
        cost_estimate=cost,
    )(*args)


def three_terms(value):
    high = value.astype(BF16).astype(F32)
    middle = (value - high).astype(BF16).astype(F32)
    return high, middle, (value - high - middle).astype(BF16).astype(F32)


def put_terms(tile, value, first):
    lane = lax.broadcasted_iota(jnp.int32, tile.shape, 1)
    for i, term in enumerate(three_terms(value)):
        tile = jnp.where(lane == first + i, term, tile)
    return tile


def project_kernel(q_hbm, wn_hbm, wr_hbm, out_ref, q_ref, wn_ref, wr_ref, sems):
    copies = []
    depth = wn_ref.shape[0] // 2
    for i, (source, target) in enumerate(((q_hbm, q_ref), (wr_hbm, wr_ref))):
        copies.append(pltpu.make_async_copy(source, target, sems.at[i]))
    for i in range(2):
        at = pl.ds(i * depth, depth)
        copies.append(pltpu.make_async_copy(wn_hbm.at[at], wn_ref.at[at], sems.at[2 + i]))
    for copy in copies:
        copy.start()
    copies[0].wait()
    copies[1].wait()
    out_ref[:, 2 * NOPE :] = (dot(q_ref[...], wr_ref[...]) * SCALE).astype(BF16)
    copies[2].wait()
    copies[3].wait()
    out_ref[:, : 2 * NOPE] = dot(q_ref[...], wn_ref[...]).astype(BF16)


def spread_kernel(own_q, mate_q, code_ref, own_ref, mate_ref, out_ref, rows):
    @pl.when(pl.program_id(0) == 0)
    def _():
        rows[...] = jnp.zeros_like(rows)
        count = own_q.shape[0]
        for rel, q_ref in enumerate((own_q, mate_q)):
            at = slice(rel * count, (rel + 1) * count)
            for par in range(2):
                first = par * 2 * NOPE + rel * NOPE
                rows[at, first : first + NOPE] = q_ref[:, par * NOPE : (par + 1) * NOPE]
            rows[at, 4 * NOPE :] = q_ref[:, 2 * NOPE :]

    column = lax.broadcasted_iota(jnp.int32, (code_ref.shape[0], rows.shape[0]), 1)
    pick = jnp.where(column == code_ref[...], 1.0, 0.0).astype(BF16)
    picked = dot(pick, rows[...]).astype(BF16)
    for par in range(2):
        weight = jnp.concatenate([own_ref[par], mate_ref[par]], axis=0)
        absorbed = dot(picked[:, par * 2 * NOPE : (par + 1) * 2 * NOPE], weight) * SCALE
        out_ref[:, par * LATENT : (par + 1) * LATENT] = absorbed.astype(BF16)
    out_ref[:, 2 * LATENT :] = picked[:, 4 * NOPE :]


def draft_kernel(
    core_ref, own_q, mate_q, own_uk, mate_uk, own_uv, mate_uv, kv_ref, hv_ref, log_ref
):
    core = core_ref[0]
    half = hv_ref.shape[0]
    row = 2 * lax.broadcasted_iota(jnp.int32, (half, TOK_GRP), 0) + core
    col = lax.broadcasted_iota(jnp.int32, (half, TOK_GRP), 1)
    seen = (row // DRAFT == col // DRAFT) & (col <= row)
    pick = jnp.where(row == col, 1.0, 0.0).astype(BF16)
    lane = lax.broadcasted_iota(jnp.int32, log_ref.shape, 1)
    logs = jnp.zeros(log_ref.shape, F32)
    sides = ((core, own_q, own_uk, own_uv), (1 - core, mate_q, mate_uk, mate_uv))
    for hp, q_ref, uk_ref, uv_ref in sides:
        rows = dot(pick, q_ref[:TOK_GRP, :]).astype(BF16)
        for par in range(2):
            narrow = rows[:, par * NOPE : (par + 1) * NOPE]
            absorbed = (dot(narrow, uk_ref[par]) * SCALE).astype(BF16)
            first = 2 * NOPE + par * ROPE
            scores = dot_t(absorbed, kv_ref[:, :LATENT])
            scores += dot_t(rows[:, first : first + ROPE], kv_ref[:, LATENT:])
            scores = jnp.where(seen, scores, EMPTY)
            peak = jnp.max(scores, axis=1, keepdims=True)
            weights = jnp.where(seen, jnp.exp(scores - peak), 0.0)
            total = jnp.sum(weights, axis=1, keepdims=True)
            mixture = dot(weights.astype(BF16), kv_ref[:, :LATENT]) / total
            head = hp * 2 + par
            at = pl.ds(pl.multiple_of(head * VDIM, VDIM), VDIM)
            hv_ref[:, at] = dot(mixture.astype(BF16), uv_ref[par])
            logs = jnp.where(lane == head, peak + jnp.log(total), logs)
    log_ref[...] = logs


def attend_kernel(
    count_ref, x_ref, kv_ref, out_hbm, queries, scores, weights, out_ref, sems
):
    half = x_ref.shape[0]
    slab = kv_ref.shape[2]
    chunk = 256
    base = SLOTS * 2 * LATENT
    lane = lax.broadcasted_iota(jnp.int32, (half, 128), 1)
    tile = jnp.zeros((half, 128), F32)
    copies = []
    for slot in range(SLOTS):
        count = count_ref[slot]
        for par in range(2):
            at = slice(par * half, (par + 1) * half)
            first = slot * WIDE + par * LATENT
            queries[at, :LATENT] = x_ref[:, first : first + LATENT]
            first = slot * WIDE + 2 * LATENT + par * ROPE
            queries[at, LATENT:] = x_ref[:, first : first + ROPE]
        peak = jnp.full((2 * half, 1), EMPTY, F32)
        for first in range(0, slab, chunk):
            score = dot(queries[...], kv_ref[slot, :, first : first + chunk])
            position = lax.broadcasted_iota(jnp.int32, score.shape, 1) + first
            score = jnp.where(position < count, score, EMPTY)
            scores[:, first : first + chunk] = score
            peak = jnp.maximum(peak, jnp.max(score, axis=1, keepdims=True))
        reference = jnp.maximum(peak, EMPTY / 10)
        total = jnp.zeros((2 * half, 1), F32)
        for first in range(0, slab, chunk):
            weight = jnp.exp(scores[:, first : first + chunk] - reference)
            total += jnp.sum(weight, axis=1, keepdims=True)
            weights[:, first : first + chunk] = weight.astype(BF16)
        total = jnp.maximum(total, 1.0)
        mixture = dot_t(weights[...], kv_ref[slot, :LATENT, :])
        mixture = (mixture * (1.0 / total)).astype(BF16)
        log = peak + jnp.log(total)
        start = slot * 2 * LATENT
        for par in range(2):
            at = slice(par * half, (par + 1) * half)
            out_ref[:, start + par * LATENT : start + (par + 1) * LATENT] = mixture[at]
            for i, term in enumerate(three_terms(log[at])):
                tile = jnp.where(lane == slot * 6 + par * 3 + i, term, tile)
        end = start + 2 * LATENT
        if slot == SLOTS - 1:
            out_ref[:, base:] = tile.astype(BF16)
            end = PART
        at = pl.ds(start, end - start)
        copies.append(pltpu.make_async_copy(out_ref.at[:, at], out_hbm.at[:, at], sems.at[slot]))
        copies[-1].start()
    for copy in copies:
        copy.wait()


def attend(count, x, kv):
    rows = x.shape[0]
    return pl.pallas_call(
        attend_kernel,
        out_shape=jax.ShapeDtypeStruct((rows, PART), BF16),
        in_specs=[SMEM, VMEM, VMEM],
        out_specs=HBM,
        scratch_shapes=[
            pltpu.VMEM((2 * rows, KEY), BF16),
            pltpu.VMEM((2 * rows, kv.shape[2]), F32),
            pltpu.VMEM((2 * rows, kv.shape[2]), BF16),
            pltpu.VMEM((rows, PART), BF16),
            pltpu.SemaphoreType.DMA((SLOTS,)),
        ],
        compiler_params=pltpu.CompilerParams(vmem_limit_bytes=32 << 20),
    )(count, x, kv)


def merge_kernel(core_ref, y_ref, code_ref, own_ref, mate_ref, out_ref):
    core = core_ref[0]
    rows, cols = out_ref.shape[0], y_ref.shape[0]
    base = SLOTS * 2 * LATENT
    logs = jnp.transpose(y_ref[:, base:].astype(F32))
    row = lax.broadcasted_iota(jnp.int32, (rows, cols), 0)
    tile = jnp.zeros((rows, 128), F32)
    for hp in range(2):
        match = [row == code_ref[hp * 2 + slot : hp * 2 + slot + 1, :] for slot in range(SLOTS)]
        for par in range(2):
            held = []
            for slot in range(SLOTS):
                at = slot * 6 + par * 3
                log = logs[at : at + 1, :] + logs[at + 1 : at + 2, :] + logs[at + 2 : at + 3, :]
                held.append(jnp.where(match[slot], log, EMPTY))
            peak = jnp.max(jnp.maximum(held[0], held[1]), axis=1, keepdims=True)
            total = jnp.zeros((rows, 1), F32)
            mixture = jnp.zeros((rows, LATENT), F32)
            for slot in range(SLOTS):
                weights = jnp.where(match[slot], jnp.exp(held[slot] - peak), 0.0)
                total += jnp.sum(weights, axis=1, keepdims=True)
                first = slot * 2 * LATENT + par * LATENT
                mixture += dot(weights.astype(BF16), y_ref[:, first : first + LATENT])
            total = jnp.maximum(total, 1.0)
            mixture = (mixture / total).astype(BF16)
            head = hp * 2 + par
            values = dot(mixture, jnp.where(core == hp, own_ref[par], mate_ref[par]))
            out_ref[:, head * VDIM : (head + 1) * VDIM] = values.astype(BF16)
            tile = put_terms(tile, peak + jnp.log(total), head * 3)
    out_ref[:, 4 * VDIM :] = tile.astype(BF16)


def finish_kernel(core_ref, z_ref, hv_ref, log_ref, o_ref, out_ref):
    half = hv_ref.shape[0]
    values = []
    for head in range(4):
        logs = [log_ref[:, head : head + 1]]
        parts = [hv_ref[:, head * VDIM : (head + 1) * VDIM]]
        for block in range(z_ref.shape[0] // half):
            at = slice(block * half, (block + 1) * half)
            terms = z_ref[at, 4 * VDIM :].astype(F32)
            first = head * 3
            logs.append(
                terms[:, first : first + 1]
                + terms[:, first + 1 : first + 2]
                + terms[:, first + 2 : first + 3]
            )
            parts.append(z_ref[at, head * VDIM : (head + 1) * VDIM].astype(F32))
        peak = logs[0]
        for log in logs[1:]:
            peak = jnp.maximum(peak, log)
        total = jnp.zeros_like(peak)
        summed = jnp.zeros_like(parts[0])
        for log, part in zip(logs, parts):
            weight = jnp.exp(log - peak)
            total += weight
            summed += weight * part
        values.append(summed / total)
    pairs = [jnp.concatenate(values[hp * 2 : hp * 2 + 2], axis=1) for hp in range(2)]
    own = jnp.where(core_ref[0] == 0, pairs[0], pairs[1])
    mate = jnp.where(core_ref[0] == 0, pairs[1], pairs[0])
    head_values = jnp.concatenate([own, mate], axis=1).astype(BF16)
    out_ref[...] = dot(head_values, o_ref[...]).astype(BF16)


def total_kernel(tiles_ref, out_ref):
    total = jnp.sum(tiles_ref[...].astype(F32), axis=0)
    width = total.shape[1]
    for i in range(total.shape[0]):
        out_ref[:, i * width : (i + 1) * width] = total[i : i + 1]


def exchange(array, axes, peers):
    blocks = array.reshape(peers, array.shape[0] // peers, *array.shape[1:])
    return lax.all_to_all(blocks, axes, 0, 0, tiled=True).reshape(array.shape)


def shards(
    q_compressed,
    w_q_nope,
    w_q_rope,
    w_uk,
    w_uv,
    w_o,
    kv_cache,
    draft_kv,
    context_length,
    slot_sequence,
    slot_slab,
):
    groups, zs, xs, cores = (lax.axis_size(a) for a in ("group", "z", "x", "core"))
    group, z, x, core = (lax.axis_index(a) for a in ("group", "z", "x", "core"))
    chips = zs * xs
    core_id = core.astype(jnp.int32).reshape(1)
    swap = [(i, 1 - i) for i in range(cores)]

    table = lax.dynamic_index_in_dim(slot_sequence, group, 0, keepdims=False)
    table = table.reshape(chips, cores, SLOTS)
    held = lax.dynamic_index_in_dim(table, core, 1, keepdims=False)
    hp = jnp.arange(2, dtype=jnp.int32)[:, None]
    draft = jnp.arange(DRAFT, dtype=jnp.int32)
    filled = (held >= 0).T[:, :, None]
    shift = (group - (held >> 4)) & (groups - 1)
    code = (shift * TOK_GRP + (held & 15) * DRAFT).T[:, :, None]
    code = code + ((hp != core) * (groups * TOK_GRP) + draft).reshape(-1)
    code = jnp.where(filled, code, -1).reshape(-1, 1)
    row = ((held >> 4) * TOK_GRP + (held & 15) * 2).T[:, :, None, None]
    row = row + (draft & 1) * (TOK_GRP // 2) + (draft >> 1)
    row = jnp.where(filled[..., None], row, -1)
    row = jnp.where(hp == hp.reshape(2, 1, 1, 1, 1), row, -1).reshape(2 * SLOTS, -1)

    chip = z * xs + x
    mine = lax.dynamic_index_in_dim(held, chip, 0, keepdims=False)
    slabs = lax.dynamic_index_in_dim(slot_slab, group, 0, keepdims=False).reshape(chips, cores, SLOTS)
    slabs = lax.dynamic_index_in_dim(slabs, chip, 0, keepdims=False)
    slabs = lax.dynamic_index_in_dim(slabs, core, 0, keepdims=False)
    is_mine = mine[:, None] == jnp.arange(context_length.shape[0], dtype=jnp.int32)
    length = jnp.sum(jnp.where(is_mine, context_length, 0), axis=1)
    count = jnp.where(mine >= 0, length - slabs * kv_cache.shape[3], 0).astype(jnp.int32)

    copies = groups * cores
    narrow = pl.pallas_call(
        project_kernel,
        out_shape=jax.ShapeDtypeStruct((TOK_GRP, NARROW), BF16),
        in_specs=[HBM] * 3,
        out_specs=VMEM,
        scratch_shapes=[
            *(pltpu.VMEM(a.shape, BF16) for a in (q_compressed, w_q_nope, w_q_rope)),
            pltpu.SemaphoreType.DMA((4,)),
        ],
        compiler_params=pltpu.CompilerParams(vmem_limit_bytes=16 << 20),
        cost_estimate=pl.CostEstimate(flops=2 << 30, transcendentals=0, bytes_accessed=4 << 20),
    )(*(in_hbm(a) for a in (q_compressed, w_q_nope, w_q_rope)))
    late_uk, narrow = lax.optimization_barrier((w_uk, narrow))
    own_q = [narrow]
    for k in range(1, groups):
        own_q.append(lax.ppermute(narrow, "group", [(i, (i + k) % groups) for i in range(groups)]))
    own_q = jnp.concatenate(own_q, axis=0)
    mate_q = lax.ppermute(own_q, "core", swap)
    mate_uk = lax.ppermute(late_uk, "core", swap)
    rows = chips * cores * DRAFT
    wide = pl.pallas_call(
        spread_kernel,
        out_shape=jax.ShapeDtypeStruct((rows, SLOTS * WIDE), BF16),
        grid=(SLOTS,),
        in_specs=[VMEM, VMEM, pl.BlockSpec((rows, 1), lambda k: (k, 0)), VMEM, VMEM],
        out_specs=pl.BlockSpec((rows, WIDE), lambda k: (0, k)),
        scratch_shapes=[pltpu.VMEM((copies * TOK_GRP, 5 * NOPE), BF16)],
        compiler_params=pltpu.CompilerParams(
            dimension_semantics=("arbitrary",), vmem_limit_bytes=16 << 20
        ),
        cost_estimate=pl.CostEstimate(flops=30 << 30, transcendentals=0, bytes_accessed=80 << 20),
    )(own_q, mate_q, code, w_uk, mate_uk)
    slabs_kv = jnp.swapaxes(kv_cache.reshape(kv_cache.shape[2:]), 1, 2)
    count, wide = lax.optimization_barrier((count, wide))
    arrived = exchange(wide, ("z", "x"), chips)
    partials = attend(count, arrived, slabs_kv)
    late_o, late_uv, partials = lax.optimization_barrier((w_o, w_uv, partials))
    mate_o = lax.ppermute(late_o, "core", swap)
    mate_uv = lax.ppermute(late_uv, "core", swap)
    draft_hv, draft_log = call(
        draft_kernel,
        (
            jax.ShapeDtypeStruct((TOK_GRP // 2, 4 * VDIM), F32),
            jax.ShapeDtypeStruct((TOK_GRP // 2, 128), F32),
        ),
        (core_id, own_q, mate_q, w_uk, mate_uk, w_uv, mate_uv, draft_kv),
        [SMEM] + [VMEM] * 7,
    )
    back = exchange(partials, ("z", "x"), chips)
    both_o = jnp.concatenate([w_o, mate_o], axis=0)
    back, draft_hv, draft_log, both_o = lax.optimization_barrier((back, draft_hv, draft_log, both_o))
    merged = call(
        merge_kernel,
        jax.ShapeDtypeStruct((groups * TOK_GRP, 4 * VDIM + 128), BF16),
        (core_id, back, row, w_uv, mate_uv),
        [SMEM] + [VMEM] * 4,
        vmem=16,
        cost=pl.CostEstimate(flops=3 << 30, transcendentals=1 << 19, bytes_accessed=8 << 20),
    )
    home = exchange(merged, ("group", "core"), copies)
    sums = call(
        finish_kernel,
        jax.ShapeDtypeStruct((chips, w_o.shape[1]), BF16),
        (core_id, home, draft_hv, draft_log, both_o),
        [SMEM] + [VMEM] * 4,
    )
    tiles = lax.all_to_all(sums.reshape(chips, 8, -1), ("z", "x"), 0, 0, tiled=True)
    return call(
        total_kernel, jax.ShapeDtypeStruct((1, w_o.shape[1]), F32), (tiles,), [VMEM]
    )


def solution(mesh):
    fine = Mesh(mesh.devices.reshape(4, 8, 4, 2), ("group", "z", "x", "core"))
    dev = ("z", "x", "core")
    placed = (
        P("group", None),
        P(None, dev),
        P(None, dev),
        P(dev, None, None),
        P(dev, None, None),
        P(dev, None),
        P("group", dev, None, None, None),
        P("group", None),
        P(),
        P(),
        P(),
    )
    return jax.shard_map(
        shards, mesh=fine, in_specs=placed, out_specs=P(("group", *dev), None), check_vma=False
    )
```

```python
import jax
import jax.numpy as jnp
from jax import lax
from jax.experimental import pallas as pl
from jax.experimental.pallas import tpu as pltpu
from jax.sharding import Mesh
from jax.sharding import PartitionSpec as P

NOPE = 128
ROPE = 64
LATENT = 512
VDIM = 128
DRAFT = 4
SEQ_GRP = 16
TOK_GRP = SEQ_GRP * DRAFT
SLOTS = 2
KEY = LATENT + ROPE
WIDE = 2 * LATENT + 2 * ROPE
PART = SLOTS * 2 * LATENT + 128
NARROW = 2 * NOPE + 2 * ROPE
EMPTY = -1e30
SCALE = (NOPE + ROPE) ** -0.5
F32 = jnp.float32
BF16 = jnp.bfloat16
CONTRACT_LAST = (((1,), (1,)), ((), ()))

VMEM = pl.BlockSpec(memory_space=pltpu.VMEM)
SMEM = pl.BlockSpec(memory_space=pltpu.SMEM)
HBM = pl.BlockSpec(memory_space=pltpu.HBM)


def in_hbm(array):
    return pltpu.with_memory_space_constraint(array, pltpu.HBM)


def dot(a, b):
    return jnp.dot(a, b, preferred_element_type=F32)


def dot_t(a, b):
    return lax.dot_general(a, b, CONTRACT_LAST, preferred_element_type=F32)


def call(kernel, outs, args, specs, scratch=(), vmem=32, cost=None):
    return pl.pallas_call(
        kernel,
        out_shape=outs,
        in_specs=specs,
        out_specs=jax.tree.map(lambda _: VMEM, outs),
        scratch_shapes=list(scratch),
        compiler_params=pltpu.CompilerParams(vmem_limit_bytes=vmem << 20),
        cost_estimate=cost,
    )(*args)


def three_terms(value):
    high = value.astype(BF16).astype(F32)
    middle = (value - high).astype(BF16).astype(F32)
    return high, middle, (value - high - middle).astype(BF16).astype(F32)


def put_terms(tile, value, first):
    lane = lax.broadcasted_iota(jnp.int32, tile.shape, 1)
    for i, term in enumerate(three_terms(value)):
        tile = jnp.where(lane == first + i, term, tile)
    return tile


def project_kernel(q_hbm, wn_hbm, wr_hbm, out_ref, q_ref, wn_ref, wr_ref, sems):
    copies = []
    depth = wn_ref.shape[0] // 2
    for i, (source, target) in enumerate(((q_hbm, q_ref), (wr_hbm, wr_ref))):
        copies.append(pltpu.make_async_copy(source, target, sems.at[i]))
    for i in range(2):
        at = pl.ds(i * depth, depth)
        copies.append(pltpu.make_async_copy(wn_hbm.at[at], wn_ref.at[at], sems.at[2 + i]))
    for copy in copies:
        copy.start()
    copies[0].wait()
    copies[1].wait()
    out_ref[:, 2 * NOPE :] = (dot(q_ref[...], wr_ref[...]) * SCALE).astype(BF16)
    copies[2].wait()
    copies[3].wait()
    out_ref[:, : 2 * NOPE] = dot(q_ref[...], wn_ref[...]).astype(BF16)


def spread_kernel(own_q, mate_q, code_ref, own_ref, mate_ref, out_ref, rows):
    @pl.when(pl.program_id(0) == 0)
    def _():
        rows[...] = jnp.zeros_like(rows)
        count = own_q.shape[0]
        for rel, q_ref in enumerate((own_q, mate_q)):
            at = slice(rel * count, (rel + 1) * count)
            for par in range(2):
                first = par * 2 * NOPE + rel * NOPE
                rows[at, first : first + NOPE] = q_ref[:, par * NOPE : (par + 1) * NOPE]
            rows[at, 4 * NOPE :] = q_ref[:, 2 * NOPE :]

    column = lax.broadcasted_iota(jnp.int32, (code_ref.shape[0], rows.shape[0]), 1)
    pick = jnp.where(column == code_ref[...], 1.0, 0.0).astype(BF16)
    picked = dot(pick, rows[...]).astype(BF16)
    for par in range(2):
        weight = jnp.concatenate([own_ref[par], mate_ref[par]], axis=0)
        absorbed = dot(picked[:, par * 2 * NOPE : (par + 1) * 2 * NOPE], weight) * SCALE
        out_ref[:, par * LATENT : (par + 1) * LATENT] = absorbed.astype(BF16)
    out_ref[:, 2 * LATENT :] = picked[:, 4 * NOPE :]


def draft_kernel(
    core_ref, own_q, mate_q, own_uk, mate_uk, own_uv, mate_uv, kv_ref, hv_ref, log_ref
):
    core = core_ref[0]
    half = hv_ref.shape[0]
    row = 2 * lax.broadcasted_iota(jnp.int32, (half, TOK_GRP), 0) + core
    col = lax.broadcasted_iota(jnp.int32, (half, TOK_GRP), 1)
    seen = (row // DRAFT == col // DRAFT) & (col <= row)
    pick = jnp.where(row == col, 1.0, 0.0).astype(BF16)
    lane = lax.broadcasted_iota(jnp.int32, log_ref.shape, 1)
    logs = jnp.zeros(log_ref.shape, F32)
    sides = ((core, own_q, own_uk, own_uv), (1 - core, mate_q, mate_uk, mate_uv))
    for hp, q_ref, uk_ref, uv_ref in sides:
        rows = dot(pick, q_ref[:TOK_GRP, :]).astype(BF16)
        for par in range(2):
            narrow = rows[:, par * NOPE : (par + 1) * NOPE]
            absorbed = (dot(narrow, uk_ref[par]) * SCALE).astype(BF16)
            first = 2 * NOPE + par * ROPE
            scores = dot_t(absorbed, kv_ref[:, :LATENT])
            scores += dot_t(rows[:, first : first + ROPE], kv_ref[:, LATENT:])
            scores = jnp.where(seen, scores, EMPTY)
            peak = jnp.max(scores, axis=1, keepdims=True)
            weights = jnp.where(seen, jnp.exp(scores - peak), 0.0)
            total = jnp.sum(weights, axis=1, keepdims=True)
            mixture = dot(weights.astype(BF16), kv_ref[:, :LATENT]) / total
            head = hp * 2 + par
            at = pl.ds(pl.multiple_of(head * VDIM, VDIM), VDIM)
            hv_ref[:, at] = dot(mixture.astype(BF16), uv_ref[par])
            logs = jnp.where(lane == head, peak + jnp.log(total), logs)
    log_ref[...] = logs


def attend_kernel(
    count_ref, x_ref, kv_ref, out_hbm, queries, scores, weights, out_ref, sems
):
    half = x_ref.shape[0]
    slab = kv_ref.shape[2]
    chunk = 256
    base = SLOTS * 2 * LATENT
    lane = lax.broadcasted_iota(jnp.int32, (half, 128), 1)
    tile = jnp.zeros((half, 128), F32)
    copies = []
    for slot in range(SLOTS):
        count = count_ref[slot]
        for par in range(2):
            at = slice(par * half, (par + 1) * half)
            first = slot * WIDE + par * LATENT
            queries[at, :LATENT] = x_ref[:, first : first + LATENT]
            first = slot * WIDE + 2 * LATENT + par * ROPE
            queries[at, LATENT:] = x_ref[:, first : first + ROPE]
        peak = jnp.full((2 * half, 1), EMPTY, F32)
        for first in range(0, slab, chunk):
            score = dot(queries[...], kv_ref[slot, :, first : first + chunk])
            position = lax.broadcasted_iota(jnp.int32, score.shape, 1) + first
            score = jnp.where(position < count, score, EMPTY)
            scores[:, first : first + chunk] = score
            peak = jnp.maximum(peak, jnp.max(score, axis=1, keepdims=True))
        reference = jnp.maximum(peak, EMPTY / 10)
        total = jnp.zeros((2 * half, 1), F32)
        for first in range(0, slab, chunk):
            weight = jnp.exp(scores[:, first : first + chunk] - reference)
            total += jnp.sum(weight, axis=1, keepdims=True)
            weights[:, first : first + chunk] = weight.astype(BF16)
        total = jnp.maximum(total, 1.0)
        mixture = dot_t(weights[...], kv_ref[slot, :LATENT, :])
        mixture = (mixture * (1.0 / total)).astype(BF16)
        log = peak + jnp.log(total)
        start = slot * 2 * LATENT
        for par in range(2):
            at = slice(par * half, (par + 1) * half)
            out_ref[:, start + par * LATENT : start + (par + 1) * LATENT] = mixture[at]
            for i, term in enumerate(three_terms(log[at])):
                tile = jnp.where(lane == slot * 6 + par * 3 + i, term, tile)
        end = start + 2 * LATENT
        if slot == SLOTS - 1:
            out_ref[:, base:] = tile.astype(BF16)
            end = PART
        at = pl.ds(start, end - start)
        copies.append(pltpu.make_async_copy(out_ref.at[:, at], out_hbm.at[:, at], sems.at[slot]))
        copies[-1].start()
    for copy in copies:
        copy.wait()


def attend(count, x, kv):
    rows = x.shape[0]
    return pl.pallas_call(
        attend_kernel,
        out_shape=jax.ShapeDtypeStruct((rows, PART), BF16),
        in_specs=[SMEM, VMEM, VMEM],
        out_specs=HBM,
        scratch_shapes=[
            pltpu.VMEM((2 * rows, KEY), BF16),
            pltpu.VMEM((2 * rows, kv.shape[2]), F32),
            pltpu.VMEM((2 * rows, kv.shape[2]), BF16),
            pltpu.VMEM((rows, PART), BF16),
            pltpu.SemaphoreType.DMA((SLOTS,)),
        ],
        compiler_params=pltpu.CompilerParams(vmem_limit_bytes=32 << 20),
    )(count, x, kv)


def merge_kernel(core_ref, y_ref, code_ref, own_ref, mate_ref, own_out, mate_out):
    core = core_ref[0]
    half = own_out.shape[0]
    rows, cols = 2 * half, y_ref.shape[0]
    base = SLOTS * 2 * LATENT
    logs = jnp.transpose(y_ref[:, base:].astype(F32))
    row = lax.broadcasted_iota(jnp.int32, (rows, cols), 0)
    tile = jnp.zeros((rows, 128), F32)
    for hp in range(2):
        match = [row == code_ref[hp * 2 + slot : hp * 2 + slot + 1, :] for slot in range(SLOTS)]
        for par in range(2):
            held = []
            for slot in range(SLOTS):
                at = slot * 6 + par * 3
                log = logs[at : at + 1, :] + logs[at + 1 : at + 2, :] + logs[at + 2 : at + 3, :]
                held.append(jnp.where(match[slot], log, EMPTY))
            peak = jnp.max(jnp.maximum(held[0], held[1]), axis=1, keepdims=True)
            total = jnp.zeros((rows, 1), F32)
            mixture = jnp.zeros((rows, LATENT), F32)
            for slot in range(SLOTS):
                weights = jnp.where(match[slot], jnp.exp(held[slot] - peak), 0.0)
                total += jnp.sum(weights, axis=1, keepdims=True)
                first = slot * 2 * LATENT + par * LATENT
                mixture += dot(weights.astype(BF16), y_ref[:, first : first + LATENT])
            total = jnp.maximum(total, 1.0)
            mixture = (mixture / total).astype(BF16)
            head = hp * 2 + par
            values = dot(mixture, jnp.where(core == hp, own_ref[par], mate_ref[par]))
            own_out[:, head * VDIM : (head + 1) * VDIM] = values[:half].astype(BF16)
            mate_out[:, head * VDIM : (head + 1) * VDIM] = values[half:].astype(BF16)
            tile = put_terms(tile, peak + jnp.log(total), head * 3)
    own_out[:, 4 * VDIM :] = tile[:half].astype(BF16)
    mate_out[:, 4 * VDIM :] = tile[half:].astype(BF16)


def finish_kernel(core_ref, own_ref, mate_ref, *refs):
    *others, hv_ref, log_ref, o_ref, out_ref = refs
    half = hv_ref.shape[0]
    blocks = [(own_ref, slice(0, half)), (mate_ref, slice(0, half))]
    for other in others:
        blocks += [(other, slice(0, half)), (other, slice(half, 2 * half))]
    values = []
    for head in range(4):
        logs = [log_ref[:, head : head + 1]]
        parts = [hv_ref[:, head * VDIM : (head + 1) * VDIM]]
        for z_ref, at in blocks:
            terms = z_ref[at, 4 * VDIM :].astype(F32)
            first = head * 3
            logs.append(
                terms[:, first : first + 1]
                + terms[:, first + 1 : first + 2]
                + terms[:, first + 2 : first + 3]
            )
            parts.append(z_ref[at, head * VDIM : (head + 1) * VDIM].astype(F32))
        peak = logs[0]
        for log in logs[1:]:
            peak = jnp.maximum(peak, log)
        total = jnp.zeros_like(peak)
        summed = jnp.zeros_like(parts[0])
        for log, part in zip(logs, parts):
            weight = jnp.exp(log - peak)
            total += weight
            summed += weight * part
        values.append(summed / total)
    pairs = [jnp.concatenate(values[hp * 2 : hp * 2 + 2], axis=1) for hp in range(2)]
    own = jnp.where(core_ref[0] == 0, pairs[0], pairs[1])
    mate = jnp.where(core_ref[0] == 0, pairs[1], pairs[0])
    head_values = jnp.concatenate([own, mate], axis=1).astype(BF16)
    out_ref[...] = dot(head_values, o_ref[...]).astype(BF16)


def total_kernel(tiles_ref, out_ref):
    total = jnp.sum(tiles_ref[...].astype(F32), axis=0)
    width = total.shape[1]
    for i in range(total.shape[0]):
        out_ref[:, i * width : (i + 1) * width] = total[i : i + 1]


def exchange(array, axes, peers):
    blocks = array.reshape(peers, array.shape[0] // peers, *array.shape[1:])
    return lax.all_to_all(blocks, axes, 0, 0, tiled=True).reshape(array.shape)


def shards(
    q_compressed,
    w_q_nope,
    w_q_rope,
    w_uk,
    w_uv,
    w_o,
    kv_cache,
    draft_kv,
    context_length,
    slot_sequence,
    slot_slab,
):
    groups, zs, xs, cores = (lax.axis_size(a) for a in ("group", "z", "x", "core"))
    group, z, x, core = (lax.axis_index(a) for a in ("group", "z", "x", "core"))
    chips = zs * xs
    core_id = core.astype(jnp.int32).reshape(1)
    swap = [(i, 1 - i) for i in range(cores)]

    table = lax.dynamic_index_in_dim(slot_sequence, group, 0, keepdims=False)
    table = table.reshape(chips, cores, SLOTS)
    held = lax.dynamic_index_in_dim(table, core, 1, keepdims=False)
    hp = jnp.arange(2, dtype=jnp.int32)[:, None]
    draft = jnp.arange(DRAFT, dtype=jnp.int32)
    filled = (held >= 0).T[:, :, None]
    shift = (group - (held >> 4)) & (groups - 1)
    code = (shift * TOK_GRP + (held & 15) * DRAFT).T[:, :, None]
    code = code + ((hp != core) * (groups * TOK_GRP) + draft).reshape(-1)
    code = jnp.where(filled, code, -1).reshape(-1, 1)
    quarter = TOK_GRP // 2
    ahead = ((held >> 4) - group) & (groups - 1)
    row = (ahead * quarter + (held & 15) * 2).T[:, :, None, None]
    row = row + ((draft & 1) != core) * (groups * quarter) + (draft >> 1)
    row = jnp.where(filled[..., None], row, -1)
    row = jnp.where(hp == hp.reshape(2, 1, 1, 1, 1), row, -1).reshape(2 * SLOTS, -1)

    chip = z * xs + x
    mine = lax.dynamic_index_in_dim(held, chip, 0, keepdims=False)
    slabs = lax.dynamic_index_in_dim(slot_slab, group, 0, keepdims=False).reshape(chips, cores, SLOTS)
    slabs = lax.dynamic_index_in_dim(slabs, chip, 0, keepdims=False)
    slabs = lax.dynamic_index_in_dim(slabs, core, 0, keepdims=False)
    is_mine = mine[:, None] == jnp.arange(context_length.shape[0], dtype=jnp.int32)
    length = jnp.sum(jnp.where(is_mine, context_length, 0), axis=1)
    count = jnp.where(mine >= 0, length - slabs * kv_cache.shape[3], 0).astype(jnp.int32)

    narrow = pl.pallas_call(
        project_kernel,
        out_shape=jax.ShapeDtypeStruct((TOK_GRP, NARROW), BF16),
        in_specs=[HBM] * 3,
        out_specs=VMEM,
        scratch_shapes=[
            *(pltpu.VMEM(a.shape, BF16) for a in (q_compressed, w_q_nope, w_q_rope)),
            pltpu.SemaphoreType.DMA((4,)),
        ],
        compiler_params=pltpu.CompilerParams(vmem_limit_bytes=16 << 20),
        cost_estimate=pl.CostEstimate(flops=2 << 30, transcendentals=0, bytes_accessed=4 << 20),
    )(*(in_hbm(a) for a in (q_compressed, w_q_nope, w_q_rope)))
    late_uk, narrow = lax.optimization_barrier((w_uk, narrow))
    own_q = [narrow]
    for k in range(1, groups):
        own_q.append(lax.ppermute(narrow, "group", [(i, (i + k) % groups) for i in range(groups)]))
    own_q = jnp.concatenate(own_q, axis=0)
    mate_q = lax.ppermute(own_q, "core", swap)
    mate_uk = lax.ppermute(late_uk, "core", swap)
    rows = chips * cores * DRAFT
    wide = pl.pallas_call(
        spread_kernel,
        out_shape=jax.ShapeDtypeStruct((rows, SLOTS * WIDE), BF16),
        grid=(SLOTS,),
        in_specs=[VMEM, VMEM, pl.BlockSpec((rows, 1), lambda k: (k, 0)), VMEM, VMEM],
        out_specs=pl.BlockSpec((rows, WIDE), lambda k: (0, k)),
        scratch_shapes=[pltpu.VMEM((groups * cores * TOK_GRP, 5 * NOPE), BF16)],
        compiler_params=pltpu.CompilerParams(
            dimension_semantics=("arbitrary",), vmem_limit_bytes=16 << 20
        ),
        cost_estimate=pl.CostEstimate(flops=30 << 30, transcendentals=0, bytes_accessed=80 << 20),
    )(own_q, mate_q, code, w_uk, mate_uk)
    slabs_kv = jnp.swapaxes(kv_cache.reshape(kv_cache.shape[2:]), 1, 2)
    count, wide = lax.optimization_barrier((count, wide))
    arrived = exchange(wide, ("z", "x"), chips)
    partials = attend(count, arrived, slabs_kv)
    late_o, late_uv, partials = lax.optimization_barrier((w_o, w_uv, partials))
    mate_o = lax.ppermute(late_o, "core", swap)
    mate_uv = lax.ppermute(late_uv, "core", swap)
    draft_hv, draft_log = call(
        draft_kernel,
        (
            jax.ShapeDtypeStruct((TOK_GRP // 2, 4 * VDIM), F32),
            jax.ShapeDtypeStruct((TOK_GRP // 2, 128), F32),
        ),
        (core_id, own_q, mate_q, w_uk, mate_uk, w_uv, mate_uv, draft_kv),
        [SMEM] + [VMEM] * 7,
    )
    back = exchange(partials, ("z", "x"), chips)
    both_o = jnp.concatenate([w_o, mate_o], axis=0)
    back, draft_hv, draft_log, both_o = lax.optimization_barrier((back, draft_hv, draft_log, both_o))
    part = jax.ShapeDtypeStruct((groups * quarter, 4 * VDIM + 128), BF16)
    own_part, mate_part = call(
        merge_kernel,
        (part, part),
        (core_id, back, row, w_uv, mate_uv),
        [SMEM] + [VMEM] * 4,
        vmem=16,
        cost=pl.CostEstimate(flops=3 << 30, transcendentals=1 << 19, bytes_accessed=8 << 20),
    )
    mate_part = lax.ppermute(mate_part, "core", swap)
    others = []
    for k in range(1, groups):
        at = slice(k * quarter, (k + 1) * quarter)
        pair = jnp.concatenate([own_part[at], mate_part[at]], axis=0)
        others.append(lax.ppermute(pair, "group", [(i, (i + k) % groups) for i in range(groups)]))
    sums = call(
        finish_kernel,
        jax.ShapeDtypeStruct((chips, w_o.shape[1]), BF16),
        (core_id, own_part, mate_part, *others, draft_hv, draft_log, both_o),
        [SMEM] + [VMEM] * (groups + 4),
    )
    tiles = lax.all_to_all(sums.reshape(chips, 8, -1), ("z", "x"), 0, 0, tiled=True)
    return call(
        total_kernel, jax.ShapeDtypeStruct((1, w_o.shape[1]), F32), (tiles,), [VMEM]
    )


def solution(mesh):
    fine = Mesh(mesh.devices.reshape(4, 8, 4, 2), ("group", "z", "x", "core"))
    dev = ("z", "x", "core")
    placed = (
        P("group", None),
        P(None, dev),
        P(None, dev),
        P(dev, None, None),
        P(dev, None, None),
        P(dev, None),
        P("group", dev, None, None, None),
        P("group", None),
        P(),
        P(),
        P(),
    )
    return jax.shard_map(
        shards, mesh=fine, in_specs=placed, out_specs=P(("group", *dev), None), check_vma=False
    )
```

```python
import jax
import jax.numpy as jnp
from jax import lax
from jax.experimental import pallas as pl
from jax.experimental.pallas import tpu as pltpu
from jax.sharding import Mesh
from jax.sharding import PartitionSpec as P

NOPE = 128
ROPE = 64
LATENT = 512
VDIM = 128
DRAFT = 4
SEQ_GRP = 16
TOK_GRP = SEQ_GRP * DRAFT
SLOTS = 2
KEY = LATENT + ROPE
WIDE = 2 * LATENT + 2 * ROPE
PART = SLOTS * 2 * LATENT + 128
NARROW = 2 * NOPE + 2 * ROPE
EMPTY = -1e30
SCALE = (NOPE + ROPE) ** -0.5
F32 = jnp.float32
BF16 = jnp.bfloat16
CONTRACT_LAST = (((1,), (1,)), ((), ()))

VMEM = pl.BlockSpec(memory_space=pltpu.VMEM)
SMEM = pl.BlockSpec(memory_space=pltpu.SMEM)
HBM = pl.BlockSpec(memory_space=pltpu.HBM)


def in_hbm(array):
    return pltpu.with_memory_space_constraint(array, pltpu.HBM)


def dot(a, b):
    return jnp.dot(a, b, preferred_element_type=F32)


def dot_t(a, b):
    return lax.dot_general(a, b, CONTRACT_LAST, preferred_element_type=F32)


def call(kernel, outs, args, specs, scratch=(), vmem=32, cost=None):
    return pl.pallas_call(
        kernel,
        out_shape=outs,
        in_specs=specs,
        out_specs=jax.tree.map(lambda _: VMEM, outs),
        scratch_shapes=list(scratch),
        compiler_params=pltpu.CompilerParams(vmem_limit_bytes=vmem << 20),
        cost_estimate=cost,
    )(*args)


def three_terms(value):
    high = value.astype(BF16).astype(F32)
    middle = (value - high).astype(BF16).astype(F32)
    return high, middle, (value - high - middle).astype(BF16).astype(F32)


def put_terms(tile, value, first):
    lane = lax.broadcasted_iota(jnp.int32, tile.shape, 1)
    for i, term in enumerate(three_terms(value)):
        tile = jnp.where(lane == first + i, term, tile)
    return tile


def project_kernel(q_hbm, wn_hbm, wr_hbm, out_ref, q_ref, wn_ref, wr_ref, sems):
    copies = []
    depth = wn_ref.shape[0] // 2
    for i, (source, target) in enumerate(((q_hbm, q_ref), (wr_hbm, wr_ref))):
        copies.append(pltpu.make_async_copy(source, target, sems.at[i]))
    for i in range(2):
        at = pl.ds(i * depth, depth)
        copies.append(pltpu.make_async_copy(wn_hbm.at[at], wn_ref.at[at], sems.at[2 + i]))
    for copy in copies:
        copy.start()
    copies[0].wait()
    copies[1].wait()
    out_ref[:, 2 * NOPE :] = (dot(q_ref[...], wr_ref[...]) * SCALE).astype(BF16)
    copies[2].wait()
    copies[3].wait()
    out_ref[:, : 2 * NOPE] = dot(q_ref[...], wn_ref[...]).astype(BF16)


def spread_kernel(own_q, mate_q, code_ref, own_ref, mate_ref, out_ref, rows):
    @pl.when(pl.program_id(0) == 0)
    def _():
        rows[...] = jnp.zeros_like(rows)
        count = own_q.shape[0]
        for rel, q_ref in enumerate((own_q, mate_q)):
            at = slice(rel * count, (rel + 1) * count)
            for par in range(2):
                first = par * 2 * NOPE + rel * NOPE
                rows[at, first : first + NOPE] = q_ref[:, par * NOPE : (par + 1) * NOPE]
            rows[at, 4 * NOPE :] = q_ref[:, 2 * NOPE :]

    column = lax.broadcasted_iota(jnp.int32, (code_ref.shape[0], rows.shape[0]), 1)
    pick = jnp.where(column == code_ref[...], 1.0, 0.0).astype(BF16)
    picked = dot(pick, rows[...]).astype(BF16)
    for par in range(2):
        weight = jnp.concatenate([own_ref[par], mate_ref[par]], axis=0)
        absorbed = dot(picked[:, par * 2 * NOPE : (par + 1) * 2 * NOPE], weight) * SCALE
        out_ref[:, par * LATENT : (par + 1) * LATENT] = absorbed.astype(BF16)
    out_ref[:, 2 * LATENT :] = picked[:, 4 * NOPE :]


def draft_kernel(
    core_ref, own_q, mate_q, own_uk, mate_uk, own_uv, mate_uv, kv_ref, hv_ref, log_ref
):
    core = core_ref[0]
    half = hv_ref.shape[0]
    row = 2 * lax.broadcasted_iota(jnp.int32, (half, TOK_GRP), 0) + core
    col = lax.broadcasted_iota(jnp.int32, (half, TOK_GRP), 1)
    seen = (row // DRAFT == col // DRAFT) & (col <= row)
    pick = jnp.where(row == col, 1.0, 0.0).astype(BF16)
    lane = lax.broadcasted_iota(jnp.int32, log_ref.shape, 1)
    logs = jnp.zeros(log_ref.shape, F32)
    sides = ((core, own_q, own_uk, own_uv), (1 - core, mate_q, mate_uk, mate_uv))
    for hp, q_ref, uk_ref, uv_ref in sides:
        rows = dot(pick, q_ref[:TOK_GRP, :]).astype(BF16)
        for par in range(2):
            narrow = rows[:, par * NOPE : (par + 1) * NOPE]
            absorbed = (dot(narrow, uk_ref[par]) * SCALE).astype(BF16)
            first = 2 * NOPE + par * ROPE
            scores = dot_t(absorbed, kv_ref[:, :LATENT])
            scores += dot_t(rows[:, first : first + ROPE], kv_ref[:, LATENT:])
            scores = jnp.where(seen, scores, EMPTY)
            peak = jnp.max(scores, axis=1, keepdims=True)
            weights = jnp.where(seen, jnp.exp(scores - peak), 0.0)
            total = jnp.sum(weights, axis=1, keepdims=True)
            mixture = dot(weights.astype(BF16), kv_ref[:, :LATENT]) / total
            head = hp * 2 + par
            at = pl.ds(pl.multiple_of(head * VDIM, VDIM), VDIM)
            hv_ref[:, at] = dot(mixture.astype(BF16), uv_ref[par])
            logs = jnp.where(lane == head, peak + jnp.log(total), logs)
    log_ref[...] = logs


def attend_kernel(
    count_ref, x_ref, kv_ref, out_hbm, queries, scores, weights, out_ref, sems
):
    half = x_ref.shape[0]
    slab = kv_ref.shape[2]
    chunk = 256
    base = SLOTS * 2 * LATENT
    lane = lax.broadcasted_iota(jnp.int32, (half, 128), 1)
    tile = jnp.zeros((half, 128), F32)
    copies = []
    for slot in range(SLOTS):
        count = count_ref[slot]
        for par in range(2):
            at = slice(par * half, (par + 1) * half)
            first = slot * WIDE + par * LATENT
            queries[at, :LATENT] = x_ref[:, first : first + LATENT]
            first = slot * WIDE + 2 * LATENT + par * ROPE
            queries[at, LATENT:] = x_ref[:, first : first + ROPE]
        peak = jnp.full((2 * half, 1), EMPTY, F32)
        for first in range(0, slab, chunk):
            score = dot(queries[...], kv_ref[slot, :, first : first + chunk])
            position = lax.broadcasted_iota(jnp.int32, score.shape, 1) + first
            score = jnp.where(position < count, score, EMPTY)
            scores[:, first : first + chunk] = score
            peak = jnp.maximum(peak, jnp.max(score, axis=1, keepdims=True))
        reference = jnp.maximum(peak, EMPTY / 10)
        total = jnp.zeros((2 * half, 1), F32)
        for first in range(0, slab, chunk):
            weight = jnp.exp(scores[:, first : first + chunk] - reference)
            total += jnp.sum(weight, axis=1, keepdims=True)
            weights[:, first : first + chunk] = weight.astype(BF16)
        total = jnp.maximum(total, 1.0)
        mixture = dot_t(weights[...], kv_ref[slot, :LATENT, :])
        mixture = (mixture * (1.0 / total)).astype(BF16)
        log = peak + jnp.log(total)
        start = slot * 2 * LATENT
        for par in range(2):
            at = slice(par * half, (par + 1) * half)
            out_ref[:, start + par * LATENT : start + (par + 1) * LATENT] = mixture[at]
            for i, term in enumerate(three_terms(log[at])):
                tile = jnp.where(lane == slot * 6 + par * 3 + i, term, tile)
        end = start + 2 * LATENT
        if slot == SLOTS - 1:
            out_ref[:, base:] = tile.astype(BF16)
            end = PART
        at = pl.ds(start, end - start)
        copies.append(pltpu.make_async_copy(out_ref.at[:, at], out_hbm.at[:, at], sems.at[slot]))
        copies[-1].start()
    for copy in copies:
        copy.wait()


def attend(count, x, kv):
    rows = x.shape[0]
    return pl.pallas_call(
        attend_kernel,
        out_shape=jax.ShapeDtypeStruct((rows, PART), BF16),
        in_specs=[SMEM, VMEM, VMEM],
        out_specs=HBM,
        scratch_shapes=[
            pltpu.VMEM((2 * rows, KEY), BF16),
            pltpu.VMEM((2 * rows, kv.shape[2]), F32),
            pltpu.VMEM((2 * rows, kv.shape[2]), BF16),
            pltpu.VMEM((rows, PART), BF16),
            pltpu.SemaphoreType.DMA((SLOTS,)),
        ],
        compiler_params=pltpu.CompilerParams(vmem_limit_bytes=32 << 20),
    )(count, x, kv)


def merge_kernel(core_ref, y_ref, code_ref, own_ref, mate_ref, own_out, mate_out):
    core = core_ref[0]
    half = own_out.shape[0]
    rows, cols = 2 * half, y_ref.shape[0]
    base = SLOTS * 2 * LATENT
    logs = jnp.transpose(y_ref[:, base:].astype(F32))
    row = lax.broadcasted_iota(jnp.int32, (rows, cols), 0)
    tile = jnp.zeros((rows, 128), F32)
    for hp in range(2):
        match = [row == code_ref[hp * 2 + slot : hp * 2 + slot + 1, :] for slot in range(SLOTS)]
        for par in range(2):
            held = []
            for slot in range(SLOTS):
                at = slot * 6 + par * 3
                log = logs[at : at + 1, :] + logs[at + 1 : at + 2, :] + logs[at + 2 : at + 3, :]
                held.append(jnp.where(match[slot], log, EMPTY))
            peak = jnp.max(jnp.maximum(held[0], held[1]), axis=1, keepdims=True)
            total = jnp.zeros((rows, 1), F32)
            mixture = jnp.zeros((rows, LATENT), F32)
            for slot in range(SLOTS):
                weights = jnp.where(match[slot], jnp.exp(held[slot] - peak), 0.0)
                total += jnp.sum(weights, axis=1, keepdims=True)
                first = slot * 2 * LATENT + par * LATENT
                mixture += dot(weights.astype(BF16), y_ref[:, first : first + LATENT])
            total = jnp.maximum(total, 1.0)
            mixture = (mixture / total).astype(BF16)
            head = hp * 2 + par
            values = dot(mixture, jnp.where(core == hp, own_ref[par], mate_ref[par]))
            own_out[:, head * VDIM : (head + 1) * VDIM] = values[:half].astype(BF16)
            mate_out[:, head * VDIM : (head + 1) * VDIM] = values[half:].astype(BF16)
            tile = put_terms(tile, peak + jnp.log(total), head * 3)
    own_out[:, 4 * VDIM :] = tile[:half].astype(BF16)
    mate_out[:, 4 * VDIM :] = tile[half:].astype(BF16)


def finish_kernel(core_ref, own_ref, mate_ref, *refs):
    *others, hv_ref, log_ref, o_ref, out_ref = refs
    half = hv_ref.shape[0]
    blocks = [(own_ref, slice(0, half)), (mate_ref, slice(0, half))]
    for other in others:
        blocks += [(other, slice(0, half)), (other, slice(half, 2 * half))]
    values = []
    for head in range(4):
        logs = [log_ref[:, head : head + 1]]
        parts = [hv_ref[:, head * VDIM : (head + 1) * VDIM]]
        for z_ref, at in blocks:
            terms = z_ref[at, 4 * VDIM :].astype(F32)
            first = head * 3
            logs.append(
                terms[:, first : first + 1]
                + terms[:, first + 1 : first + 2]
                + terms[:, first + 2 : first + 3]
            )
            parts.append(z_ref[at, head * VDIM : (head + 1) * VDIM].astype(F32))
        peak = logs[0]
        for log in logs[1:]:
            peak = jnp.maximum(peak, log)
        total = jnp.zeros_like(peak)
        summed = jnp.zeros_like(parts[0])
        for log, part in zip(logs, parts):
            weight = jnp.exp(log - peak)
            total += weight
            summed += weight * part
        values.append(summed / total)
    pairs = [jnp.concatenate(values[hp * 2 : hp * 2 + 2], axis=1) for hp in range(2)]
    own = jnp.where(core_ref[0] == 0, pairs[0], pairs[1])
    mate = jnp.where(core_ref[0] == 0, pairs[1], pairs[0])
    head_values = jnp.concatenate([own, mate], axis=1).astype(BF16)
    out_ref[...] = dot(head_values, o_ref[...]).astype(BF16)


def total_kernel(tiles_ref, out_ref):
    total = jnp.sum(tiles_ref[...].astype(F32), axis=0)
    width = total.shape[1]
    for i in range(total.shape[0]):
        out_ref[:, i * width : (i + 1) * width] = total[i : i + 1]


def exchange(array, axes, peers):
    blocks = array.reshape(peers, array.shape[0] // peers, *array.shape[1:])
    return lax.all_to_all(blocks, axes, 0, 0, tiled=True).reshape(array.shape)


def shards(
    q_compressed,
    w_q_nope,
    w_q_rope,
    w_uk,
    w_uv,
    w_o,
    kv_cache,
    draft_kv,
    context_length,
    slot_sequence,
    slot_slab,
):
    groups, zs, xs, cores = (lax.axis_size(a) for a in ("group", "z", "x", "core"))
    group, z, x, core = (lax.axis_index(a) for a in ("group", "z", "x", "core"))
    chips = zs * xs
    core_id = core.astype(jnp.int32).reshape(1)
    swap = [(i, 1 - i) for i in range(cores)]

    table = lax.dynamic_index_in_dim(slot_sequence, group, 0, keepdims=False)
    table = table.reshape(chips, cores, SLOTS)
    held = lax.dynamic_index_in_dim(table, core, 1, keepdims=False)
    hp = jnp.arange(2, dtype=jnp.int32)[:, None]
    draft = jnp.arange(DRAFT, dtype=jnp.int32)
    filled = (held >= 0).T[:, :, None]
    shift = (group - (held >> 4)) & (groups - 1)
    code = (shift * TOK_GRP + (held & 15) * DRAFT).T[:, :, None]
    code = code + ((hp != core) * (groups * TOK_GRP) + draft).reshape(-1)
    code = jnp.where(filled, code, -1).reshape(-1, 1)
    quarter = TOK_GRP // 2
    ahead = ((held >> 4) - group) & (groups - 1)
    row = (ahead * quarter + (held & 15) * 2).T[:, :, None, None]
    row = row + ((draft & 1) != core) * (groups * quarter) + (draft >> 1)
    row = jnp.where(filled[..., None], row, -1)
    row = jnp.where(hp == hp.reshape(2, 1, 1, 1, 1), row, -1).reshape(2 * SLOTS, -1)

    chip = z * xs + x
    mine = lax.dynamic_index_in_dim(held, chip, 0, keepdims=False)
    slabs = lax.dynamic_index_in_dim(slot_slab, group, 0, keepdims=False).reshape(chips, cores, SLOTS)
    slabs = lax.dynamic_index_in_dim(slabs, chip, 0, keepdims=False)
    slabs = lax.dynamic_index_in_dim(slabs, core, 0, keepdims=False)
    is_mine = mine[:, None] == jnp.arange(context_length.shape[0], dtype=jnp.int32)
    length = jnp.sum(jnp.where(is_mine, context_length, 0), axis=1)
    count = jnp.where(mine >= 0, length - slabs * kv_cache.shape[3], 0).astype(jnp.int32)

    narrow = pl.pallas_call(
        project_kernel,
        out_shape=jax.ShapeDtypeStruct((TOK_GRP, NARROW), BF16),
        in_specs=[HBM] * 3,
        out_specs=VMEM,
        scratch_shapes=[
            *(pltpu.VMEM(a.shape, BF16) for a in (q_compressed, w_q_nope, w_q_rope)),
            pltpu.SemaphoreType.DMA((4,)),
        ],
        compiler_params=pltpu.CompilerParams(vmem_limit_bytes=16 << 20),
        cost_estimate=pl.CostEstimate(flops=2 << 30, transcendentals=0, bytes_accessed=4 << 20),
    )(*(in_hbm(a) for a in (q_compressed, w_q_nope, w_q_rope)))
    own_q = [narrow]
    for k in range(1, groups):
        own_q.append(lax.ppermute(narrow, "group", [(i, (i + k) % groups) for i in range(groups)]))
    own_q = jnp.concatenate(own_q, axis=0)
    mate_q = lax.ppermute(own_q, "core", swap)
    late_o, mate_q = lax.optimization_barrier((w_o, mate_q))
    mate_o = lax.ppermute(late_o, "core", swap)
    mate_uk = lax.ppermute(w_uk, "core", swap)
    rows = chips * cores * DRAFT
    wide = pl.pallas_call(
        spread_kernel,
        out_shape=jax.ShapeDtypeStruct((rows, SLOTS * WIDE), BF16),
        grid=(SLOTS,),
        in_specs=[VMEM, VMEM, pl.BlockSpec((rows, 1), lambda k: (k, 0)), VMEM, VMEM],
        out_specs=pl.BlockSpec((rows, WIDE), lambda k: (0, k)),
        scratch_shapes=[pltpu.VMEM((groups * cores * TOK_GRP, 5 * NOPE), BF16)],
        compiler_params=pltpu.CompilerParams(
            dimension_semantics=("arbitrary",), vmem_limit_bytes=16 << 20
        ),
        cost_estimate=pl.CostEstimate(flops=30 << 30, transcendentals=0, bytes_accessed=80 << 20),
    )(own_q, mate_q, code, w_uk, mate_uk)
    slabs_kv = jnp.swapaxes(kv_cache.reshape(kv_cache.shape[2:]), 1, 2)
    count, wide = lax.optimization_barrier((count, wide))
    arrived = exchange(wide, ("z", "x"), chips)
    partials = attend(count, arrived, slabs_kv)
    late_uv, partials = lax.optimization_barrier((w_uv, partials))
    mate_uv = lax.ppermute(late_uv, "core", swap)
    draft_hv, draft_log = call(
        draft_kernel,
        (
            jax.ShapeDtypeStruct((TOK_GRP // 2, 4 * VDIM), F32),
            jax.ShapeDtypeStruct((TOK_GRP // 2, 128), F32),
        ),
        (core_id, own_q, mate_q, w_uk, mate_uk, w_uv, mate_uv, draft_kv),
        [SMEM] + [VMEM] * 7,
    )
    back = exchange(partials, ("z", "x"), chips)
    both_o = jnp.concatenate([w_o, mate_o], axis=0)
    back, draft_hv, draft_log, both_o = lax.optimization_barrier((back, draft_hv, draft_log, both_o))
    part = jax.ShapeDtypeStruct((groups * quarter, 4 * VDIM + 128), BF16)
    own_part, mate_part = call(
        merge_kernel,
        (part, part),
        (core_id, back, row, w_uv, mate_uv),
        [SMEM] + [VMEM] * 4,
        vmem=16,
        cost=pl.CostEstimate(flops=3 << 30, transcendentals=1 << 19, bytes_accessed=8 << 20),
    )
    mate_part = lax.ppermute(mate_part, "core", swap)
    others = []
    for k in range(1, groups):
        at = slice(k * quarter, (k + 1) * quarter)
        pair = jnp.concatenate([own_part[at], mate_part[at]], axis=0)
        others.append(lax.ppermute(pair, "group", [(i, (i + k) % groups) for i in range(groups)]))
    sums = call(
        finish_kernel,
        jax.ShapeDtypeStruct((chips, w_o.shape[1]), BF16),
        (core_id, own_part, mate_part, *others, draft_hv, draft_log, both_o),
        [SMEM] + [VMEM] * (groups + 4),
    )
    tiles = lax.all_to_all(sums.reshape(chips, 8, -1), ("z", "x"), 0, 0, tiled=True)
    return call(
        total_kernel, jax.ShapeDtypeStruct((1, w_o.shape[1]), F32), (tiles,), [VMEM]
    )


def solution(mesh):
    fine = Mesh(mesh.devices.reshape(4, 8, 4, 2), ("group", "z", "x", "core"))
    dev = ("z", "x", "core")
    placed = (
        P("group", None),
        P(None, dev),
        P(None, dev),
        P(dev, None, None),
        P(dev, None, None),
        P(dev, None),
        P("group", dev, None, None, None),
        P("group", None),
        P(),
        P(),
        P(),
    )
    return jax.shard_map(
        shards, mesh=fine, in_specs=placed, out_specs=P(("group", *dev), None), check_vma=False
    )
```

```python
import jax
import jax.numpy as jnp
from jax import lax
from jax.experimental import pallas as pl
from jax.experimental.pallas import tpu as pltpu
from jax.sharding import Mesh
from jax.sharding import PartitionSpec as P

NOPE = 128
ROPE = 64
LATENT = 512
VDIM = 128
DRAFT = 4
SEQ_GRP = 16
TOK_GRP = SEQ_GRP * DRAFT
SLOTS = 2
KEY = LATENT + ROPE
WIDE = 2 * LATENT + 2 * ROPE
PART = SLOTS * 2 * LATENT + 128
NARROW = 2 * NOPE + 2 * ROPE
EMPTY = -1e30
SCALE = (NOPE + ROPE) ** -0.5
F32 = jnp.float32
BF16 = jnp.bfloat16
CONTRACT_LAST = (((1,), (1,)), ((), ()))

VMEM = pl.BlockSpec(memory_space=pltpu.VMEM)
SMEM = pl.BlockSpec(memory_space=pltpu.SMEM)
HBM = pl.BlockSpec(memory_space=pltpu.HBM)


def in_hbm(array):
    return pltpu.with_memory_space_constraint(array, pltpu.HBM)


def dot(a, b):
    return jnp.dot(a, b, preferred_element_type=F32)


def dot_t(a, b):
    return lax.dot_general(a, b, CONTRACT_LAST, preferred_element_type=F32)


def call(kernel, outs, args, specs, scratch=(), vmem=32, cost=None):
    return pl.pallas_call(
        kernel,
        out_shape=outs,
        in_specs=specs,
        out_specs=jax.tree.map(lambda _: VMEM, outs),
        scratch_shapes=list(scratch),
        compiler_params=pltpu.CompilerParams(vmem_limit_bytes=vmem << 20),
        cost_estimate=cost,
    )(*args)


def three_terms(value):
    high = value.astype(BF16).astype(F32)
    middle = (value - high).astype(BF16).astype(F32)
    return high, middle, (value - high - middle).astype(BF16).astype(F32)


def put_terms(tile, value, first):
    lane = lax.broadcasted_iota(jnp.int32, tile.shape, 1)
    for i, term in enumerate(three_terms(value)):
        tile = jnp.where(lane == first + i, term, tile)
    return tile


def project_kernel(q_hbm, wn_hbm, wr_hbm, out_ref, q_ref, wn_ref, wr_ref, sems):
    copies = []
    depth = wn_ref.shape[0] // 2
    for i, (source, target) in enumerate(((q_hbm, q_ref), (wr_hbm, wr_ref))):
        copies.append(pltpu.make_async_copy(source, target, sems.at[i]))
    for i in range(2):
        at = pl.ds(i * depth, depth)
        copies.append(pltpu.make_async_copy(wn_hbm.at[at], wn_ref.at[at], sems.at[2 + i]))
    for copy in copies:
        copy.start()
    copies[0].wait()
    copies[1].wait()
    out_ref[:, 2 * NOPE :] = (dot(q_ref[...], wr_ref[...]) * SCALE).astype(BF16)
    copies[2].wait()
    copies[3].wait()
    out_ref[:, : 2 * NOPE] = dot(q_ref[...], wn_ref[...]).astype(BF16)


def spread_kernel(own_q, mate_q, code_ref, own_ref, mate_ref, out_ref, rows):
    @pl.when(pl.program_id(0) == 0)
    def _():
        rows[...] = jnp.zeros_like(rows)
        count = own_q.shape[0]
        for rel, q_ref in enumerate((own_q, mate_q)):
            at = slice(rel * count, (rel + 1) * count)
            for par in range(2):
                first = par * 2 * NOPE + rel * NOPE
                rows[at, first : first + NOPE] = q_ref[:, par * NOPE : (par + 1) * NOPE]
            rows[at, 4 * NOPE :] = q_ref[:, 2 * NOPE :]

    column = lax.broadcasted_iota(jnp.int32, (code_ref.shape[0], rows.shape[0]), 1)
    pick = jnp.where(column == code_ref[...], 1.0, 0.0).astype(BF16)
    picked = dot(pick, rows[...]).astype(BF16)
    for par in range(2):
        weight = jnp.concatenate([own_ref[par], mate_ref[par]], axis=0)
        absorbed = dot(picked[:, par * 2 * NOPE : (par + 1) * 2 * NOPE], weight) * SCALE
        out_ref[:, par * LATENT : (par + 1) * LATENT] = absorbed.astype(BF16)
    out_ref[:, 2 * LATENT :] = picked[:, 4 * NOPE :]


def draft_kernel(
    core_ref, own_q, mate_q, own_uk, mate_uk, own_uv, mate_uv, kv_ref, hv_ref, log_ref
):
    core = core_ref[0]
    half = hv_ref.shape[0]
    row = 2 * lax.broadcasted_iota(jnp.int32, (half, TOK_GRP), 0) + core
    col = lax.broadcasted_iota(jnp.int32, (half, TOK_GRP), 1)
    seen = (row // DRAFT == col // DRAFT) & (col <= row)
    pick = jnp.where(row == col, 1.0, 0.0).astype(BF16)
    lane = lax.broadcasted_iota(jnp.int32, log_ref.shape, 1)
    logs = jnp.zeros(log_ref.shape, F32)
    sides = ((core, own_q, own_uk, own_uv), (1 - core, mate_q, mate_uk, mate_uv))
    for hp, q_ref, uk_ref, uv_ref in sides:
        rows = dot(pick, q_ref[:TOK_GRP, :]).astype(BF16)
        for par in range(2):
            narrow = rows[:, par * NOPE : (par + 1) * NOPE]
            absorbed = (dot(narrow, uk_ref[par]) * SCALE).astype(BF16)
            first = 2 * NOPE + par * ROPE
            scores = dot_t(absorbed, kv_ref[:, :LATENT])
            scores += dot_t(rows[:, first : first + ROPE], kv_ref[:, LATENT:])
            scores = jnp.where(seen, scores, EMPTY)
            peak = jnp.max(scores, axis=1, keepdims=True)
            weights = jnp.where(seen, jnp.exp(scores - peak), 0.0)
            total = jnp.sum(weights, axis=1, keepdims=True)
            mixture = dot(weights.astype(BF16), kv_ref[:, :LATENT]) / total
            head = hp * 2 + par
            at = pl.ds(pl.multiple_of(head * VDIM, VDIM), VDIM)
            hv_ref[:, at] = dot(mixture.astype(BF16), uv_ref[par])
            logs = jnp.where(lane == head, peak + jnp.log(total), logs)
    log_ref[...] = logs


def attend_kernel(
    count_ref, x_ref, kv_ref, out_hbm, queries, scores, weights, out_ref, sems
):
    half = x_ref.shape[0]
    slab = kv_ref.shape[2]
    chunk = 256
    base = SLOTS * 2 * LATENT
    lane = lax.broadcasted_iota(jnp.int32, (half, 128), 1)
    tile = jnp.zeros((half, 128), F32)
    copies = []
    for slot in range(SLOTS):
        count = count_ref[slot]
        for par in range(2):
            at = slice(par * half, (par + 1) * half)
            first = slot * WIDE + par * LATENT
            queries[at, :LATENT] = x_ref[:, first : first + LATENT]
            first = slot * WIDE + 2 * LATENT + par * ROPE
            queries[at, LATENT:] = x_ref[:, first : first + ROPE]
        peak = jnp.full((2 * half, 1), EMPTY, F32)
        for first in range(0, slab, chunk):
            score = dot(queries[...], kv_ref[slot, :, first : first + chunk])
            position = lax.broadcasted_iota(jnp.int32, score.shape, 1) + first
            score = jnp.where(position < count, score, EMPTY)
            scores[:, first : first + chunk] = score
            peak = jnp.maximum(peak, jnp.max(score, axis=1, keepdims=True))
        reference = jnp.maximum(peak, EMPTY / 10)
        total = jnp.zeros((2 * half, 1), F32)
        for first in range(0, slab, chunk):
            weight = jnp.exp(scores[:, first : first + chunk] - reference)
            total += jnp.sum(weight, axis=1, keepdims=True)
            weights[:, first : first + chunk] = weight.astype(BF16)
        total = jnp.maximum(total, 1.0)
        mixture = dot_t(weights[...], kv_ref[slot, :LATENT, :])
        mixture = (mixture * (1.0 / total)).astype(BF16)
        log = peak + jnp.log(total)
        start = slot * 2 * LATENT
        for par in range(2):
            at = slice(par * half, (par + 1) * half)
            out_ref[:, start + par * LATENT : start + (par + 1) * LATENT] = mixture[at]
            for i, term in enumerate(three_terms(log[at])):
                tile = jnp.where(lane == slot * 6 + par * 3 + i, term, tile)
        end = start + 2 * LATENT
        if slot == SLOTS - 1:
            out_ref[:, base:] = tile.astype(BF16)
            end = PART
        at = pl.ds(start, end - start)
        copies.append(pltpu.make_async_copy(out_ref.at[:, at], out_hbm.at[:, at], sems.at[slot]))
        copies[-1].start()
    for copy in copies:
        copy.wait()


def attend(count, x, kv):
    rows = x.shape[0]
    return pl.pallas_call(
        attend_kernel,
        out_shape=jax.ShapeDtypeStruct((rows, PART), BF16),
        in_specs=[SMEM, VMEM, VMEM],
        out_specs=HBM,
        scratch_shapes=[
            pltpu.VMEM((2 * rows, KEY), BF16),
            pltpu.VMEM((2 * rows, kv.shape[2]), F32),
            pltpu.VMEM((2 * rows, kv.shape[2]), BF16),
            pltpu.VMEM((rows, PART), BF16),
            pltpu.SemaphoreType.DMA((SLOTS,)),
        ],
        compiler_params=pltpu.CompilerParams(vmem_limit_bytes=32 << 20),
    )(count, x, kv)


def merge_kernel(core_ref, y_ref, code_ref, own_ref, mate_ref, own_out, mate_out):
    core = core_ref[0]
    half = own_out.shape[0]
    rows, cols = 2 * half, y_ref.shape[0]
    base = SLOTS * 2 * LATENT
    logs = jnp.transpose(y_ref[:, base:].astype(F32))
    row = lax.broadcasted_iota(jnp.int32, (rows, cols), 0)
    tile = jnp.zeros((rows, 128), F32)
    for hp in range(2):
        match = [row == code_ref[hp * 2 + slot : hp * 2 + slot + 1, :] for slot in range(SLOTS)]
        for par in range(2):
            held = []
            for slot in range(SLOTS):
                at = slot * 6 + par * 3
                log = logs[at : at + 1, :] + logs[at + 1 : at + 2, :] + logs[at + 2 : at + 3, :]
                held.append(jnp.where(match[slot], log, EMPTY))
            peak = jnp.max(jnp.maximum(held[0], held[1]), axis=1, keepdims=True)
            total = jnp.zeros((rows, 1), F32)
            mixture = jnp.zeros((rows, LATENT), F32)
            for slot in range(SLOTS):
                weights = jnp.where(match[slot], jnp.exp(held[slot] - peak), 0.0)
                total += jnp.sum(weights, axis=1, keepdims=True)
                first = slot * 2 * LATENT + par * LATENT
                mixture += dot(weights.astype(BF16), y_ref[:, first : first + LATENT])
            total = jnp.maximum(total, 1.0)
            mixture = (mixture / total).astype(BF16)
            head = hp * 2 + par
            values = dot(mixture, jnp.where(core == hp, own_ref[par], mate_ref[par]))
            own_out[:, head * VDIM : (head + 1) * VDIM] = values[:half].astype(BF16)
            mate_out[:, head * VDIM : (head + 1) * VDIM] = values[half:].astype(BF16)
            tile = put_terms(tile, peak + jnp.log(total), head * 3)
    own_out[:, 4 * VDIM :] = tile[:half].astype(BF16)
    mate_out[:, 4 * VDIM :] = tile[half:].astype(BF16)


def finish_kernel(core_ref, own_ref, mate_ref, *refs):
    *others, hv_ref, log_ref, o_ref, out_ref = refs
    half = hv_ref.shape[0]
    blocks = [(own_ref, slice(0, half)), (mate_ref, slice(0, half))]
    for other in others:
        blocks += [(other, slice(0, half)), (other, slice(half, 2 * half))]
    values = []
    for head in range(4):
        logs = [log_ref[:, head : head + 1]]
        parts = [hv_ref[:, head * VDIM : (head + 1) * VDIM]]
        for z_ref, at in blocks:
            terms = z_ref[at, 4 * VDIM :].astype(F32)
            first = head * 3
            logs.append(
                terms[:, first : first + 1]
                + terms[:, first + 1 : first + 2]
                + terms[:, first + 2 : first + 3]
            )
            parts.append(z_ref[at, head * VDIM : (head + 1) * VDIM].astype(F32))
        peak = logs[0]
        for log in logs[1:]:
            peak = jnp.maximum(peak, log)
        total = jnp.zeros_like(peak)
        summed = jnp.zeros_like(parts[0])
        for log, part in zip(logs, parts):
            weight = jnp.exp(log - peak)
            total += weight
            summed += weight * part
        values.append(summed / total)
    pairs = [jnp.concatenate(values[hp * 2 : hp * 2 + 2], axis=1) for hp in range(2)]
    own = jnp.where(core_ref[0] == 0, pairs[0], pairs[1])
    mate = jnp.where(core_ref[0] == 0, pairs[1], pairs[0])
    head_values = jnp.concatenate([own, mate], axis=1).astype(BF16)
    out_ref[...] = dot(head_values, o_ref[...]).astype(BF16)


def total_kernel(tiles_ref, out_ref):
    total = jnp.sum(tiles_ref[...].astype(F32), axis=0)
    width = total.shape[1]
    for i in range(total.shape[0]):
        out_ref[:, i * width : (i + 1) * width] = total[i : i + 1]


def exchange(array, axes, peers):
    blocks = array.reshape(peers, array.shape[0] // peers, *array.shape[1:])
    return lax.all_to_all(blocks, axes, 0, 0, tiled=True).reshape(array.shape)


def shards(
    q_compressed,
    w_q_nope,
    w_q_rope,
    w_uk,
    w_uv,
    w_o,
    kv_cache,
    draft_kv,
    context_length,
    slot_sequence,
    slot_slab,
):
    groups, zs, xs, cores = (lax.axis_size(a) for a in ("group", "z", "x", "core"))
    group, z, x, core = (lax.axis_index(a) for a in ("group", "z", "x", "core"))
    chips = zs * xs
    core_id = core.astype(jnp.int32).reshape(1)
    swap = [(i, 1 - i) for i in range(cores)]

    table = lax.dynamic_index_in_dim(slot_sequence, group, 0, keepdims=False)
    table = table.reshape(chips, cores, SLOTS)
    held = lax.dynamic_index_in_dim(table, core, 1, keepdims=False)
    hp = jnp.arange(2, dtype=jnp.int32)[:, None]
    draft = jnp.arange(DRAFT, dtype=jnp.int32)
    filled = (held >= 0).T[:, :, None]
    shift = (group - (held >> 4)) & (groups - 1)
    code = (shift * TOK_GRP + (held & 15) * DRAFT).T[:, :, None]
    code = code + ((hp != core) * (groups * TOK_GRP) + draft).reshape(-1)
    code = jnp.where(filled, code, -1).reshape(-1, 1)
    quarter = TOK_GRP // 2
    ahead = ((held >> 4) - group) & (groups - 1)
    row = (ahead * quarter + (held & 15) * 2).T[:, :, None, None]
    row = row + ((draft & 1) != core) * (groups * quarter) + (draft >> 1)
    row = jnp.where(filled[..., None], row, -1)
    row = jnp.where(hp == hp.reshape(2, 1, 1, 1, 1), row, -1).reshape(2 * SLOTS, -1)

    chip = z * xs + x
    mine = lax.dynamic_index_in_dim(held, chip, 0, keepdims=False)
    slabs = lax.dynamic_index_in_dim(slot_slab, group, 0, keepdims=False).reshape(chips, cores, SLOTS)
    slabs = lax.dynamic_index_in_dim(slabs, chip, 0, keepdims=False)
    slabs = lax.dynamic_index_in_dim(slabs, core, 0, keepdims=False)
    is_mine = mine[:, None] == jnp.arange(context_length.shape[0], dtype=jnp.int32)
    length = jnp.sum(jnp.where(is_mine, context_length, 0), axis=1)
    count = jnp.where(mine >= 0, length - slabs * kv_cache.shape[3], 0).astype(jnp.int32)

    narrow = pl.pallas_call(
        project_kernel,
        out_shape=jax.ShapeDtypeStruct((TOK_GRP, NARROW), BF16),
        in_specs=[HBM] * 3,
        out_specs=VMEM,
        scratch_shapes=[
            *(pltpu.VMEM(a.shape, BF16) for a in (q_compressed, w_q_nope, w_q_rope)),
            pltpu.SemaphoreType.DMA((4,)),
        ],
        compiler_params=pltpu.CompilerParams(vmem_limit_bytes=16 << 20),
        cost_estimate=pl.CostEstimate(flops=2 << 30, transcendentals=0, bytes_accessed=4 << 20),
    )(*(in_hbm(a) for a in (q_compressed, w_q_nope, w_q_rope)))
    own_q = [narrow]
    for k in range(1, groups):
        own_q.append(lax.ppermute(narrow, "group", [(i, (i + k) % groups) for i in range(groups)]))
    own_q = jnp.concatenate(own_q, axis=0)
    mate_q = lax.ppermute(own_q, "core", swap)
    late_o, mate_q = lax.optimization_barrier((w_o, mate_q))
    mate_o = lax.ppermute(late_o, "core", swap)
    mate_uk = lax.ppermute(w_uk, "core", swap)
    rows = chips * cores * DRAFT
    wide = pl.pallas_call(
        spread_kernel,
        out_shape=jax.ShapeDtypeStruct((rows, SLOTS * WIDE), BF16),
        grid=(SLOTS,),
        in_specs=[VMEM, VMEM, pl.BlockSpec((rows, 1), lambda k: (k, 0)), VMEM, VMEM],
        out_specs=pl.BlockSpec((rows, WIDE), lambda k: (0, k)),
        scratch_shapes=[pltpu.VMEM((groups * cores * TOK_GRP, 5 * NOPE), BF16)],
        compiler_params=pltpu.CompilerParams(
            dimension_semantics=("arbitrary",), vmem_limit_bytes=16 << 20
        ),
        cost_estimate=pl.CostEstimate(flops=30 << 30, transcendentals=0, bytes_accessed=80 << 20),
    )(own_q, mate_q, code, w_uk, mate_uk)
    slabs_kv = jnp.swapaxes(kv_cache.reshape(kv_cache.shape[2:]), 1, 2)
    count, wide = lax.optimization_barrier((count, wide))
    arrived = exchange(wide, ("z", "x"), chips)
    partials = attend(count, arrived, slabs_kv)
    late_uv, partials = lax.optimization_barrier((w_uv, partials))
    mate_uv = lax.ppermute(late_uv, "core", swap)
    draft_hv, draft_log = call(
        draft_kernel,
        (
            jax.ShapeDtypeStruct((TOK_GRP // 2, 4 * VDIM), F32),
            jax.ShapeDtypeStruct((TOK_GRP // 2, 128), F32),
        ),
        (core_id, own_q, mate_q, w_uk, mate_uk, w_uv, mate_uv, draft_kv),
        [SMEM] + [VMEM] * 7,
    )
    back = exchange(partials, ("z", "x"), chips)
    both_o = jnp.concatenate([w_o, mate_o], axis=0)
    back, draft_hv, draft_log, both_o = lax.optimization_barrier((back, draft_hv, draft_log, both_o))
    part = jax.ShapeDtypeStruct((groups * quarter, 4 * VDIM + 128), BF16)
    own_part, mate_part = call(
        merge_kernel,
        (part, part),
        (core_id, back, row, w_uv, mate_uv),
        [SMEM] + [VMEM] * 4,
        vmem=16,
        cost=pl.CostEstimate(flops=3 << 30, transcendentals=1 << 19, bytes_accessed=8 << 20),
    )
    mate_part = lax.ppermute(mate_part, "core", swap)
    others = []
    for k in reversed(range(1, groups)):
        at = slice(k * quarter, (k + 1) * quarter)
        pair = jnp.concatenate([own_part[at], mate_part[at]], axis=0)
        others.append(lax.ppermute(pair, "group", [(i, (i + k) % groups) for i in range(groups)]))
    sums = call(
        finish_kernel,
        jax.ShapeDtypeStruct((chips, w_o.shape[1]), BF16),
        (core_id, own_part, mate_part, *others, draft_hv, draft_log, both_o),
        [SMEM] + [VMEM] * (groups + 4),
    )
    tiles = lax.all_to_all(sums.reshape(chips, 8, -1), ("z", "x"), 0, 0, tiled=True)
    return call(
        total_kernel, jax.ShapeDtypeStruct((1, w_o.shape[1]), F32), (tiles,), [VMEM]
    )


def solution(mesh):
    fine = Mesh(mesh.devices.reshape(4, 8, 4, 2), ("group", "z", "x", "core"))
    dev = ("z", "x", "core")
    placed = (
        P("group", None),
        P(None, dev),
        P(None, dev),
        P(dev, None, None),
        P(dev, None, None),
        P(dev, None),
        P("group", dev, None, None, None),
        P("group", None),
        P(),
        P(),
        P(),
    )
    return jax.shard_map(
        shards, mesh=fine, in_specs=placed, out_specs=P(("group", *dev), None), check_vma=False
    )
```

```python
import jax
import jax.numpy as jnp
from jax import lax
from jax.experimental import pallas as pl
from jax.experimental.pallas import tpu as pltpu
from jax.sharding import Mesh
from jax.sharding import PartitionSpec as P

NOPE = 128
ROPE = 64
LATENT = 512
VDIM = 128
DRAFT = 4
SEQ_GRP = 16
TOK_GRP = SEQ_GRP * DRAFT
SLOTS = 2
KEY = LATENT + ROPE
WIDE = 2 * LATENT + 2 * ROPE
PART = SLOTS * 2 * LATENT + 128
NARROW = 2 * NOPE + 2 * ROPE
EMPTY = -1e30
SCALE = (NOPE + ROPE) ** -0.5
F32 = jnp.float32
BF16 = jnp.bfloat16
CONTRACT_LAST = (((1,), (1,)), ((), ()))

VMEM = pl.BlockSpec(memory_space=pltpu.VMEM)
SMEM = pl.BlockSpec(memory_space=pltpu.SMEM)
HBM = pl.BlockSpec(memory_space=pltpu.HBM)


def in_hbm(array):
    return pltpu.with_memory_space_constraint(array, pltpu.HBM)


def dot(a, b):
    return jnp.dot(a, b, preferred_element_type=F32)


def dot_t(a, b):
    return lax.dot_general(a, b, CONTRACT_LAST, preferred_element_type=F32)


def call(kernel, outs, args, specs, scratch=(), vmem=32, cost=None):
    return pl.pallas_call(
        kernel,
        out_shape=outs,
        in_specs=specs,
        out_specs=jax.tree.map(lambda _: VMEM, outs),
        scratch_shapes=list(scratch),
        compiler_params=pltpu.CompilerParams(vmem_limit_bytes=vmem << 20),
        cost_estimate=cost,
    )(*args)


def three_terms(value):
    high = value.astype(BF16).astype(F32)
    middle = (value - high).astype(BF16).astype(F32)
    return high, middle, (value - high - middle).astype(BF16).astype(F32)


def put_terms(tile, value, first):
    lane = lax.broadcasted_iota(jnp.int32, tile.shape, 1)
    for i, term in enumerate(three_terms(value)):
        tile = jnp.where(lane == first + i, term, tile)
    return tile


def project_kernel(q_hbm, wn_hbm, wr_hbm, out_ref, q_ref, wn_ref, wr_ref, sems):
    copies = []
    depth = wn_ref.shape[0] // 2
    for i, (source, target) in enumerate(((q_hbm, q_ref), (wr_hbm, wr_ref))):
        copies.append(pltpu.make_async_copy(source, target, sems.at[i]))
    for i in range(2):
        at = pl.ds(i * depth, depth)
        copies.append(pltpu.make_async_copy(wn_hbm.at[at], wn_ref.at[at], sems.at[2 + i]))
    for copy in copies:
        copy.start()
    copies[0].wait()
    copies[1].wait()
    out_ref[:, 2 * NOPE :] = (dot(q_ref[...], wr_ref[...]) * SCALE).astype(BF16)
    copies[2].wait()
    copies[3].wait()
    out_ref[:, : 2 * NOPE] = dot(q_ref[...], wn_ref[...]).astype(BF16)


def spread_kernel(own_q, mate_q, code_ref, own_ref, mate_ref, out_ref, rows):
    @pl.when(pl.program_id(0) == 0)
    def _():
        rows[...] = jnp.zeros_like(rows)
        count = own_q.shape[0]
        for rel, q_ref in enumerate((own_q, mate_q)):
            at = slice(rel * count, (rel + 1) * count)
            for par in range(2):
                first = par * 2 * NOPE + rel * NOPE
                rows[at, first : first + NOPE] = q_ref[:, par * NOPE : (par + 1) * NOPE]
            rows[at, 4 * NOPE :] = q_ref[:, 2 * NOPE :]

    column = lax.broadcasted_iota(jnp.int32, (code_ref.shape[0], rows.shape[0]), 1)
    pick = jnp.where(column == code_ref[...], 1.0, 0.0).astype(BF16)
    picked = dot(pick, rows[...]).astype(BF16)
    for par in range(2):
        weight = jnp.concatenate([own_ref[par], mate_ref[par]], axis=0)
        absorbed = dot(picked[:, par * 2 * NOPE : (par + 1) * 2 * NOPE], weight) * SCALE
        out_ref[:, par * LATENT : (par + 1) * LATENT] = absorbed.astype(BF16)
    out_ref[:, 2 * LATENT :] = picked[:, 4 * NOPE :]


def draft_kernel(
    core_ref, own_q, mate_q, own_uk, mate_uk, own_uv, mate_uv, kv_ref, hv_ref, log_ref
):
    core = core_ref[0]
    half = hv_ref.shape[0]
    row = 2 * lax.broadcasted_iota(jnp.int32, (half, TOK_GRP), 0) + core
    col = lax.broadcasted_iota(jnp.int32, (half, TOK_GRP), 1)
    seen = (row // DRAFT == col // DRAFT) & (col <= row)
    pick = jnp.where(row == col, 1.0, 0.0).astype(BF16)
    lane = lax.broadcasted_iota(jnp.int32, log_ref.shape, 1)
    logs = jnp.zeros(log_ref.shape, F32)
    sides = ((core, own_q, own_uk, own_uv), (1 - core, mate_q, mate_uk, mate_uv))
    for hp, q_ref, uk_ref, uv_ref in sides:
        rows = dot(pick, q_ref[:TOK_GRP, :]).astype(BF16)
        for par in range(2):
            narrow = rows[:, par * NOPE : (par + 1) * NOPE]
            absorbed = (dot(narrow, uk_ref[par]) * SCALE).astype(BF16)
            first = 2 * NOPE + par * ROPE
            scores = dot_t(absorbed, kv_ref[:, :LATENT])
            scores += dot_t(rows[:, first : first + ROPE], kv_ref[:, LATENT:])
            scores = jnp.where(seen, scores, EMPTY)
            peak = jnp.max(scores, axis=1, keepdims=True)
            weights = jnp.where(seen, jnp.exp(scores - peak), 0.0)
            total = jnp.sum(weights, axis=1, keepdims=True)
            mixture = dot(weights.astype(BF16), kv_ref[:, :LATENT]) / total
            head = hp * 2 + par
            at = pl.ds(pl.multiple_of(head * VDIM, VDIM), VDIM)
            hv_ref[:, at] = dot(mixture.astype(BF16), uv_ref[par])
            logs = jnp.where(lane == head, peak + jnp.log(total), logs)
    log_ref[...] = logs


def attend_kernel(
    count_ref, x_ref, kv_ref, out_hbm, queries, scores, weights, out_ref, sems
):
    half = x_ref.shape[0]
    slab = kv_ref.shape[2]
    chunk = 256
    base = SLOTS * 2 * LATENT
    lane = lax.broadcasted_iota(jnp.int32, (half, 128), 1)
    tile = jnp.zeros((half, 128), F32)
    copies = []
    for slot in range(SLOTS):
        count = count_ref[slot]
        for par in range(2):
            at = slice(par * half, (par + 1) * half)
            first = slot * WIDE + par * LATENT
            queries[at, :LATENT] = x_ref[:, first : first + LATENT]
            first = slot * WIDE + 2 * LATENT + par * ROPE
            queries[at, LATENT:] = x_ref[:, first : first + ROPE]

        def score_slab(masked, slot=slot, count=count):
            peak = jnp.full((2 * half, 1), EMPTY, F32)
            for first in range(0, slab, chunk):
                score = dot(queries[...], kv_ref[slot, :, first : first + chunk])
                if masked:
                    position = lax.broadcasted_iota(jnp.int32, score.shape, 1) + first
                    score = jnp.where(position < count, score, EMPTY)
                scores[:, first : first + chunk] = score
                peak = jnp.maximum(peak, jnp.max(score, axis=1, keepdims=True))
            return peak

        peak = lax.cond(count >= slab, lambda: score_slab(False), lambda: score_slab(True))
        reference = jnp.maximum(peak, EMPTY / 10)
        total = jnp.zeros((2 * half, 1), F32)
        for first in range(0, slab, chunk):
            weight = jnp.exp(scores[:, first : first + chunk] - reference)
            total += jnp.sum(weight, axis=1, keepdims=True)
            weights[:, first : first + chunk] = weight.astype(BF16)
        total = jnp.maximum(total, 1.0)
        mixture = dot_t(weights[...], kv_ref[slot, :LATENT, :])
        mixture = (mixture * (1.0 / total)).astype(BF16)
        log = peak + jnp.log(total)
        start = slot * 2 * LATENT
        for par in range(2):
            at = slice(par * half, (par + 1) * half)
            out_ref[:, start + par * LATENT : start + (par + 1) * LATENT] = mixture[at]
            for i, term in enumerate(three_terms(log[at])):
                tile = jnp.where(lane == slot * 6 + par * 3 + i, term, tile)
        end = start + 2 * LATENT
        if slot == SLOTS - 1:
            out_ref[:, base:] = tile.astype(BF16)
            end = PART
        at = pl.ds(start, end - start)
        copies.append(pltpu.make_async_copy(out_ref.at[:, at], out_hbm.at[:, at], sems.at[slot]))
        copies[-1].start()
    for copy in copies:
        copy.wait()


def attend(count, x, kv):
    rows = x.shape[0]
    return pl.pallas_call(
        attend_kernel,
        out_shape=jax.ShapeDtypeStruct((rows, PART), BF16),
        in_specs=[SMEM, VMEM, VMEM],
        out_specs=HBM,
        scratch_shapes=[
            pltpu.VMEM((2 * rows, KEY), BF16),
            pltpu.VMEM((2 * rows, kv.shape[2]), F32),
            pltpu.VMEM((2 * rows, kv.shape[2]), BF16),
            pltpu.VMEM((rows, PART), BF16),
            pltpu.SemaphoreType.DMA((SLOTS,)),
        ],
        compiler_params=pltpu.CompilerParams(vmem_limit_bytes=32 << 20),
    )(count, x, kv)


def merge_kernel(core_ref, y_ref, code_ref, own_ref, mate_ref, own_out, mate_out):
    core = core_ref[0]
    half = own_out.shape[0]
    rows, cols = 2 * half, y_ref.shape[0]
    base = SLOTS * 2 * LATENT
    logs = jnp.transpose(y_ref[:, base:].astype(F32))
    row = lax.broadcasted_iota(jnp.int32, (rows, cols), 0)
    tile = jnp.zeros((rows, 128), F32)
    for hp in range(2):
        match = [row == code_ref[hp * 2 + slot : hp * 2 + slot + 1, :] for slot in range(SLOTS)]
        for par in range(2):
            held = []
            for slot in range(SLOTS):
                at = slot * 6 + par * 3
                log = logs[at : at + 1, :] + logs[at + 1 : at + 2, :] + logs[at + 2 : at + 3, :]
                held.append(jnp.where(match[slot], log, EMPTY))
            peak = jnp.max(jnp.maximum(held[0], held[1]), axis=1, keepdims=True)
            total = jnp.zeros((rows, 1), F32)
            mixture = jnp.zeros((rows, LATENT), F32)
            for slot in range(SLOTS):
                weights = jnp.where(match[slot], jnp.exp(held[slot] - peak), 0.0)
                total += jnp.sum(weights, axis=1, keepdims=True)
                first = slot * 2 * LATENT + par * LATENT
                mixture += dot(weights.astype(BF16), y_ref[:, first : first + LATENT])
            total = jnp.maximum(total, 1.0)
            mixture = (mixture / total).astype(BF16)
            head = hp * 2 + par
            values = dot(mixture, jnp.where(core == hp, own_ref[par], mate_ref[par]))
            own_out[:, head * VDIM : (head + 1) * VDIM] = values[:half].astype(BF16)
            mate_out[:, head * VDIM : (head + 1) * VDIM] = values[half:].astype(BF16)
            tile = put_terms(tile, peak + jnp.log(total), head * 3)
    own_out[:, 4 * VDIM :] = tile[:half].astype(BF16)
    mate_out[:, 4 * VDIM :] = tile[half:].astype(BF16)


def finish_kernel(core_ref, own_ref, mate_ref, *refs):
    *others, hv_ref, log_ref, o_ref, out_ref = refs
    half = hv_ref.shape[0]
    blocks = [(own_ref, slice(0, half)), (mate_ref, slice(0, half))]
    for other in others:
        blocks += [(other, slice(0, half)), (other, slice(half, 2 * half))]
    values = []
    for head in range(4):
        logs = [log_ref[:, head : head + 1]]
        parts = [hv_ref[:, head * VDIM : (head + 1) * VDIM]]
        for z_ref, at in blocks:
            terms = z_ref[at, 4 * VDIM :].astype(F32)
            first = head * 3
            logs.append(
                terms[:, first : first + 1]
                + terms[:, first + 1 : first + 2]
                + terms[:, first + 2 : first + 3]
            )
            parts.append(z_ref[at, head * VDIM : (head + 1) * VDIM].astype(F32))
        peak = logs[0]
        for log in logs[1:]:
            peak = jnp.maximum(peak, log)
        total = jnp.zeros_like(peak)
        summed = jnp.zeros_like(parts[0])
        for log, part in zip(logs, parts):
            weight = jnp.exp(log - peak)
            total += weight
            summed += weight * part
        values.append(summed / total)
    pairs = [jnp.concatenate(values[hp * 2 : hp * 2 + 2], axis=1) for hp in range(2)]
    own = jnp.where(core_ref[0] == 0, pairs[0], pairs[1])
    mate = jnp.where(core_ref[0] == 0, pairs[1], pairs[0])
    head_values = jnp.concatenate([own, mate], axis=1).astype(BF16)
    out_ref[...] = dot(head_values, o_ref[...]).astype(BF16)


def total_kernel(tiles_ref, out_ref):
    total = jnp.sum(tiles_ref[...].astype(F32), axis=0)
    width = total.shape[1]
    for i in range(total.shape[0]):
        out_ref[:, i * width : (i + 1) * width] = total[i : i + 1]


def exchange(array, axes, peers):
    blocks = array.reshape(peers, array.shape[0] // peers, *array.shape[1:])
    return lax.all_to_all(blocks, axes, 0, 0, tiled=True).reshape(array.shape)


def shards(
    q_compressed,
    w_q_nope,
    w_q_rope,
    w_uk,
    w_uv,
    w_o,
    kv_cache,
    draft_kv,
    context_length,
    slot_sequence,
    slot_slab,
):
    groups, zs, xs, cores = (lax.axis_size(a) for a in ("group", "z", "x", "core"))
    group, z, x, core = (lax.axis_index(a) for a in ("group", "z", "x", "core"))
    chips = zs * xs
    core_id = core.astype(jnp.int32).reshape(1)
    swap = [(i, 1 - i) for i in range(cores)]

    table = lax.dynamic_index_in_dim(slot_sequence, group, 0, keepdims=False)
    table = table.reshape(chips, cores, SLOTS)
    held = lax.dynamic_index_in_dim(table, core, 1, keepdims=False)
    hp = jnp.arange(2, dtype=jnp.int32)[:, None]
    draft = jnp.arange(DRAFT, dtype=jnp.int32)
    filled = (held >= 0).T[:, :, None]
    shift = (group - (held >> 4)) & (groups - 1)
    code = (shift * TOK_GRP + (held & 15) * DRAFT).T[:, :, None]
    code = code + ((hp != core) * (groups * TOK_GRP) + draft).reshape(-1)
    code = jnp.where(filled, code, -1).reshape(-1, 1)
    quarter = TOK_GRP // 2
    ahead = ((held >> 4) - group) & (groups - 1)
    row = (ahead * quarter + (held & 15) * 2).T[:, :, None, None]
    row = row + ((draft & 1) != core) * (groups * quarter) + (draft >> 1)
    row = jnp.where(filled[..., None], row, -1)
    row = jnp.where(hp == hp.reshape(2, 1, 1, 1, 1), row, -1).reshape(2 * SLOTS, -1)

    chip = z * xs + x
    mine = lax.dynamic_index_in_dim(held, chip, 0, keepdims=False)
    slabs = lax.dynamic_index_in_dim(slot_slab, group, 0, keepdims=False).reshape(chips, cores, SLOTS)
    slabs = lax.dynamic_index_in_dim(slabs, chip, 0, keepdims=False)
    slabs = lax.dynamic_index_in_dim(slabs, core, 0, keepdims=False)
    is_mine = mine[:, None] == jnp.arange(context_length.shape[0], dtype=jnp.int32)
    length = jnp.sum(jnp.where(is_mine, context_length, 0), axis=1)
    count = jnp.where(mine >= 0, length - slabs * kv_cache.shape[3], 0).astype(jnp.int32)

    narrow = pl.pallas_call(
        project_kernel,
        out_shape=jax.ShapeDtypeStruct((TOK_GRP, NARROW), BF16),
        in_specs=[HBM] * 3,
        out_specs=VMEM,
        scratch_shapes=[
            *(pltpu.VMEM(a.shape, BF16) for a in (q_compressed, w_q_nope, w_q_rope)),
            pltpu.SemaphoreType.DMA((4,)),
        ],
        compiler_params=pltpu.CompilerParams(vmem_limit_bytes=16 << 20),
        cost_estimate=pl.CostEstimate(flops=2 << 30, transcendentals=0, bytes_accessed=4 << 20),
    )(*(in_hbm(a) for a in (q_compressed, w_q_nope, w_q_rope)))
    own_q = [narrow]
    for k in range(1, groups):
        own_q.append(lax.ppermute(narrow, "group", [(i, (i + k) % groups) for i in range(groups)]))
    own_q = jnp.concatenate(own_q, axis=0)
    mate_q = lax.ppermute(own_q, "core", swap)
    late_o, mate_q = lax.optimization_barrier((w_o, mate_q))
    mate_o = lax.ppermute(late_o, "core", swap)
    mate_uk = lax.ppermute(w_uk, "core", swap)
    rows = chips * cores * DRAFT
    wide = pl.pallas_call(
        spread_kernel,
        out_shape=jax.ShapeDtypeStruct((rows, SLOTS * WIDE), BF16),
        grid=(SLOTS,),
        in_specs=[VMEM, VMEM, pl.BlockSpec((rows, 1), lambda k: (k, 0)), VMEM, VMEM],
        out_specs=pl.BlockSpec((rows, WIDE), lambda k: (0, k)),
        scratch_shapes=[pltpu.VMEM((groups * cores * TOK_GRP, 5 * NOPE), BF16)],
        compiler_params=pltpu.CompilerParams(
            dimension_semantics=("arbitrary",), vmem_limit_bytes=16 << 20
        ),
        cost_estimate=pl.CostEstimate(flops=30 << 30, transcendentals=0, bytes_accessed=80 << 20),
    )(own_q, mate_q, code, w_uk, mate_uk)
    slabs_kv = jnp.swapaxes(kv_cache.reshape(kv_cache.shape[2:]), 1, 2)
    count, wide = lax.optimization_barrier((count, wide))
    arrived = exchange(wide, ("z", "x"), chips)
    partials = attend(count, arrived, slabs_kv)
    late_uv, partials = lax.optimization_barrier((w_uv, partials))
    mate_uv = lax.ppermute(late_uv, "core", swap)
    draft_hv, draft_log = call(
        draft_kernel,
        (
            jax.ShapeDtypeStruct((TOK_GRP // 2, 4 * VDIM), F32),
            jax.ShapeDtypeStruct((TOK_GRP // 2, 128), F32),
        ),
        (core_id, own_q, mate_q, w_uk, mate_uk, w_uv, mate_uv, draft_kv),
        [SMEM] + [VMEM] * 7,
    )
    back = exchange(partials, ("z", "x"), chips)
    both_o = jnp.concatenate([w_o, mate_o], axis=0)
    back, draft_hv, draft_log, both_o = lax.optimization_barrier((back, draft_hv, draft_log, both_o))
    part = jax.ShapeDtypeStruct((groups * quarter, 4 * VDIM + 128), BF16)
    own_part, mate_part = call(
        merge_kernel,
        (part, part),
        (core_id, back, row, w_uv, mate_uv),
        [SMEM] + [VMEM] * 4,
        vmem=16,
        cost=pl.CostEstimate(flops=3 << 30, transcendentals=1 << 19, bytes_accessed=8 << 20),
    )
    mate_part = lax.ppermute(mate_part, "core", swap)
    others = []
    for k in reversed(range(1, groups)):
        at = slice(k * quarter, (k + 1) * quarter)
        pair = jnp.concatenate([own_part[at], mate_part[at]], axis=0)
        others.append(lax.ppermute(pair, "group", [(i, (i + k) % groups) for i in range(groups)]))
    sums = call(
        finish_kernel,
        jax.ShapeDtypeStruct((chips, w_o.shape[1]), BF16),
        (core_id, own_part, mate_part, *others, draft_hv, draft_log, both_o),
        [SMEM] + [VMEM] * (groups + 4),
    )
    tiles = lax.all_to_all(sums.reshape(chips, 8, -1), ("z", "x"), 0, 0, tiled=True)
    return call(
        total_kernel, jax.ShapeDtypeStruct((1, w_o.shape[1]), F32), (tiles,), [VMEM]
    )


def solution(mesh):
    fine = Mesh(mesh.devices.reshape(4, 8, 4, 2), ("group", "z", "x", "core"))
    dev = ("z", "x", "core")
    placed = (
        P("group", None),
        P(None, dev),
        P(None, dev),
        P(dev, None, None),
        P(dev, None, None),
        P(dev, None),
        P("group", dev, None, None, None),
        P("group", None),
        P(),
        P(),
        P(),
    )
    return jax.shard_map(
        shards, mesh=fine, in_specs=placed, out_specs=P(("group", *dev), None), check_vma=False
    )
```
